32 devices in a mesh: groups: 2 (over y), wide: 4 (over z), narrow: 2 (over x), pair: 2 (over core).
Axes of the slice: x: 2, y: 2, z: 4, core: 2. Of those that a mesh axis runs over, the one named last changes fastest.
Arguments:
- volume: bfloat16 [48, 16, 64, 128], P(('groups', 'wide'), 'narrow', 'pair'), parts along dimension 0, may hold values from -6 to 6
- w_encode: bfloat16 [3, 3, 3, 128, 128], replicated, may hold values from -0.109375 to 0.109375
- b_encode: float32 [128], replicated, may hold values from -3 to 3
- w_down: bfloat16 [2, 2, 2, 128, 256], replicated, may hold values from -0.1875 to 0.1875
- b_down: float32 [256], replicated, may hold values from -3 to 3
- w_bottom: bfloat16 [3, 3, 3, 256, 256], replicated, may hold values from -0.078125 to 0.078125
- b_bottom: float32 [256], replicated, may hold values from -3 to 3
- w_up: bfloat16 [2, 2, 2, 256, 128], replicated, may hold values from -0.375 to 0.375
- b_up: float32 [128], replicated, may hold values from -3 to 3
- w_decode: bfloat16 [3, 3, 3, 256, 128], replicated, may hold values from -0.078125 to 0.078125
- b_decode: float32 [128], replicated, may hold values from -3 to 3
Outputs:
- decoded: bfloat16 [48, 16, 64, 128], P(('groups', 'wide'), 'narrow', 'pair'), parts along dimension 0
The draws below stay inside these ranges and needn't reach their ends.
There are 2 independent parts, one for each index of `groups`. The reference program is written for one: setup_inputs(seed, part) draws one part's arguments, and reference() takes and returns one part's arrays. A program takes and returns all parts, laid end to end along the dimension named above; an argument that names none is the same for every part. Nothing has to cross between parts.
All inputs are finite; a program needn't handle non-finite values.
Results may differ from the reference program's by a relative error of at most 0.008.
Values may be sent and summed in bfloat16 or wider, within the bound.
No kernel may reach another device: no remote copies, remote signals or barrier semaphores. Data moves between devices by JAX's collectives and lax.ppermute only.
A program may use at most 64 MiB of HBM per device.

```python
import jax
import jax.numpy as jnp
from jax import lax

C2 = 128
C3 = 256
DEPTH = 24
HEIGHT = 16
WIDTH = 64


def shard_levels(stream_key, extent, shards, least, high):
    loudness = 1.0
    for dim, shards_of in shards:
        heights = jax.random.uniform(jax.random.fold_in(jax.random.fold_in(stream_key, 6), dim), (shards_of,), jnp.float32, least / len(shards), high / len(shards))
        loudness = loudness * jnp.repeat(jnp.exp(heights), extent[dim] // shards_of).reshape((-1,) + (1,) * (len(extent) - 1 - dim))
    return loudness


def gaussian(own_key, dims, scale, bound, split=(), dtype=jnp.bfloat16):
    result = scale * jax.random.normal(own_key, dims, jnp.float32)
    if split:
        result = result * shard_levels(own_key, dims, split, -0.22, 0.18)
    return jnp.clip(result, -bound, bound).astype(dtype)


def setup_inputs(seed: int = 0, part: int = 0) -> dict:
    arg_keys = jax.random.split(jax.random.key(seed), 12)
    own_keys = jax.random.split(jax.random.fold_in(arg_keys[11], part), 12)
    return {
        "volume": gaussian(own_keys[0], (DEPTH, HEIGHT, WIDTH, C2), 1.0, 6.0, ((0, 4), (1, 2), (2, 2))),
        "w_encode": gaussian(arg_keys[1], (3, 3, 3, C2, C2), (27 * C2) ** -0.5, 0.109375),
        "b_encode": gaussian(arg_keys[2], (C2,), 0.5, 3.0, (), jnp.float32),
        "w_down": gaussian(arg_keys[3], (2, 2, 2, C2, C3), (8 * C2) ** -0.5, 0.1875),
        "b_down": gaussian(arg_keys[4], (C3,), 0.5, 3.0, (), jnp.float32),
        "w_bottom": gaussian(arg_keys[5], (3, 3, 3, C3, C3), (27 * C3) ** -0.5, 0.078125),
        "b_bottom": gaussian(arg_keys[6], (C3,), 0.5, 3.0, (), jnp.float32),
        "w_up": gaussian(arg_keys[7], (2, 2, 2, C3, C2), C3 ** -0.5, 0.375),
        "b_up": gaussian(arg_keys[8], (C2,), 0.5, 3.0, (), jnp.float32),
        "w_decode": gaussian(arg_keys[9], (3, 3, 3, 2 * C2, C2), (54 * C2) ** -0.5, 0.078125),
        "b_decode": gaussian(arg_keys[10], (C2,), 0.5, 3.0, (), jnp.float32),
    }


def leaky_relu(values):
    return jnp.maximum(values, 0.01 * values)


def conv_cube(field, kernel):
    return lax.conv_general_dilated(
        field.astype(jnp.float32)[None], kernel.astype(jnp.float32), (1, 1, 1),
        ((1, 1), (1, 1), (1, 1)), dimension_numbers=("NDHWC", "DHWIO", "NDHWC"),
        precision=lax.Precision.HIGHEST)[0]


def reference(volume, w_encode, b_encode, w_down, b_down, w_bottom, b_bottom, w_up, b_up, w_decode, b_decode):
    encoded = leaky_relu(conv_cube(volume, w_encode) + b_encode).astype(jnp.bfloat16)
    depth_cells, height_cells, width_cells, skip_width = encoded.shape
    blocks = encoded.astype(jnp.float32).reshape(depth_cells // 2, 2, height_cells // 2, 2, width_cells // 2, 2, skip_width)
    coarse = leaky_relu(jnp.einsum("zaybxci,abcio->zyxo", blocks, w_down.astype(jnp.float32),
                                   precision=lax.Precision.HIGHEST) + b_down).astype(jnp.bfloat16)
    bottom = leaky_relu(conv_cube(coarse, w_bottom) + b_bottom).astype(jnp.bfloat16)
    lifted = jnp.einsum("zyxi,abcio->zaybxco", bottom.astype(jnp.float32), w_up.astype(jnp.float32),
                        precision=lax.Precision.HIGHEST) + b_up
    raised = lifted.reshape(depth_cells, height_cells, width_cells, skip_width).astype(jnp.bfloat16)
    joined = jnp.concatenate([raised, encoded], axis=-1)
    return leaky_relu(conv_cube(joined, w_decode) + b_decode).astype(jnp.bfloat16)
```

```python
import functools

import jax
import jax.numpy as jnp
from jax import lax
from jax.experimental import pallas as pl
from jax.experimental.pallas import tpu as pltpu
from jax.sharding import PartitionSpec as P

leak_slope = 0.01
f32 = jnp.float32
bf16 = jnp.bfloat16


def leaky_relu(values):
    return jnp.maximum(values, leak_slope * values)


def line_exchange(axis, to_low, to_high):
    count = lax.axis_size(axis)
    if count == 2:
        sent = jnp.where(lax.axis_index(axis) == 0, to_high, to_low)
        got = lax.ppermute(sent, axis, [(0, 1), (1, 0)])
        return got, got
    up = [(i, i + 1) for i in range(count - 1)]
    down = [(b, a) for a, b in up]
    return lax.ppermute(to_high, axis, up), lax.ppermute(to_low, axis, down)


def snake_pairs(groups, count, step):
    order = [
        group * count + (place if group % 2 == 0 else count - 1 - place)
        for group in range(groups)
        for place in range(count)
    ]
    total = len(order)
    return [(order[i], order[(i + step) % total]) for i in range(total)]


def wide_exchange(to_low, to_high):
    groups, count = lax.axis_size("groups"), lax.axis_size("wide")
    even = lax.axis_index("groups") % 2 == 0
    axes = ("groups", "wide")
    forward = lax.ppermute(
        jnp.where(even, to_high, to_low), axes, snake_pairs(groups, count, 1)
    )
    backward = lax.ppermute(
        jnp.where(even, to_low, to_high), axes, snake_pairs(groups, count, -1)
    )
    return forward, backward


def call(kernel, outs, scratch=()):
    return pl.pallas_call(
        kernel,
        out_shape=[jax.ShapeDtypeStruct(shape, bf16) for shape in outs],
        scratch_shapes=list(scratch),
    )


def edges(axis):
    place = lax.axis_index(axis)
    return place == 0, place == lax.axis_size(axis) - 1


def fill_frame(ext, own, rows_low, rows_high, planes_ahead, planes_behind, deep, tall):
    depth, height = own.shape[0], own.shape[1]
    ext[deep : deep + depth, tall : tall + height] = own[...]
    ext[deep : deep + depth, :tall] = rows_low
    ext[deep : deep + depth, tall + height :] = rows_high
    even = lax.axis_index("groups") % 2 == 0

    @pl.when(even)
    def _():
        ext[:deep] = planes_ahead
        ext[deep + depth :] = planes_behind

    @pl.when(jnp.logical_not(even))
    def _():
        ext[:deep] = planes_behind
        ext[deep + depth :] = planes_ahead

    first, last = edges("narrow")

    @pl.when(first)
    def _():
        ext[:, :tall] = jnp.zeros((ext.shape[0], tall) + ext.shape[2:], bf16)

    @pl.when(last)
    def _():
        ext[:, tall + height :] = jnp.zeros((ext.shape[0], tall) + ext.shape[2:], bf16)

    first, last = edges("wide")

    @pl.when(first)
    def _():
        ext[:deep] = jnp.zeros((deep,) + ext.shape[1:], bf16)

    @pl.when(last)
    def _():
        ext[deep + depth :] = jnp.zeros((deep,) + ext.shape[1:], bf16)


def write_columns(columns, plane, low, high, lanes):
    if columns.shape[0] == 1:
        at_low = lax.axis_index("pair") == 0
        columns[0, plane, :, lanes] = jnp.where(at_low, high, low)
    else:
        columns[0, plane, :, lanes] = low
        columns[1, plane, :, lanes] = high


def column_values(block, half):
    lanes = block.shape[-1]
    wide = block.astype(f32)
    if half:
        return wide[:, 0, : lanes // 2].astype(bf16), wide[:, -1, lanes // 2 :].astype(bf16)
    return wide[:, 0, :].astype(bf16), wide[:, -1, :].astype(bf16)


def shifted(values, column, step):
    columns = values.shape[1]
    spot = lax.broadcasted_iota(jnp.int32, values.shape, 1)
    if step > 0:
        return jnp.where(spot == 0, column[:, None, :], pltpu.roll(values, 1, 1))
    return jnp.where(
        spot == columns - 1, column[:, None, :], pltpu.roll(values, columns - 1, 1)
    )


def pair_columns(left, right, plane, lanes):
    first, last = edges("pair")
    low = left[plane, :, lanes].astype(f32)
    high = right[plane, :, lanes].astype(f32)
    return (
        jnp.where(first, jnp.zeros_like(low), low),
        jnp.where(last, jnp.zeros_like(high), high),
    )


def spread_pairs(taps, base, block, low, high):
    lanes = block.shape[-1] // 2
    wide = block.astype(f32)
    taps[:, :, base : base + lanes] = shifted(wide[:, :, lanes:], low, 1).astype(bf16)
    taps[:, :, base + lanes : base + 3 * lanes] = block
    taps[:, :, base + 3 * lanes : base + 4 * lanes] = shifted(
        wide[:, :, :lanes], high, -1
    ).astype(bf16)


def spread_weights(packed, tap, base, taken):
    rows, outs = taken[0].shape
    blank = jnp.zeros((rows, outs), bf16)
    for cell in range(4):
        at = base + cell * rows
        packed[tap, at : at + rows, :outs] = taken[cell] if cell < 3 else blank
        packed[tap, at : at + rows, outs:] = taken[cell - 1] if cell > 0 else blank


def conv_rows(taps, packed, depth, height):
    lanes = taps.shape[-1]
    summed = None
    for a in range(3):
        for b in range(3):
            rows = taps[a : a + depth, b : b + height].reshape(-1, lanes)
            part = jnp.dot(rows, packed[3 * a + b], preferred_element_type=f32)
            summed = part if summed is None else summed + part
    return summed


def frame_kernel(own, low, high, ahead, behind, ext, columns):
    fill_frame(ext, own, low[...], high[...], ahead[...], behind[...], 1, 1)
    for plane in range(ext.shape[0]):
        left, right = column_values(ext[plane], True)
        write_columns(columns, plane, left, right, slice(None))


def encode_kernel(ext, left, right, weight, bias, down, down_bias, encoded, coarse, taps, packed):
    lanes = ext.shape[-1]
    for plane in range(ext.shape[0]):
        low, high = pair_columns(left, right, plane, slice(None))
        spread_pairs(taps.at[plane], 0, ext[plane], low, high)
    for tap in range(9):
        spread_weights(packed, tap, 0, [weight[tap, c] for c in range(3)])
    deep, _, tall, _, columns, _ = encoded.shape
    summed = conv_rows(taps, packed, 2 * deep, 2 * tall)
    summed = leaky_relu(summed + jnp.tile(bias[...], (1, 2))).astype(bf16)
    encoded[...] = summed.reshape(encoded.shape)
    lifted = None
    for a in range(2):
        for b in range(2):
            part = jnp.dot(
                encoded[:, a, :, b].reshape(-1, lanes), down[2 * a + b], preferred_element_type=f32
            )
            lifted = part if lifted is None else lifted + part
    coarse[...] = leaky_relu(lifted + down_bias[...]).astype(bf16).reshape(coarse.shape)


def frame_two_kernel(
    coarse, encoded, low, high, ahead, behind, coarse_ext, encoded_ext, columns
):
    depth, height = coarse.shape[:2]
    flat = 2 * depth
    tail = low.shape[1:]
    split = 2 * coarse_ext.shape[1]

    def planes(ref):
        return (
            ref[:split].reshape((2,) + coarse_ext.shape[1:]),
            ref[split:].reshape((1,) + encoded_ext.shape[1:]),
        )

    def rows(ref):
        return (
            ref[:flat].reshape((depth, 2) + tail),
            ref[flat:].reshape((2 * depth, 1) + tail),
        )

    low_c, low_e = rows(low)
    high_c, high_e = rows(high)
    ahead_c, ahead_e = planes(ahead)
    behind_c, behind_e = planes(behind)
    fill_frame(coarse_ext, coarse, low_c, high_c, ahead_c, behind_c, 2, 2)
    fill_frame(encoded_ext, encoded, low_e, high_e, ahead_e, behind_e, 1, 1)
    for plane in range(coarse_ext.shape[0]):
        left, right = column_values(coarse_ext[plane], False)
        write_columns(columns, plane, left, right, slice(None))


def bottom_kernel(
    coarse_ext, left, right, weight, bias, up, up_bias, encoded_ext, raised, columns, taps
):
    lanes = coarse_ext.shape[-1]
    for plane in range(coarse_ext.shape[0]):
        low, high = pair_columns(left, right, plane, slice(None))
        block = coarse_ext[plane]
        wide = block.astype(f32)
        taps[plane, :, :, :lanes] = shifted(wide, low, 1).astype(bf16)
        taps[plane, :, :, lanes : 2 * lanes] = block
        taps[plane, :, :, 2 * lanes :] = shifted(wide, high, -1).astype(bf16)
    deep, _, tall, _, count, _ = raised.shape
    summed = conv_rows(taps, weight, deep, tall)
    bottom = leaky_relu(summed + bias[...]).astype(bf16)
    both = jnp.tile(up_bias[...], (1, 2))
    for a in range(2):
        for b in range(2):
            matrix = jnp.concatenate([up[2 * a + b, 0], up[2 * a + b, 1]], axis=-1)
            lifted = jnp.dot(bottom, matrix, preferred_element_type=f32) + both
            raised[:, a, :, b] = lifted.astype(bf16).reshape(deep, tall, count, lanes)
    blank_plane = jnp.zeros(raised.shape[1:], bf16)
    blank_row = jnp.zeros((deep, 2, 2, count, lanes), bf16)
    first, last = edges("narrow")

    @pl.when(first)
    def _():
        raised[:, :, 0] = blank_row

    @pl.when(last)
    def _():
        raised[:, :, tall - 1] = blank_row

    first, last = edges("wide")

    @pl.when(first)
    def _():
        raised[0] = blank_plane

    @pl.when(last)
    def _():
        raised[deep - 1] = blank_plane

    planes, height = encoded_ext.shape[:2]
    half = lanes // 2
    for plane in range(planes):
        z, a = (plane + 1) // 2, (plane + 1) % 2
        whole = raised[z, a].reshape(2 * tall, count, lanes)[1 : 1 + height]
        low, high = column_values(whole, True)
        write_columns(columns, plane, low, high, slice(0, half))
        low, high = column_values(encoded_ext[plane], True)
        write_columns(columns, plane, low, high, slice(half, lanes))


def decode_kernel(raised, encoded_ext, left, right, weight, bias, decoded, taps, packed):
    planes, height, columns, lanes = encoded_ext.shape
    half = lanes // 2
    for plane in range(planes):
        low, high = pair_columns(left, right, plane, slice(0, half))
        spread_pairs(taps.at[plane], 0, raised[plane + 1, 1 : 1 + height], low, high)
        low, high = pair_columns(left, right, plane, slice(half, lanes))
        spread_pairs(taps.at[plane], 2 * lanes, encoded_ext[plane], low, high)
    for tap in range(9):
        spread_weights(packed, tap, 0, [weight[tap, c, :half] for c in range(3)])
        spread_weights(packed, tap, 2 * lanes, [weight[tap, c, half:] for c in range(3)])
    depth, rows = decoded.shape[:2]
    summed = conv_rows(taps, packed, depth, rows)
    summed = leaky_relu(summed + jnp.tile(bias[...], (1, 2)))
    decoded[...] = summed.astype(bf16).reshape(decoded.shape)


def rows_of(block, low, high, tall):
    return line_exchange("narrow", block[:, :tall], block[:, block.shape[1] - tall :])


def frame_planes(block, low, high, deep):
    depth = block.shape[0]
    return tuple(
        jnp.concatenate([low[at], block[at], high[at]], axis=1)
        for at in (slice(0, deep), slice(depth - deep, depth))
    )


def pair_exchange(columns):
    return line_exchange("pair", columns[0], columns[-1])


def body(
    volume, w_encode, b_encode, w_down, b_down, w_bottom, b_bottom, w_up, b_up, w_decode, b_decode
):
    depth, height, width, skip = volume.shape
    deep_width = w_down.shape[4]
    half_depth, half_height, pairs = depth // 2, height // 2, width // 2
    lanes = 2 * skip
    sides = 1 if lax.axis_size("pair") == 2 else 2

    packed = volume.reshape(depth, height, pairs, lanes)
    low, high = line_exchange("narrow", packed[:, :1], packed[:, -1:])
    ahead, behind = wide_exchange(*frame_planes(packed, low, high, 1))
    framed, columns = call(
        frame_kernel,
        [(depth + 2, height + 2, pairs, lanes), (sides, depth + 2, height + 2, skip)],
    )(packed, low, high, ahead, behind)
    left, right = pair_exchange(columns)

    encoded, coarse = call(
        encode_kernel,
        [
            (half_depth, 2, half_height, 2, pairs, lanes),
            (half_depth, half_height, pairs, deep_width),
        ],
        [
            pltpu.VMEM((depth + 2, height + 2, pairs, 2 * lanes), bf16),
            pltpu.VMEM((9, 2 * lanes, lanes), bf16),
        ],
    )(
        framed,
        left,
        right,
        w_encode.reshape(9, 3, skip, skip),
        b_encode.reshape(1, skip),
        w_down.reshape(4, lanes, deep_width),
        b_down.reshape(1, deep_width),
    )
    encoded = encoded.reshape(depth, height, pairs, lanes)

    def rows(start_c, start_e):
        c = lax.slice_in_dim(coarse, start_c, start_c + 2, axis=1)
        e = lax.slice_in_dim(encoded, start_e, start_e + 1, axis=1)
        return jnp.concatenate(
            [c.reshape(-1, pairs, deep_width), e.reshape(-1, pairs, lanes)], axis=0
        )

    low, high = line_exchange(
        "narrow", rows(0, 0), rows(half_height - 2, height - 1)
    )
    split = 2 * half_depth

    def parts(got):
        return (
            got[:split].reshape(half_depth, 2, pairs, deep_width),
            got[split:].reshape(depth, 1, pairs, lanes),
        )

    (low_c, low_e), (high_c, high_e) = parts(low), parts(high)
    sent = [
        jnp.concatenate(
            [c.reshape(-1, pairs, deep_width), e.reshape(-1, pairs, lanes)], axis=0
        )
        for c, e in zip(
            frame_planes(coarse, low_c, high_c, 2), frame_planes(encoded, low_e, high_e, 1)
        )
    ]
    ahead, behind = wide_exchange(*sent)
    coarse_ext, encoded_ext, columns = call(
        frame_two_kernel,
        [
            (half_depth + 4, half_height + 4, pairs, deep_width),
            (depth + 2, height + 2, pairs, lanes),
            (sides, half_depth + 4, half_height + 4, deep_width),
        ],
    )(coarse, encoded, low, high, ahead, behind)
    left, right = pair_exchange(columns)

    raised, columns = call(
        bottom_kernel,
        [
            (half_depth + 2, 2, half_height + 2, 2, pairs, lanes),
            (sides, depth + 2, height + 2, lanes),
        ],
        [pltpu.VMEM((half_depth + 4, half_height + 4, pairs, 3 * deep_width), bf16)],
    )(
        coarse_ext,
        left,
        right,
        w_bottom.reshape(9, 3 * deep_width, deep_width),
        b_bottom.reshape(1, deep_width),
        w_up.reshape(4, 2, deep_width, skip),
        b_up.reshape(1, skip),
        encoded_ext,
    )
    left, right = pair_exchange(columns)

    (decoded,) = call(
        decode_kernel,
        [(depth, height, pairs, lanes)],
        [
            pltpu.VMEM((depth + 2, height + 2, pairs, 4 * lanes), bf16),
            pltpu.VMEM((9, 4 * lanes, lanes), bf16),
        ],
    )(
        raised.reshape(depth + 4, height + 4, pairs, lanes),
        encoded_ext,
        left,
        right,
        w_decode.reshape(9, 3, lanes, skip),
        b_decode.reshape(1, skip),
    )
    return decoded.reshape(depth, height, width, skip)


def solution(mesh):
    return jax.shard_map(
        body,
        mesh=mesh,
        in_specs=(
            P(("groups", "wide"), "narrow", "pair", None),
            P(),
            P(),
            P(),
            P(),
            P(),
            P(),
            P(),
            P(),
            P(),
            P(),
        ),
        out_specs=P(("groups", "wide"), "narrow", "pair", None),
        check_vma=False,
    )
```

```python
import functools

import jax
import jax.numpy as jnp
from jax import lax
from jax.experimental import pallas as pl
from jax.experimental.pallas import tpu as pltpu
from jax.sharding import PartitionSpec as P

leak_slope = 0.01
f32 = jnp.float32
bf16 = jnp.bfloat16


def leaky_relu(values):
    return jnp.maximum(values, leak_slope * values)


def sides_of(axis):
    return 1 if lax.axis_size(axis) == 2 else 2


def line_exchange(axis, sent):
    count = lax.axis_size(axis)
    if count == 2:
        got = lax.ppermute(sent[0], axis, [(0, 1), (1, 0)])
        return got, got
    up = [(i, i + 1) for i in range(count - 1)]
    down = [(b, a) for a, b in up]
    return lax.ppermute(sent[1], axis, up), lax.ppermute(sent[0], axis, down)


def snake_pairs(groups, count, step):
    order = [
        group * count + (place if group % 2 == 0 else count - 1 - place)
        for group in range(groups)
        for place in range(count)
    ]
    total = len(order)
    return [(order[i], order[(i + step) % total]) for i in range(total)]


def wide_exchange(ahead, behind):
    groups, count = lax.axis_size("groups"), lax.axis_size("wide")
    axes = ("groups", "wide")
    return (
        lax.ppermute(ahead, axes, snake_pairs(groups, count, 1)),
        lax.ppermute(behind, axes, snake_pairs(groups, count, -1)),
    )


def call(kernel, outs, scratch=(), megabytes=24):
    return pl.pallas_call(
        kernel,
        out_shape=[jax.ShapeDtypeStruct(shape, bf16) for shape in outs],
        scratch_shapes=list(scratch),
        compiler_params=pltpu.CompilerParams(vmem_limit_bytes=megabytes << 20),
    )


def edges(axis):
    place = lax.axis_index(axis)
    return place == 0, place == lax.axis_size(axis) - 1


def fill_frame(ext, own, rows_low, rows_high, planes_ahead, planes_behind, deep, tall):
    depth, height = own.shape[0], own.shape[1]
    ext[deep : deep + depth, tall : tall + height] = own[...]
    ext[deep : deep + depth, :tall] = rows_low
    ext[deep : deep + depth, tall + height :] = rows_high
    even = lax.axis_index("groups") % 2 == 0

    @pl.when(even)
    def _():
        ext[:deep] = planes_ahead
        ext[deep + depth :] = planes_behind

    @pl.when(jnp.logical_not(even))
    def _():
        ext[:deep] = planes_behind
        ext[deep + depth :] = planes_ahead

    first, last = edges("narrow")

    @pl.when(first)
    def _():
        ext[:, :tall] = jnp.zeros((ext.shape[0], tall) + ext.shape[2:], bf16)

    @pl.when(last)
    def _():
        ext[:, tall + height :] = jnp.zeros((ext.shape[0], tall) + ext.shape[2:], bf16)

    first, last = edges("wide")

    @pl.when(first)
    def _():
        ext[:deep] = jnp.zeros((deep,) + ext.shape[1:], bf16)

    @pl.when(last)
    def _():
        ext[deep + depth :] = jnp.zeros((deep,) + ext.shape[1:], bf16)


def write_columns(columns, plane, low, high, lanes):
    if columns.shape[0] == 1:
        at_low = lax.axis_index("pair") == 0
        columns[0, plane, :, lanes] = jnp.where(at_low, high, low)
    else:
        columns[0, plane, :, lanes] = low
        columns[1, plane, :, lanes] = high


def column_values(block, half):
    lanes = block.shape[-1]
    wide = block.astype(f32)
    if half:
        return wide[:, 0, : lanes // 2].astype(bf16), wide[:, -1, lanes // 2 :].astype(bf16)
    return wide[:, 0, :].astype(bf16), wide[:, -1, :].astype(bf16)


def shifted(values, column, step):
    columns = values.shape[1]
    spot = lax.broadcasted_iota(jnp.int32, values.shape, 1)
    if step > 0:
        return jnp.where(spot == 0, column[:, None, :], pltpu.roll(values, 1, 1))
    return jnp.where(
        spot == columns - 1, column[:, None, :], pltpu.roll(values, columns - 1, 1)
    )


def pair_columns(left, right, plane, lanes):
    first, last = edges("pair")
    low = left[plane, :, lanes].astype(f32)
    high = right[plane, :, lanes].astype(f32)
    return (
        jnp.where(first, jnp.zeros_like(low), low),
        jnp.where(last, jnp.zeros_like(high), high),
    )


def spread_pairs(taps, base, block, low, high):
    lanes = block.shape[-1] // 2
    wide = block.astype(f32)
    taps[:, :, base : base + lanes] = shifted(wide[:, :, lanes:], low, 1).astype(bf16)
    taps[:, :, base + lanes : base + 3 * lanes] = block
    taps[:, :, base + 3 * lanes : base + 4 * lanes] = shifted(
        wide[:, :, :lanes], high, -1
    ).astype(bf16)


def spread_weights(packed, tap, base, taken):
    rows, outs = taken[0].shape
    blank = jnp.zeros((rows, outs), bf16)
    for cell in range(4):
        at = base + cell * rows
        packed[tap, at : at + rows, :outs] = taken[cell] if cell < 3 else blank
        packed[tap, at : at + rows, outs:] = taken[cell - 1] if cell > 0 else blank


def conv_rows(taps, packed, depth, height):
    lanes = taps.shape[-1]
    summed = None
    for a in range(3):
        for b in range(3):
            rows = taps[a : a + depth, b : b + height].reshape(-1, lanes)
            part = jnp.dot(rows, packed[3 * a + b], preferred_element_type=f32)
            summed = part if summed is None else summed + part
    return summed


def choose_side(axis, sent, put):
    if sent.shape[0] == 1:
        at_low = lax.axis_index(axis) == 0

        @pl.when(at_low)
        def _():
            put(0, True)

        @pl.when(jnp.logical_not(at_low))
        def _():
            put(0, False)

    else:
        put(0, False)
        put(1, True)


def pack_pairs(out, cells, spread):
    pairs, lanes = out.shape[1], cells.shape[-1]
    spread[...] = cells.astype(f32)
    for odd in range(2):
        half = spread[:, pl.ds(odd, pairs, stride=2), :]
        out[:, :, odd * lanes : (odd + 1) * lanes] = half.astype(bf16)


def edge_row_kernel(volume, edge_rows, spread):
    height = volume.shape[1]

    def put(slot, high):
        pack_pairs(edge_rows.at[slot], volume[:, height - 1 if high else 0], spread)

    choose_side("narrow", edge_rows, put)


def pack_kernel(volume, packed, spread):
    for plane in range(volume.shape[0]):
        pack_pairs(packed.at[plane], volume[plane], spread.at[plane])


def put_planes(ahead, behind, put):
    even = lax.axis_index("groups") % 2 == 0

    @pl.when(even)
    def _():
        put(ahead, True)
        put(behind, False)

    @pl.when(jnp.logical_not(even))
    def _():
        put(ahead, False)
        put(behind, True)


def edge_plane_kernel(own, low, high, ahead, behind):
    depth, height = own.shape[:2]

    def put(ref, top):
        plane = depth - 1 if top else 0
        ref[0, :1] = low[plane][None]
        ref[0, 1 : 1 + height] = own[plane]
        ref[0, 1 + height :] = high[plane][None]

    put_planes(ahead, behind, put)


def edge_plane_two_kernel(coarse, encoded, low, high, ahead, behind):
    deep, tall = coarse.shape[:2]
    depth, height = encoded.shape[:2]
    step = tall + 4
    split = 2 * step

    def put(ref, top):
        for layer in range(2):
            plane = deep - 2 + layer if top else layer
            at = layer * step
            ref[at : at + 2] = low[2 * plane : 2 * plane + 2]
            ref[at + 2 : at + 2 + tall] = coarse[plane]
            ref[at + 2 + tall : at + step] = high[2 * plane : 2 * plane + 2]
        plane = depth - 1 if top else 0
        ref[split] = low[2 * deep + plane]
        ref[split + 1 : split + 1 + height] = encoded[plane]
        ref[split + 1 + height] = high[2 * deep + plane]

    put_planes(ahead, behind, put)


def frame_kernel(own, low, high, ahead, behind, ext, columns):
    fill_frame(ext, own, low[...][:, None], high[...][:, None], ahead[...], behind[...], 1, 1)
    for plane in range(ext.shape[0]):
        left, right = column_values(ext[plane], True)
        write_columns(columns, plane, left, right, slice(None))


def encode_kernel(
    ext, left, right, weight, bias, down, down_bias, encoded, coarse, edge_rows, taps, packed
):
    lanes = ext.shape[-1]
    for plane in range(ext.shape[0]):
        low, high = pair_columns(left, right, plane, slice(None))
        spread_pairs(taps.at[plane], 0, ext[plane], low, high)
    for tap in range(9):
        spread_weights(packed, tap, 0, [weight[tap, c] for c in range(3)])
    depth, height, columns, _ = encoded.shape
    deep, tall, _, deep_lanes = coarse.shape
    summed = conv_rows(taps, packed, depth, height)
    fine = leaky_relu(summed + jnp.tile(bias[...], (1, 2))).astype(bf16)
    fine = fine.reshape(deep, 2, tall, 2, columns, lanes)
    encoded[...] = fine.reshape(encoded.shape)
    lifted = None
    for a in range(2):
        for b in range(2):
            part = jnp.dot(
                fine[:, a, :, b].reshape(-1, lanes), down[2 * a + b], preferred_element_type=f32
            )
            lifted = part if lifted is None else lifted + part
    coarse[...] = leaky_relu(lifted + down_bias[...]).astype(bf16).reshape(coarse.shape)

    def put(slot, high):
        first = tall - 2 if high else 0
        edge_rows[slot, : 2 * deep] = coarse[:, first : first + 2].reshape(
            2 * deep, columns, deep_lanes
        )
        edge_rows[slot, 2 * deep :] = encoded[:, height - 1 if high else 0]

    choose_side("narrow", edge_rows, put)


def frame_two_kernel(
    coarse, encoded, low, high, ahead, behind, coarse_ext, encoded_ext, columns
):
    depth, height = coarse.shape[:2]
    flat = 2 * depth
    tail = low.shape[1:]
    split = 2 * coarse_ext.shape[1]

    def planes(ref):
        return (
            ref[:split].reshape((2,) + coarse_ext.shape[1:]),
            ref[split:].reshape((1,) + encoded_ext.shape[1:]),
        )

    def rows(ref):
        return (
            ref[:flat].reshape((depth, 2) + tail),
            ref[flat:].reshape((2 * depth, 1) + tail),
        )

    low_c, low_e = rows(low)
    high_c, high_e = rows(high)
    ahead_c, ahead_e = planes(ahead)
    behind_c, behind_e = planes(behind)
    fill_frame(coarse_ext, coarse, low_c, high_c, ahead_c, behind_c, 2, 2)
    fill_frame(encoded_ext, encoded, low_e, high_e, ahead_e, behind_e, 1, 1)
    for plane in range(coarse_ext.shape[0]):
        left, right = column_values(coarse_ext[plane], False)
        write_columns(columns, plane, left, right, slice(None))


def bottom_kernel(
    coarse_ext, left, right, weight, bias, up, up_bias, encoded_ext, raised, columns, taps
):
    lanes = coarse_ext.shape[-1]
    for plane in range(coarse_ext.shape[0]):
        low, high = pair_columns(left, right, plane, slice(None))
        block = coarse_ext[plane]
        wide = block.astype(f32)
        taps[plane, :, :, :lanes] = shifted(wide, low, 1).astype(bf16)
        taps[plane, :, :, lanes : 2 * lanes] = block
        taps[plane, :, :, 2 * lanes :] = shifted(wide, high, -1).astype(bf16)
    deep, _, tall, _, count, _ = raised.shape
    summed = conv_rows(taps, weight, deep, tall)
    bottom = leaky_relu(summed + bias[...]).astype(bf16)
    both = jnp.tile(up_bias[...], (1, 2))
    for a in range(2):
        for b in range(2):
            matrix = jnp.concatenate([up[2 * a + b, 0], up[2 * a + b, 1]], axis=-1)
            lifted = jnp.dot(bottom, matrix, preferred_element_type=f32) + both
            raised[:, a, :, b] = lifted.astype(bf16).reshape(deep, tall, count, lanes)
    blank_plane = jnp.zeros(raised.shape[1:], bf16)
    blank_row = jnp.zeros((deep, 2, 2, count, lanes), bf16)
    first, last = edges("narrow")

    @pl.when(first)
    def _():
        raised[:, :, 0] = blank_row

    @pl.when(last)
    def _():
        raised[:, :, tall - 1] = blank_row

    first, last = edges("wide")

    @pl.when(first)
    def _():
        raised[0] = blank_plane

    @pl.when(last)
    def _():
        raised[deep - 1] = blank_plane

    planes, height = encoded_ext.shape[:2]
    half = lanes // 2
    for plane in range(planes):
        z, a = (plane + 1) // 2, (plane + 1) % 2
        whole = raised[z, a].reshape(2 * tall, count, lanes)[1 : 1 + height]
        low, high = column_values(whole, True)
        write_columns(columns, plane, low, high, slice(0, half))
        low, high = column_values(encoded_ext[plane], True)
        write_columns(columns, plane, low, high, slice(half, lanes))


def decode_kernel(
    raised, encoded_ext, left, right, weight, bias, decoded, taps, packed, spread
):
    planes, height, columns, lanes = encoded_ext.shape
    half = lanes // 2
    for plane in range(planes):
        low, high = pair_columns(left, right, plane, slice(0, half))
        spread_pairs(taps.at[plane], 0, raised[plane + 1, 1 : 1 + height], low, high)
        low, high = pair_columns(left, right, plane, slice(half, lanes))
        spread_pairs(taps.at[plane], 2 * lanes, encoded_ext[plane], low, high)
    for tap in range(9):
        spread_weights(packed, tap, 0, [weight[tap, c, :half] for c in range(3)])
        spread_weights(packed, tap, 2 * lanes, [weight[tap, c, half:] for c in range(3)])
    depth, rows, _, outs = decoded.shape
    summed = conv_rows(taps, packed, depth, rows)
    summed = leaky_relu(summed + jnp.tile(bias[...], (1, 2)))
    for odd in range(2):
        half = summed[:, odd * outs : (odd + 1) * outs].reshape(depth, rows, columns, outs)
        spread[:, :, pl.ds(odd, columns, stride=2), :] = half
    decoded[...] = spread[...].astype(bf16)


def body(
    volume, w_encode, b_encode, w_down, b_down, w_bottom, b_bottom, w_up, b_up, w_decode, b_decode
):
    depth, height, width, skip = volume.shape
    deep_width = w_down.shape[4]
    half_depth, half_height, pairs = depth // 2, height // 2, width // 2
    lanes = 2 * skip
    sides, row_sides = sides_of("pair"), sides_of("narrow")

    (edge_rows,) = call(
        edge_row_kernel,
        [(row_sides, depth, pairs, lanes)],
        [pltpu.VMEM((depth, width, skip), f32)],
        8,
    )(volume)
    low, high = line_exchange("narrow", edge_rows)
    (packed,) = call(
        pack_kernel,
        [(depth, height, pairs, lanes)],
        [pltpu.VMEM((depth, height, width, skip), f32)],
        8,
    )(volume)
    ahead, behind = call(edge_plane_kernel, [(1, height + 2, pairs, lanes)] * 2, (), 8)(
        packed, low, high
    )
    ahead, behind = wide_exchange(ahead, behind)
    framed, columns = call(
        frame_kernel,
        [(depth + 2, height + 2, pairs, lanes), (sides, depth + 2, height + 2, skip)],
    )(packed, low, high, ahead, behind)
    left, right = line_exchange("pair", columns)

    encoded, coarse, edge_rows = call(
        encode_kernel,
        [
            (depth, height, pairs, lanes),
            (half_depth, half_height, pairs, deep_width),
            (row_sides, 2 * half_depth + depth, pairs, lanes),
        ],
        [
            pltpu.VMEM((depth + 2, height + 2, pairs, 2 * lanes), bf16),
            pltpu.VMEM((9, 2 * lanes, lanes), bf16),
        ],
    )(
        framed,
        left,
        right,
        w_encode.reshape(9, 3, skip, skip),
        b_encode.reshape(1, skip),
        w_down.reshape(4, lanes, deep_width),
        b_down.reshape(1, deep_width),
    )
    low, high = line_exchange("narrow", edge_rows)
    message = (2 * (half_height + 4) + height + 2, pairs, lanes)
    ahead, behind = call(edge_plane_two_kernel, [message] * 2, (), 8)(coarse, encoded, low, high)
    ahead, behind = wide_exchange(ahead, behind)
    coarse_ext, encoded_ext, columns = call(
        frame_two_kernel,
        [
            (half_depth + 4, half_height + 4, pairs, deep_width),
            (depth + 2, height + 2, pairs, lanes),
            (sides, half_depth + 4, half_height + 4, deep_width),
        ],
    )(coarse, encoded, low, high, ahead, behind)
    left, right = line_exchange("pair", columns)

    raised, columns = call(
        bottom_kernel,
        [
            (half_depth + 2, 2, half_height + 2, 2, pairs, lanes),
            (sides, depth + 2, height + 2, lanes),
        ],
        [pltpu.VMEM((half_depth + 4, half_height + 4, pairs, 3 * deep_width), bf16)],
    )(
        coarse_ext,
        left,
        right,
        w_bottom.reshape(9, 3 * deep_width, deep_width),
        b_bottom.reshape(1, deep_width),
        w_up.reshape(4, 2, deep_width, skip),
        b_up.reshape(1, skip),
        encoded_ext,
    )
    left, right = line_exchange("pair", columns)

    (decoded,) = call(
        decode_kernel,
        [(depth, height, width, skip)],
        [
            pltpu.VMEM((depth + 2, height + 2, pairs, 4 * lanes), bf16),
            pltpu.VMEM((9, 4 * lanes, lanes), bf16),
            pltpu.VMEM((depth, height, width, skip), f32),
        ],
    )(
        raised.reshape(depth + 4, height + 4, pairs, lanes),
        encoded_ext,
        left,
        right,
        w_decode.reshape(9, 3, lanes, skip),
        b_decode.reshape(1, skip),
    )
    return decoded


def solution(mesh):
    return jax.shard_map(
        body,
        mesh=mesh,
        in_specs=(
            P(("groups", "wide"), "narrow", "pair", None),
            P(),
            P(),
            P(),
            P(),
            P(),
            P(),
            P(),
            P(),
            P(),
            P(),
        ),
        out_specs=P(("groups", "wide"), "narrow", "pair", None),
        check_vma=False,
    )
```

```python
import functools

import jax
import jax.numpy as jnp
from jax import lax
from jax.experimental import pallas as pl
from jax.experimental.pallas import tpu as pltpu
from jax.sharding import PartitionSpec as P

leak_slope = 0.01
f32 = jnp.float32
bf16 = jnp.bfloat16


def leaky_relu(values):
    return jnp.maximum(values, leak_slope * values)


def sides_of(axis):
    return 1 if lax.axis_size(axis) == 2 else 2


def line_exchange(axis, sent):
    count = lax.axis_size(axis)
    if count == 2:
        got = lax.ppermute(sent[0], axis, [(0, 1), (1, 0)])
        return got, got
    up = [(i, i + 1) for i in range(count - 1)]
    down = [(b, a) for a, b in up]
    return lax.ppermute(sent[1], axis, up), lax.ppermute(sent[0], axis, down)


def snake_pairs(groups, count, step):
    order = [
        group * count + (place if group % 2 == 0 else count - 1 - place)
        for group in range(groups)
        for place in range(count)
    ]
    total = len(order)
    return [(order[i], order[(i + step) % total]) for i in range(total)]


def wide_exchange(ahead, behind):
    groups, count = lax.axis_size("groups"), lax.axis_size("wide")
    axes = ("groups", "wide")
    return (
        lax.ppermute(ahead, axes, snake_pairs(groups, count, 1)),
        lax.ppermute(behind, axes, snake_pairs(groups, count, -1)),
    )


def call(kernel, outs, scratch=(), megabytes=24):
    return pl.pallas_call(
        kernel,
        out_shape=[jax.ShapeDtypeStruct(shape, bf16) for shape in outs],
        scratch_shapes=list(scratch),
        cost_estimate=pl.CostEstimate(flops=4 * 10**9, transcendentals=0, bytes_accessed=10**6),
        compiler_params=pltpu.CompilerParams(vmem_limit_bytes=megabytes << 20),
    )


def edges(axis):
    place = lax.axis_index(axis)
    return place == 0, place == lax.axis_size(axis) - 1


def fill_frame(ext, own, rows_low, rows_high, planes_ahead, planes_behind, deep, tall):
    depth, height = own.shape[0], own.shape[1]
    ext[deep : deep + depth, tall : tall + height] = own[...]
    ext[deep : deep + depth, :tall] = rows_low
    ext[deep : deep + depth, tall + height :] = rows_high
    even = lax.axis_index("groups") % 2 == 0

    @pl.when(even)
    def _():
        ext[:deep] = planes_ahead
        ext[deep + depth :] = planes_behind

    @pl.when(jnp.logical_not(even))
    def _():
        ext[:deep] = planes_behind
        ext[deep + depth :] = planes_ahead

    first, last = edges("narrow")

    @pl.when(first)
    def _():
        ext[:, :tall] = jnp.zeros((ext.shape[0], tall) + ext.shape[2:], bf16)

    @pl.when(last)
    def _():
        ext[:, tall + height :] = jnp.zeros((ext.shape[0], tall) + ext.shape[2:], bf16)

    first, last = edges("wide")

    @pl.when(first)
    def _():
        ext[:deep] = jnp.zeros((deep,) + ext.shape[1:], bf16)

    @pl.when(last)
    def _():
        ext[deep + depth :] = jnp.zeros((deep,) + ext.shape[1:], bf16)


def write_columns(columns, plane, low, high, lanes):
    if columns.shape[0] == 1:
        at_low = lax.axis_index("pair") == 0
        columns[0, plane, :, lanes] = jnp.where(at_low, high, low)
    else:
        columns[0, plane, :, lanes] = low
        columns[1, plane, :, lanes] = high


def column_values(block, half):
    lanes = block.shape[-1]
    wide = block.astype(f32)
    if half:
        return wide[:, 0, : lanes // 2].astype(bf16), wide[:, -1, lanes // 2 :].astype(bf16)
    return wide[:, 0, :].astype(bf16), wide[:, -1, :].astype(bf16)


def shifted(values, column, step):
    columns = values.shape[1]
    spot = lax.broadcasted_iota(jnp.int32, values.shape, 1)
    if step > 0:
        return jnp.where(spot == 0, column[:, None, :], pltpu.roll(values, 1, 1))
    return jnp.where(
        spot == columns - 1, column[:, None, :], pltpu.roll(values, columns - 1, 1)
    )


def pair_columns(left, right, plane, lanes):
    first, last = edges("pair")
    low = left[plane, :, lanes].astype(f32)
    high = right[plane, :, lanes].astype(f32)
    return (
        jnp.where(first, jnp.zeros_like(low), low),
        jnp.where(last, jnp.zeros_like(high), high),
    )


def spread_pairs(taps, base, block, low, high):
    lanes = block.shape[-1] // 2
    wide = block.astype(f32)
    taps[:, :, base : base + lanes] = shifted(wide[:, :, lanes:], low, 1).astype(bf16)
    taps[:, :, base + lanes : base + 3 * lanes] = block
    taps[:, :, base + 3 * lanes : base + 4 * lanes] = shifted(
        wide[:, :, :lanes], high, -1
    ).astype(bf16)


def spread_weights(packed, tap, base, taken):
    rows, outs = taken[0].shape
    blank = jnp.zeros((rows, outs), bf16)
    for cell in range(4):
        at = base + cell * rows
        packed[tap, at : at + rows, :outs] = taken[cell] if cell < 3 else blank
        packed[tap, at : at + rows, outs:] = taken[cell - 1] if cell > 0 else blank


def conv_rows(taps, packed, depth, height):
    lanes = taps.shape[-1]
    summed = None
    for a in range(3):
        for b in range(3):
            rows = taps[a : a + depth, b : b + height].reshape(-1, lanes)
            part = jnp.dot(rows, packed[3 * a + b], preferred_element_type=f32)
            summed = part if summed is None else summed + part
    return summed


def choose_side(axis, sent, put):
    if sent.shape[0] == 1:
        at_low = lax.axis_index(axis) == 0

        @pl.when(at_low)
        def _():
            put(0, True)

        @pl.when(jnp.logical_not(at_low))
        def _():
            put(0, False)

    else:
        put(0, False)
        put(1, True)


def pack_pairs(out, cells, spread):
    pairs, lanes = out.shape[1], cells.shape[-1]
    spread[...] = cells.astype(f32)
    for odd in range(2):
        half = spread[:, pl.ds(odd, pairs, stride=2), :]
        out[:, :, odd * lanes : (odd + 1) * lanes] = half.astype(bf16)


def edge_row_kernel(volume, edge_rows, spread):
    height = volume.shape[1]

    def put(slot, high):
        pack_pairs(edge_rows.at[slot], volume[:, height - 1 if high else 0], spread)

    choose_side("narrow", edge_rows, put)


def pack_kernel(volume, packed, spread):
    for plane in range(volume.shape[0]):
        pack_pairs(packed.at[plane], volume[plane], spread.at[plane])


def put_planes(ahead, behind, put):
    even = lax.axis_index("groups") % 2 == 0

    @pl.when(even)
    def _():
        put(ahead, True)
        put(behind, False)

    @pl.when(jnp.logical_not(even))
    def _():
        put(ahead, False)
        put(behind, True)


def edge_plane_kernel(own, low, high, ahead, behind):
    depth, height = own.shape[:2]

    def put(ref, top):
        plane = depth - 1 if top else 0
        ref[0, :1] = low[plane][None]
        ref[0, 1 : 1 + height] = own[plane]
        ref[0, 1 + height :] = high[plane][None]

    put_planes(ahead, behind, put)


def edge_plane_two_kernel(coarse, encoded, low, high, ahead, behind):
    deep, tall = coarse.shape[:2]
    depth, height = encoded.shape[:2]
    step = tall + 4
    split = 2 * step

    def put(ref, top):
        for layer in range(2):
            plane = deep - 2 + layer if top else layer
            at = layer * step
            ref[at : at + 2] = low[2 * plane : 2 * plane + 2]
            ref[at + 2 : at + 2 + tall] = coarse[plane]
            ref[at + 2 + tall : at + step] = high[2 * plane : 2 * plane + 2]
        plane = depth - 1 if top else 0
        ref[split] = low[2 * deep + plane]
        ref[split + 1 : split + 1 + height] = encoded[plane]
        ref[split + 1 + height] = high[2 * deep + plane]

    put_planes(ahead, behind, put)


def frame_kernel(own, low, high, ahead, behind, ext, columns):
    fill_frame(ext, own, low[...][:, None], high[...][:, None], ahead[...], behind[...], 1, 1)
    for plane in range(ext.shape[0]):
        left, right = column_values(ext[plane], True)
        write_columns(columns, plane, left, right, slice(None))


def encode_kernel(
    ext, left, right, weight, bias, down, down_bias, encoded, coarse, edge_rows, taps, packed
):
    lanes = ext.shape[-1]
    for plane in range(ext.shape[0]):
        low, high = pair_columns(left, right, plane, slice(None))
        spread_pairs(taps.at[plane], 0, ext[plane], low, high)
    for tap in range(9):
        spread_weights(packed, tap, 0, [weight[tap, c] for c in range(3)])
    depth, height, columns, _ = encoded.shape
    deep, tall, _, deep_lanes = coarse.shape
    summed = conv_rows(taps, packed, depth, height)
    fine = leaky_relu(summed + jnp.tile(bias[...], (1, 2))).astype(bf16)
    fine = fine.reshape(deep, 2, tall, 2, columns, lanes)
    encoded[...] = fine.reshape(encoded.shape)
    lifted = None
    for a in range(2):
        for b in range(2):
            part = jnp.dot(
                fine[:, a, :, b].reshape(-1, lanes), down[2 * a + b], preferred_element_type=f32
            )
            lifted = part if lifted is None else lifted + part
    coarse[...] = leaky_relu(lifted + down_bias[...]).astype(bf16).reshape(coarse.shape)

    def put(slot, high):
        first = tall - 2 if high else 0
        edge_rows[slot, : 2 * deep] = coarse[:, first : first + 2].reshape(
            2 * deep, columns, deep_lanes
        )
        edge_rows[slot, 2 * deep :] = encoded[:, height - 1 if high else 0]

    choose_side("narrow", edge_rows, put)


def frame_two_kernel(
    coarse, encoded, low, high, ahead, behind, coarse_ext, encoded_ext, columns
):
    depth, height = coarse.shape[:2]
    flat = 2 * depth
    tail = low.shape[1:]
    split = 2 * coarse_ext.shape[1]

    def planes(ref):
        return (
            ref[:split].reshape((2,) + coarse_ext.shape[1:]),
            ref[split:].reshape((1,) + encoded_ext.shape[1:]),
        )

    def rows(ref):
        return (
            ref[:flat].reshape((depth, 2) + tail),
            ref[flat:].reshape((2 * depth, 1) + tail),
        )

    low_c, low_e = rows(low)
    high_c, high_e = rows(high)
    ahead_c, ahead_e = planes(ahead)
    behind_c, behind_e = planes(behind)
    fill_frame(coarse_ext, coarse, low_c, high_c, ahead_c, behind_c, 2, 2)
    fill_frame(encoded_ext, encoded, low_e, high_e, ahead_e, behind_e, 1, 1)
    for plane in range(coarse_ext.shape[0]):
        left, right = column_values(coarse_ext[plane], False)
        write_columns(columns, plane, left, right, slice(None))


def bottom_kernel(
    coarse_ext, left, right, weight, bias, up, up_bias, encoded_ext, raised, columns, taps
):
    lanes = coarse_ext.shape[-1]
    for plane in range(coarse_ext.shape[0]):
        low, high = pair_columns(left, right, plane, slice(None))
        block = coarse_ext[plane]
        wide = block.astype(f32)
        taps[plane, :, :, :lanes] = shifted(wide, low, 1).astype(bf16)
        taps[plane, :, :, lanes : 2 * lanes] = block
        taps[plane, :, :, 2 * lanes :] = shifted(wide, high, -1).astype(bf16)
    deep, _, tall, _, count, _ = raised.shape
    summed = conv_rows(taps, weight, deep, tall)
    bottom = leaky_relu(summed + bias[...]).astype(bf16)
    both = jnp.tile(up_bias[...], (1, 2))
    for a in range(2):
        for b in range(2):
            matrix = jnp.concatenate([up[2 * a + b, 0], up[2 * a + b, 1]], axis=-1)
            lifted = jnp.dot(bottom, matrix, preferred_element_type=f32) + both
            raised[:, a, :, b] = lifted.astype(bf16).reshape(deep, tall, count, lanes)
    blank_plane = jnp.zeros(raised.shape[1:], bf16)
    blank_row = jnp.zeros((deep, 2, 2, count, lanes), bf16)
    first, last = edges("narrow")

    @pl.when(first)
    def _():
        raised[:, :, 0] = blank_row

    @pl.when(last)
    def _():
        raised[:, :, tall - 1] = blank_row

    first, last = edges("wide")

    @pl.when(first)
    def _():
        raised[0] = blank_plane

    @pl.when(last)
    def _():
        raised[deep - 1] = blank_plane

    planes, height = encoded_ext.shape[:2]
    half = lanes // 2
    for plane in range(planes):
        z, a = (plane + 1) // 2, (plane + 1) % 2
        whole = raised[z, a].reshape(2 * tall, count, lanes)[1 : 1 + height]
        low, high = column_values(whole, True)
        write_columns(columns, plane, low, high, slice(0, half))
        low, high = column_values(encoded_ext[plane], True)
        write_columns(columns, plane, low, high, slice(half, lanes))


def decode_kernel(
    raised, encoded_ext, left, right, weight, bias, decoded, taps, packed, spread
):
    planes, height, columns, lanes = encoded_ext.shape
    half = lanes // 2
    for plane in range(planes):
        low, high = pair_columns(left, right, plane, slice(0, half))
        spread_pairs(taps.at[plane], 0, raised[plane + 1, 1 : 1 + height], low, high)
        low, high = pair_columns(left, right, plane, slice(half, lanes))
        spread_pairs(taps.at[plane], 2 * lanes, encoded_ext[plane], low, high)
    for tap in range(9):
        spread_weights(packed, tap, 0, [weight[tap, c, :half] for c in range(3)])
        spread_weights(packed, tap, 2 * lanes, [weight[tap, c, half:] for c in range(3)])
    depth, rows, _, outs = decoded.shape
    summed = conv_rows(taps, packed, depth, rows)
    summed = leaky_relu(summed + jnp.tile(bias[...], (1, 2)))
    for odd in range(2):
        half = summed[:, odd * outs : (odd + 1) * outs].reshape(depth, rows, columns, outs)
        spread[:, :, pl.ds(odd, columns, stride=2), :] = half
    decoded[...] = spread[...].astype(bf16)


def body(
    volume, w_encode, b_encode, w_down, b_down, w_bottom, b_bottom, w_up, b_up, w_decode, b_decode
):
    depth, height, width, skip = volume.shape
    deep_width = w_down.shape[4]
    half_depth, half_height, pairs = depth // 2, height // 2, width // 2
    lanes = 2 * skip
    sides, row_sides = sides_of("pair"), sides_of("narrow")

    (edge_rows,) = call(
        edge_row_kernel,
        [(row_sides, depth, pairs, lanes)],
        [pltpu.VMEM((depth, width, skip), f32)],
        8,
    )(volume)
    low, high = line_exchange("narrow", edge_rows)
    (packed,) = call(
        pack_kernel,
        [(depth, height, pairs, lanes)],
        [pltpu.VMEM((depth, height, width, skip), f32)],
        8,
    )(volume)
    ahead, behind = call(edge_plane_kernel, [(1, height + 2, pairs, lanes)] * 2, (), 8)(
        packed, low, high
    )
    ahead, behind = wide_exchange(ahead, behind)
    framed, columns = call(
        frame_kernel,
        [(depth + 2, height + 2, pairs, lanes), (sides, depth + 2, height + 2, skip)],
    )(packed, low, high, ahead, behind)
    left, right = line_exchange("pair", columns)

    encoded, coarse, edge_rows = call(
        encode_kernel,
        [
            (depth, height, pairs, lanes),
            (half_depth, half_height, pairs, deep_width),
            (row_sides, 2 * half_depth + depth, pairs, lanes),
        ],
        [
            pltpu.VMEM((depth + 2, height + 2, pairs, 2 * lanes), bf16),
            pltpu.VMEM((9, 2 * lanes, lanes), bf16),
        ],
    )(
        framed,
        left,
        right,
        w_encode.reshape(9, 3, skip, skip),
        b_encode.reshape(1, skip),
        w_down.reshape(4, lanes, deep_width),
        b_down.reshape(1, deep_width),
    )
    low, high = line_exchange("narrow", edge_rows)
    message = (2 * (half_height + 4) + height + 2, pairs, lanes)
    ahead, behind = call(edge_plane_two_kernel, [message] * 2, (), 8)(coarse, encoded, low, high)
    ahead, behind = wide_exchange(ahead, behind)
    coarse_ext, encoded_ext, columns = call(
        frame_two_kernel,
        [
            (half_depth + 4, half_height + 4, pairs, deep_width),
            (depth + 2, height + 2, pairs, lanes),
            (sides, half_depth + 4, half_height + 4, deep_width),
        ],
    )(coarse, encoded, low, high, ahead, behind)
    left, right = line_exchange("pair", columns)

    raised, columns = call(
        bottom_kernel,
        [
            (half_depth + 2, 2, half_height + 2, 2, pairs, lanes),
            (sides, depth + 2, height + 2, lanes),
        ],
        [pltpu.VMEM((half_depth + 4, half_height + 4, pairs, 3 * deep_width), bf16)],
    )(
        coarse_ext,
        left,
        right,
        w_bottom.reshape(9, 3 * deep_width, deep_width),
        b_bottom.reshape(1, deep_width),
        w_up.reshape(4, 2, deep_width, skip),
        b_up.reshape(1, skip),
        encoded_ext,
    )
    left, right = line_exchange("pair", columns)

    (decoded,) = call(
        decode_kernel,
        [(depth, height, width, skip)],
        [
            pltpu.VMEM((depth + 2, height + 2, pairs, 4 * lanes), bf16),
            pltpu.VMEM((9, 4 * lanes, lanes), bf16),
            pltpu.VMEM((depth, height, width, skip), f32),
        ],
    )(
        raised.reshape(depth + 4, height + 4, pairs, lanes),
        encoded_ext,
        left,
        right,
        w_decode.reshape(9, 3, lanes, skip),
        b_decode.reshape(1, skip),
    )
    return decoded


def solution(mesh):
    return jax.shard_map(
        body,
        mesh=mesh,
        in_specs=(
            P(("groups", "wide"), "narrow", "pair", None),
            P(),
            P(),
            P(),
            P(),
            P(),
            P(),
            P(),
            P(),
            P(),
            P(),
        ),
        out_specs=P(("groups", "wide"), "narrow", "pair", None),
        check_vma=False,
    )
```

```python
import functools

import jax
import jax.numpy as jnp
from jax import lax
from jax.experimental import pallas as pl
from jax.experimental.pallas import tpu as pltpu
from jax.sharding import PartitionSpec as P

leak_slope = 0.01
f32 = jnp.float32
bf16 = jnp.bfloat16


def leaky_relu(values):
    return jnp.maximum(values, leak_slope * values)


def sides_of(axis):
    return 1 if lax.axis_size(axis) == 2 else 2


def line_exchange(axis, sent):
    count = lax.axis_size(axis)
    if count == 2:
        got = lax.ppermute(sent[0], axis, [(0, 1), (1, 0)])
        return got, got
    up = [(i, i + 1) for i in range(count - 1)]
    down = [(b, a) for a, b in up]
    return lax.ppermute(sent[1], axis, up), lax.ppermute(sent[0], axis, down)


def snake_pairs(groups, count, step):
    order = [
        group * count + (place if group % 2 == 0 else count - 1 - place)
        for group in range(groups)
        for place in range(count)
    ]
    total = len(order)
    return [(order[i], order[(i + step) % total]) for i in range(total)]


def ring_exchange(sent):
    groups, count = lax.axis_size("groups"), lax.axis_size("wide")
    pairs = [
        (2 * a + core, 2 * b + core)
        for core, step in ((0, 1), (1, -1))
        for a, b in snake_pairs(groups, count, step)
    ]
    return lax.ppermute(sent, ("groups", "wide", "pair"), pairs)


def corner_exchange(sent):
    groups, count, tall = (lax.axis_size(axis) for axis in ("groups", "wide", "narrow"))
    moves = [(0, 1), (1, 0)] if tall == 2 else [(i, i + 1) for i in range(tall - 1)]

    def move(array, rows):
        pairs = [
            ((a * tall + c) * 2 + core, (b * tall + d) * 2 + core)
            for core, step in ((0, 1), (1, -1))
            for a, b in snake_pairs(groups, count, step)
            for c, d in rows
        ]
        return lax.ppermute(array, ("groups", "wide", "narrow", "pair"), pairs)

    if tall == 2:
        got = move(sent[0], moves)
        return got, got
    return move(sent[1], moves), move(sent[0], [(d, c) for c, d in moves])


def call(kernel, outs, scratch=(), megabytes=24):
    return pl.pallas_call(
        kernel,
        out_shape=[jax.ShapeDtypeStruct(shape, bf16) for shape in outs],
        scratch_shapes=list(scratch),
        cost_estimate=pl.CostEstimate(flops=4 * 10**9, transcendentals=0, bytes_accessed=10**6),
        compiler_params=pltpu.CompilerParams(vmem_limit_bytes=megabytes << 20),
    )


def edges(axis):
    place = lax.axis_index(axis)
    return place == 0, place == lax.axis_size(axis) - 1


def sends_high():
    even = lax.axis_index("groups") % 2 == 0
    return (lax.axis_index("pair") == 0) == even


def either(condition, put):
    @pl.when(condition)
    def _():
        put(True)

    @pl.when(jnp.logical_not(condition))
    def _():
        put(False)


def rows_at(ref, at, *lead):
    count = 1
    for size in lead:
        count *= size
    return ref[at : at + count].reshape(lead + tuple(ref.shape[1:]))


def layout(fields):
    planes, corners, spots = 0, 0, []
    for shape, deep, tall in fields:
        spots.append((planes, corners))
        planes += deep * shape[1]
        corners += deep * tall
    return spots, planes, corners


def fill_planes(ext, base, middle, low, high):
    deep, height = middle.shape[:2]
    tall = low.shape[1]
    ext[base : base + deep, :tall] = low
    ext[base : base + deep, tall : tall + height] = middle
    ext[base : base + deep, tall + height :] = high


def fill_block(ext, own, low, high, at, deep, tall):
    depth = own.shape[0]
    fill_planes(
        ext,
        deep,
        own[...],
        rows_at(low, at, depth, tall),
        rows_at(high, at, depth, tall),
    )


def clear_edges(ext, deep, tall):
    first, last = edges("narrow")
    planes, rows = ext.shape[:2]
    blank_rows = jnp.zeros((planes, tall) + ext.shape[2:], bf16)
    blank_planes = jnp.zeros((deep,) + ext.shape[1:], bf16)

    @pl.when(first)
    def _():
        ext[:, :tall] = blank_rows

    @pl.when(last)
    def _():
        ext[:, rows - tall :] = blank_rows

    first, last = edges("wide")

    @pl.when(first)
    def _():
        ext[:deep] = blank_planes

    @pl.when(last)
    def _():
        ext[planes - deep :] = blank_planes


def fill_frame(ext, own, low, high, planes, corner_low, corner_high, passed, spot, at, deep, tall):
    depth, height = own.shape[:2]
    plane_at, corner_at = spot
    count = corner_low.shape[0] // 2
    split = planes.shape[0] // 2
    fill_block(ext, own, low, high, at, deep, tall)
    near = (
        rows_at(planes, plane_at, deep, height),
        rows_at(corner_low, corner_at, deep, tall),
        rows_at(corner_high, corner_at, deep, tall),
    )
    last = passed.shape[0] - count
    far = (
        rows_at(passed, plane_at, deep, height),
        rows_at(passed, split + corner_at, deep, tall),
        rows_at(passed, last + corner_at, deep, tall),
    )

    either(sends_high(), put_sides(ext, depth, deep, near, far))
    clear_edges(ext, deep, tall)


def put_sides(ext, depth, deep, near, far):
    def put(low_is_near):
        fill_planes(ext, 0, *(near if low_is_near else far))
        fill_planes(ext, deep + depth, *(far if low_is_near else near))

    return put


def fill_columns(columns, got, frame, planes, corner_low, corner_high, spot, height, deep, tall, half):
    plane_at, corner_at = spot
    count, corners = planes.shape[0] // 2, corner_low.shape[0] // 2
    columns[...] = got[...]
    fill_planes(
        frame,
        0,
        rows_at(planes, count + plane_at, deep, height),
        rows_at(corner_low, corners + corner_at, deep, tall),
        rows_at(corner_high, corners + corner_at, deep, tall),
    )
    first, last = edges("narrow")
    blank = jnp.zeros((deep, tall) + frame.shape[2:], bf16)

    @pl.when(first)
    def _():
        frame[:, :tall] = blank

    @pl.when(last)
    def _():
        frame[:, tall + height :] = blank

    at_low = lax.axis_index("pair") == 0
    total = columns.shape[0]
    at_edge = edges("wide")

    def put(low_side):
        edge = at_edge[0] if low_side else at_edge[1]
        for layer in range(deep):
            low, high = column_values(frame[layer], half)
            chosen = jnp.where(at_low, low, high)
            chosen = jnp.where(edge, jnp.zeros_like(chosen), chosen)
            columns[layer if low_side else total - deep + layer] = chosen

    either(sends_high(), put)


def write_columns(columns, plane, low, high, lanes):
    at_low = lax.axis_index("pair") == 0
    columns[plane, :, lanes] = jnp.where(at_low, high, low)


def column_values(block, half):
    lanes = block.shape[-1]
    wide = block.astype(f32)
    if half:
        return wide[:, 0, : lanes // 2].astype(bf16), wide[:, -1, lanes // 2 :].astype(bf16)
    return wide[:, 0, :].astype(bf16), wide[:, -1, :].astype(bf16)


def shifted(values, column, step):
    columns = values.shape[1]
    spot = lax.broadcasted_iota(jnp.int32, values.shape, 1)
    if step > 0:
        return jnp.where(spot == 0, column[:, None, :], pltpu.roll(values, 1, 1))
    return jnp.where(
        spot == columns - 1, column[:, None, :], pltpu.roll(values, columns - 1, 1)
    )


def pair_columns(got, plane, lanes):
    first, last = edges("pair")
    column = got[plane, :, lanes].astype(f32)
    blank = jnp.zeros_like(column)
    return jnp.where(first, blank, column), jnp.where(last, blank, column)


def spread_pairs(taps, base, block, low, high):
    lanes = block.shape[-1] // 2
    wide = block.astype(f32)
    taps[:, :, base : base + lanes] = shifted(wide[:, :, lanes:], low, 1).astype(bf16)
    taps[:, :, base + lanes : base + 3 * lanes] = block
    taps[:, :, base + 3 * lanes : base + 4 * lanes] = shifted(
        wide[:, :, :lanes], high, -1
    ).astype(bf16)


def spread_weights(packed, tap, base, taken):
    rows, outs = taken[0].shape
    blank = jnp.zeros((rows, outs), bf16)
    for cell in range(4):
        at = base + cell * rows
        packed[tap, at : at + rows, :outs] = taken[cell] if cell < 3 else blank
        packed[tap, at : at + rows, outs:] = taken[cell - 1] if cell > 0 else blank


def conv_rows(taps, packed, depth, height):
    lanes = taps.shape[-1]
    summed = None
    for a in range(3):
        for b in range(3):
            rows = taps[a : a + depth, b : b + height].reshape(-1, lanes)
            part = jnp.dot(rows, packed[3 * a + b], preferred_element_type=f32)
            summed = part if summed is None else summed + part
    return summed


def choose_side(axis, sent, put):
    if sent.shape[0] == 1:
        at_low = lax.axis_index(axis) == 0

        @pl.when(at_low)
        def _():
            put(0, True)

        @pl.when(jnp.logical_not(at_low))
        def _():
            put(0, False)

    else:
        put(0, False)
        put(1, True)


def pack_pairs(out, cells, spread):
    pairs, lanes = out.shape[1], cells.shape[-1]
    spread[...] = cells.astype(f32)
    for odd in range(2):
        half = spread[:, pl.ds(odd, pairs, stride=2), :]
        out[:, :, odd * lanes : (odd + 1) * lanes] = half.astype(bf16)


def pack_kernel(volume, packed, spread):
    for plane in range(volume.shape[0]):
        pack_pairs(packed.at[plane], volume[plane], spread.at[plane])


def edge_kernel(sizes, *refs):
    fields, (edge_rows, handed) = refs[: len(sizes)], refs[len(sizes) :]

    def put_rows(slot, high):
        at = 0
        for field, (_, _, tall) in zip(fields, sizes):
            depth, height = field.shape[:2]
            first = height - tall if high else 0
            rows = field[:, first : first + tall]
            edge_rows[slot, at : at + depth * tall] = rows.reshape((depth * tall,) + rows.shape[2:])
            at += depth * tall

    choose_side("narrow", edge_rows, put_rows)
    either(sends_high(), lambda high: put_boundary(handed, fields, sizes, not high))


def put_boundary(out, fields, sizes, high):
    at = 0
    for field, (_, deep, _) in zip(fields, sizes):
        depth, height = field.shape[:2]
        planes = field[depth - deep :] if high else field[:deep]
        out[at : at + deep * height] = planes.reshape((deep * height,) + planes.shape[2:])
        at += deep * height


def plane_kernel(sizes, *refs):
    fields, (handed, planes, corners) = refs[: len(sizes)], refs[len(sizes) :]
    spots, count, few = layout(sizes)
    planes[count:] = handed[...]
    either(sends_high(), lambda high: put_boundary(planes, fields, sizes, high))

    def put(slot, high):
        for (shape, deep, tall), (plane_at, corner_at) in zip(sizes, spots):
            height = shape[1]
            first = height - tall if high else 0
            for part in range(2):
                for layer in range(deep):
                    source = part * count + plane_at + layer * height + first
                    target = part * few + corner_at + layer * tall
                    corners[slot, target : target + tall] = planes[source : source + tall]

    choose_side("narrow", corners, put)


def pass_kernel(sizes, half, *refs):
    own, low, high, planes, corner_low, corner_high, passed, columns, ext = refs
    (shape, deep, tall), (_, count, few) = sizes[0], layout(sizes)
    depth, height = shape[:2]
    passed[:count] = planes[count:]
    passed[count : count + few] = corner_low[few:]
    passed[passed.shape[0] - few :] = corner_high[few:]
    fill_block(ext, own, low, high, 0, deep, tall)
    near = (
        rows_at(planes, 0, deep, height),
        rows_at(corner_low, 0, deep, tall),
        rows_at(corner_high, 0, deep, tall),
    )
    blank = tuple(jnp.zeros_like(part) for part in near)
    either(sends_high(), put_sides(ext, depth, deep, near, blank))
    clear_edges(ext, deep, tall)
    for plane in range(ext.shape[0]):
        left, right = column_values(ext[plane], half)
        write_columns(columns, plane, left, right, slice(None))


def encode_kernel(
    own,
    low,
    high,
    planes,
    corner_low,
    corner_high,
    passed,
    got,
    weight,
    bias,
    down,
    down_bias,
    encoded,
    coarse,
    ext,
    columns_in,
    frame,
    taps,
    packed,
):
    lanes = ext.shape[-1]
    spot = (0, 0)
    fill_frame(ext, own, low, high, planes, corner_low, corner_high, passed, spot, 0, 1, 1)
    fill_columns(
        columns_in, got, frame, planes, corner_low, corner_high, spot, own.shape[1], 1, 1, True
    )
    for plane in range(ext.shape[0]):
        before, after = pair_columns(columns_in, plane, slice(None))
        spread_pairs(taps.at[plane], 0, ext[plane], before, after)
    for tap in range(9):
        spread_weights(packed, tap, 0, [weight[tap, c] for c in range(3)])
    depth, height, columns, _ = encoded.shape
    deep, tall = coarse.shape[:2]
    summed = conv_rows(taps, packed, depth, height)
    fine = leaky_relu(summed + jnp.tile(bias[...], (1, 2))).astype(bf16)
    fine = fine.reshape(deep, 2, tall, 2, columns, lanes)
    encoded[...] = fine.reshape(encoded.shape)
    lifted = None
    for a in range(2):
        for b in range(2):
            part = jnp.dot(
                fine[:, a, :, b].reshape(-1, lanes), down[2 * a + b], preferred_element_type=f32
            )
            lifted = part if lifted is None else lifted + part
    coarse[...] = leaky_relu(lifted + down_bias[...]).astype(bf16).reshape(coarse.shape)


def bottom_kernel(
    sizes,
    coarse,
    encoded,
    low,
    high,
    planes,
    corner_low,
    corner_high,
    passed,
    got,
    weight,
    bias,
    up,
    up_bias,
    raised,
    encoded_ext,
    columns,
    coarse_ext,
    columns_in,
    frame,
    taps,
):
    lanes = coarse_ext.shape[-1]
    spots = layout(sizes)[0]
    at = 0
    for ext, own, spot, (shape, deep, tall) in zip(
        (coarse_ext, encoded_ext), (coarse, encoded), spots, sizes
    ):
        fill_frame(
            ext, own, low, high, planes, corner_low, corner_high, passed, spot, at, deep, tall
        )
        at += shape[0] * tall
    (shape, deep, tall), spot = sizes[0], spots[0]
    fill_columns(
        columns_in, got, frame, planes, corner_low, corner_high, spot, shape[1], deep, tall, False
    )
    for plane in range(coarse_ext.shape[0]):
        before, after = pair_columns(columns_in, plane, slice(None))
        block = coarse_ext[plane]
        wide = block.astype(f32)
        taps[plane, :, :, :lanes] = shifted(wide, before, 1).astype(bf16)
        taps[plane, :, :, lanes : 2 * lanes] = block
        taps[plane, :, :, 2 * lanes :] = shifted(wide, after, -1).astype(bf16)
    deep, _, tall, _, count, _ = raised.shape
    summed = conv_rows(taps, weight, deep, tall)
    bottom = leaky_relu(summed + bias[...]).astype(bf16)
    both = jnp.tile(up_bias[...], (1, 2))
    for a in range(2):
        for b in range(2):
            matrix = jnp.concatenate([up[2 * a + b, 0], up[2 * a + b, 1]], axis=-1)
            lifted = jnp.dot(bottom, matrix, preferred_element_type=f32) + both
            raised[:, a, :, b] = lifted.astype(bf16).reshape(deep, tall, count, lanes)
    blank_plane = jnp.zeros(raised.shape[1:], bf16)
    blank_row = jnp.zeros((deep, 2, 2, count, lanes), bf16)
    first, last = edges("narrow")

    @pl.when(first)
    def _():
        raised[:, :, 0] = blank_row

    @pl.when(last)
    def _():
        raised[:, :, tall - 1] = blank_row

    first, last = edges("wide")

    @pl.when(first)
    def _():
        raised[0] = blank_plane

    @pl.when(last)
    def _():
        raised[deep - 1] = blank_plane

    planes, height = encoded_ext.shape[:2]
    half = lanes // 2
    for plane in range(planes):
        z, a = (plane + 1) // 2, (plane + 1) % 2
        whole = raised[z, a].reshape(2 * tall, count, lanes)[1 : 1 + height]
        low, high = column_values(whole, True)
        write_columns(columns, plane, low, high, slice(0, half))
        low, high = column_values(encoded_ext[plane], True)
        write_columns(columns, plane, low, high, slice(half, lanes))


def decode_kernel(
    raised, encoded_ext, columns_in, weight, bias, decoded, taps, packed, spread
):
    planes, height, columns, lanes = encoded_ext.shape
    half = lanes // 2
    for plane in range(planes):
        low, high = pair_columns(columns_in, plane, slice(0, half))
        spread_pairs(taps.at[plane], 0, raised[plane + 1, 1 : 1 + height], low, high)
        low, high = pair_columns(columns_in, plane, slice(half, lanes))
        spread_pairs(taps.at[plane], 2 * lanes, encoded_ext[plane], low, high)
    for tap in range(9):
        spread_weights(packed, tap, 0, [weight[tap, c, :half] for c in range(3)])
        spread_weights(packed, tap, 2 * lanes, [weight[tap, c, half:] for c in range(3)])
    depth, rows, _, outs = decoded.shape
    summed = conv_rows(taps, packed, depth, rows)
    summed = leaky_relu(summed + jnp.tile(bias[...], (1, 2)))
    for odd in range(2):
        half = summed[:, odd * outs : (odd + 1) * outs].reshape(depth, rows, columns, outs)
        spread[:, :, pl.ds(odd, columns, stride=2), :] = half
    decoded[...] = spread[...].astype(bf16)


def exchange(fields, halos, half):
    sizes = [(field.shape, deep, tall) for field, (deep, tall) in zip(fields, halos)]
    _, planes, corners = layout(sizes)
    cells = fields[0].shape[2:]
    sides = sides_of("narrow")
    swap = [(0, 1), (1, 0)]
    rows = sum(shape[0] * tall for shape, _, tall in sizes)
    edge_rows, handed = call(
        functools.partial(edge_kernel, sizes), [(sides, rows) + cells, (planes,) + cells], (), 8
    )(*fields)
    handed = lax.ppermute(handed, "pair", swap)
    low, high = line_exchange("narrow", edge_rows)
    ring, corner = call(
        functools.partial(plane_kernel, sizes),
        [(2 * planes,) + cells, (sides, 2 * corners) + cells],
        (),
        8,
    )(*fields, handed)
    ring = ring_exchange(ring)
    corner_low, corner_high = corner_exchange(corner)
    received = (low, high, ring, corner_low, corner_high)
    shape, deep, tall = sizes[0]
    framed = (shape[0] + 2 * deep, shape[1] + 2 * tall)
    lanes = cells[1] // 2 if half else cells[1]
    passed, columns = call(
        functools.partial(pass_kernel, sizes, half),
        [(planes + sides * corners,) + cells, framed + (lanes,)],
        [pltpu.VMEM(framed + cells, bf16)],
        8,
    )(fields[0], *received)
    passed = lax.ppermute(passed, "pair", swap)
    columns = lax.ppermute(columns, "pair", swap)
    return sizes, received + (passed, columns)


def body(
    volume, w_encode, b_encode, w_down, b_down, w_bottom, b_bottom, w_up, b_up, w_decode, b_decode
):
    depth, height, width, skip = volume.shape
    deep_width = w_down.shape[4]
    half_depth, half_height, pairs = depth // 2, height // 2, width // 2
    lanes = 2 * skip
    framed = (depth + 2, height + 2)
    coarse_framed = (half_depth + 4, half_height + 4)

    (packed,) = call(
        pack_kernel,
        [(depth, height, pairs, lanes)],
        [pltpu.VMEM((depth, height, width, skip), f32)],
        8,
    )(volume)
    _, received = exchange([packed], [(1, 1)], True)
    encoded, coarse = call(
        encode_kernel,
        [(depth, height, pairs, lanes), (half_depth, half_height, pairs, deep_width)],
        [
            pltpu.VMEM(framed + (pairs, lanes), bf16),
            pltpu.VMEM(framed + (skip,), bf16),
            pltpu.VMEM((1, height + 2, pairs, lanes), bf16),
            pltpu.VMEM(framed + (pairs, 2 * lanes), bf16),
            pltpu.VMEM((9, 2 * lanes, lanes), bf16),
        ],
    )(
        packed,
        *received,
        w_encode.reshape(9, 3, skip, skip),
        b_encode.reshape(1, skip),
        w_down.reshape(4, lanes, deep_width),
        b_down.reshape(1, deep_width),
    )

    sizes, received = exchange([coarse, encoded], [(2, 2), (1, 1)], False)
    raised, encoded_ext, columns = call(
        functools.partial(bottom_kernel, sizes),
        [
            (half_depth + 2, 2, half_height + 2, 2, pairs, lanes),
            framed + (pairs, lanes),
            framed + (lanes,),
        ],
        [
            pltpu.VMEM(coarse_framed + (pairs, deep_width), bf16),
            pltpu.VMEM(coarse_framed + (deep_width,), bf16),
            pltpu.VMEM((2, half_height + 4, pairs, deep_width), bf16),
            pltpu.VMEM(coarse_framed + (pairs, 3 * deep_width), bf16),
        ],
    )(
        coarse,
        encoded,
        *received,
        w_bottom.reshape(9, 3 * deep_width, deep_width),
        b_bottom.reshape(1, deep_width),
        w_up.reshape(4, 2, deep_width, skip),
        b_up.reshape(1, skip),
    )
    columns = lax.ppermute(columns, "pair", [(0, 1), (1, 0)])

    (decoded,) = call(
        decode_kernel,
        [(depth, height, width, skip)],
        [
            pltpu.VMEM(framed + (pairs, 4 * lanes), bf16),
            pltpu.VMEM((9, 4 * lanes, lanes), bf16),
            pltpu.VMEM((depth, height, width, skip), f32),
        ],
    )(
        raised.reshape(depth + 4, height + 4, pairs, lanes),
        encoded_ext,
        columns,
        w_decode.reshape(9, 3, lanes, skip),
        b_decode.reshape(1, skip),
    )
    return decoded


def solution(mesh):
    return jax.shard_map(
        body,
        mesh=mesh,
        in_specs=(
            P(("groups", "wide"), "narrow", "pair", None),
            P(),
            P(),
            P(),
            P(),
            P(),
            P(),
            P(),
            P(),
            P(),
            P(),
        ),
        out_specs=P(("groups", "wide"), "narrow", "pair", None),
        check_vma=False,
    )
```

```python
import functools

import jax
import jax.numpy as jnp
from jax import lax
from jax.experimental import pallas as pl
from jax.experimental.pallas import tpu as pltpu
from jax.sharding import PartitionSpec as P


leak_slope = 0.01
f32 = jnp.float32
bf16 = jnp.bfloat16


def leaky_relu(values):
    return jnp.maximum(values, leak_slope * values)


def sides_of(axis):
    return 1 if lax.axis_size(axis) == 2 else 2


def line_exchange(axis, sent):
    count = lax.axis_size(axis)
    if count == 2:
        got = lax.ppermute(sent[0], axis, [(0, 1), (1, 0)])
        return got, got
    up = [(i, i + 1) for i in range(count - 1)]
    down = [(b, a) for a, b in up]
    return lax.ppermute(sent[1], axis, up), lax.ppermute(sent[0], axis, down)


def snake_pairs(groups, count, step):
    order = [
        group * count + (place if group % 2 == 0 else count - 1 - place)
        for group in range(groups)
        for place in range(count)
    ]
    total = len(order)
    return [(order[i], order[(i + step) % total]) for i in range(total)]


def ring_exchange(sent):
    groups, count = lax.axis_size("groups"), lax.axis_size("wide")
    pairs = [
        (2 * a + core, 2 * b + core)
        for core, step in ((0, 1), (1, -1))
        for a, b in snake_pairs(groups, count, step)
    ]
    return lax.ppermute(sent, ("groups", "wide", "pair"), pairs)


def corner_exchange(sent):
    groups, count, tall = (lax.axis_size(axis) for axis in ("groups", "wide", "narrow"))
    moves = [(0, 1), (1, 0)] if tall == 2 else [(i, i + 1) for i in range(tall - 1)]

    def move(array, rows):
        pairs = [
            ((a * tall + c) * 2 + core, (b * tall + d) * 2 + core)
            for core, step in ((0, 1), (1, -1))
            for a, b in snake_pairs(groups, count, step)
            for c, d in rows
        ]
        return lax.ppermute(array, ("groups", "wide", "narrow", "pair"), pairs)

    if tall == 2:
        got = move(sent[0], moves)
        return got, got
    return move(sent[1], moves), move(sent[0], [(d, c) for c, d in moves])


def call(kernel, outs, scratch=(), megabytes=24):
    return pl.pallas_call(
        kernel,
        out_shape=[jax.ShapeDtypeStruct(shape, bf16) for shape in outs],
        scratch_shapes=list(scratch),
        cost_estimate=pl.CostEstimate(flops=4 * 10**9, transcendentals=0, bytes_accessed=10**6),
        compiler_params=pltpu.CompilerParams(vmem_limit_bytes=megabytes << 20),
    )


def edges(axis):
    place = lax.axis_index(axis)
    return place == 0, place == lax.axis_size(axis) - 1


def sends_high():
    even = lax.axis_index("groups") % 2 == 0
    return (lax.axis_index("pair") == 0) == even


def either(condition, put):
    @pl.when(condition)
    def _():
        put(True)

    @pl.when(jnp.logical_not(condition))
    def _():
        put(False)


def rows_at(ref, at, *lead):
    count = 1
    for size in lead:
        count *= size
    return ref[at : at + count].reshape(lead + tuple(ref.shape[1:]))


def layout(fields):
    planes, corners, spots = 0, 0, []
    for shape, deep, tall in fields:
        spots.append((planes, corners))
        planes += deep * shape[1]
        corners += deep * tall
    return spots, planes, corners


def fill_planes(ext, base, middle, low, high):
    deep, height = middle.shape[:2]
    tall = low.shape[1]
    ext[base : base + deep, :tall] = low
    ext[base : base + deep, tall : tall + height] = middle
    ext[base : base + deep, tall + height :] = high


def fill_block(ext, own, low, high, at, deep, tall):
    depth = own.shape[0]
    fill_planes(
        ext,
        deep,
        own[...],
        rows_at(low, at, depth, tall),
        rows_at(high, at, depth, tall),
    )


def clear_edges(ext, deep, tall):
    first, last = edges("narrow")
    planes, rows = ext.shape[:2]
    blank_rows = jnp.zeros((planes, tall) + ext.shape[2:], bf16)
    blank_planes = jnp.zeros((deep,) + ext.shape[1:], bf16)

    @pl.when(first)
    def _():
        ext[:, :tall] = blank_rows

    @pl.when(last)
    def _():
        ext[:, rows - tall :] = blank_rows

    first, last = edges("wide")

    @pl.when(first)
    def _():
        ext[:deep] = blank_planes

    @pl.when(last)
    def _():
        ext[planes - deep :] = blank_planes


def fill_frame(ext, own, low, high, planes, corner_low, corner_high, passed, spot, at, deep, tall):
    depth, height = own.shape[:2]
    plane_at, corner_at = spot
    count = corner_low.shape[0] // 2
    split = planes.shape[0] // 2
    fill_block(ext, own, low, high, at, deep, tall)
    near = (
        rows_at(planes, plane_at, deep, height),
        rows_at(corner_low, corner_at, deep, tall),
        rows_at(corner_high, corner_at, deep, tall),
    )
    last = passed.shape[0] - count
    far = (
        rows_at(passed, plane_at, deep, height),
        rows_at(passed, split + corner_at, deep, tall),
        rows_at(passed, last + corner_at, deep, tall),
    )

    either(sends_high(), put_sides(ext, depth, deep, near, far))
    clear_edges(ext, deep, tall)


def put_sides(ext, depth, deep, near, far):
    def put(low_is_near):
        fill_planes(ext, 0, *(near if low_is_near else far))
        fill_planes(ext, deep + depth, *(far if low_is_near else near))

    return put


def fill_columns(columns, got, frame, planes, corner_low, corner_high, spot, height, deep, tall, half):
    plane_at, corner_at = spot
    count, corners = planes.shape[0] // 2, corner_low.shape[0] // 2
    columns[...] = got[...]
    fill_planes(
        frame,
        0,
        rows_at(planes, count + plane_at, deep, height),
        rows_at(corner_low, corners + corner_at, deep, tall),
        rows_at(corner_high, corners + corner_at, deep, tall),
    )
    first, last = edges("narrow")
    blank = jnp.zeros((deep, tall) + frame.shape[2:], bf16)

    @pl.when(first)
    def _():
        frame[:, :tall] = blank

    @pl.when(last)
    def _():
        frame[:, tall + height :] = blank

    at_low = lax.axis_index("pair") == 0
    total = columns.shape[0]
    at_edge = edges("wide")

    def put(low_side):
        edge = at_edge[0] if low_side else at_edge[1]
        for layer in range(deep):
            low, high = column_values(frame[layer], half)
            chosen = jnp.where(at_low, low, high)
            chosen = jnp.where(edge, jnp.zeros_like(chosen), chosen)
            columns[layer if low_side else total - deep + layer] = chosen

    either(sends_high(), put)


def write_columns(columns, plane, low, high, lanes):
    at_low = lax.axis_index("pair") == 0
    columns[plane, :, lanes] = jnp.where(at_low, high, low)


def column_values(block, half):
    lanes = block.shape[-1]
    wide = block.astype(f32)
    if half:
        return wide[:, 0, : lanes // 2].astype(bf16), wide[:, -1, lanes // 2 :].astype(bf16)
    return wide[:, 0, :].astype(bf16), wide[:, -1, :].astype(bf16)


def shifted(values, column, step):
    columns = values.shape[1]
    spot = lax.broadcasted_iota(jnp.int32, values.shape, 1)
    if step > 0:
        return jnp.where(spot == 0, column[:, None, :], pltpu.roll(values, 1, 1))
    return jnp.where(
        spot == columns - 1, column[:, None, :], pltpu.roll(values, columns - 1, 1)
    )


def pair_columns(got, plane, lanes):
    first, last = edges("pair")
    column = got[plane, :, lanes].astype(f32)
    blank = jnp.zeros_like(column)
    return jnp.where(first, blank, column), jnp.where(last, blank, column)


def spread_pairs(taps, base, block, low, high):
    lanes = block.shape[-1] // 2
    wide = block.astype(f32)
    taps[:, :, base : base + lanes] = shifted(wide[:, :, lanes:], low, 1).astype(bf16)
    taps[:, :, base + lanes : base + 3 * lanes] = block
    taps[:, :, base + 3 * lanes : base + 4 * lanes] = shifted(
        wide[:, :, :lanes], high, -1
    ).astype(bf16)


def spread_weights(packed, tap, base, taken):
    rows, outs = taken[0].shape
    blank = jnp.zeros((rows, outs), bf16)
    for cell in range(4):
        at = base + cell * rows
        packed[tap, at : at + rows, :outs] = taken[cell] if cell < 3 else blank
        packed[tap, at : at + rows, outs:] = taken[cell - 1] if cell > 0 else blank


def conv_rows(taps, packed, depth, height):
    lanes = taps.shape[-1]
    summed = None
    for a in range(3):
        for b in range(3):
            rows = taps[a : a + depth, b : b + height].reshape(-1, lanes)
            part = jnp.dot(rows, packed[3 * a + b], preferred_element_type=f32)
            summed = part if summed is None else summed + part
    return summed


def choose_side(axis, sent, put):
    if sent.shape[0] == 1:
        at_low = lax.axis_index(axis) == 0

        @pl.when(at_low)
        def _():
            put(0, True)

        @pl.when(jnp.logical_not(at_low))
        def _():
            put(0, False)

    else:
        put(0, False)
        put(1, True)


def pack_pairs(out, cells, spread):
    pairs, lanes = out.shape[1], cells.shape[-1]
    spread[...] = cells.astype(f32)
    for odd in range(2):
        half = spread[:, pl.ds(odd, pairs, stride=2), :]
        out[:, :, odd * lanes : (odd + 1) * lanes] = half.astype(bf16)


def pack_kernel(volume, packed, spread):
    for plane in range(volume.shape[0]):
        pack_pairs(packed.at[plane], volume[plane], spread.at[plane])


def edge_kernel(sizes, *refs):
    fields, (edge_rows, handed) = refs[: len(sizes)], refs[len(sizes) :]

    def put_rows(slot, high):
        at = 0
        for field, (_, _, tall) in zip(fields, sizes):
            depth, height = field.shape[:2]
            first = height - tall if high else 0
            rows = field[:, first : first + tall]
            edge_rows[slot, at : at + depth * tall] = rows.reshape((depth * tall,) + rows.shape[2:])
            at += depth * tall

    choose_side("narrow", edge_rows, put_rows)
    either(sends_high(), lambda high: put_boundary(handed, fields, sizes, not high))


def put_boundary(out, fields, sizes, high):
    at = 0
    for field, (_, deep, _) in zip(fields, sizes):
        depth, height = field.shape[:2]
        planes = field[depth - deep :] if high else field[:deep]
        out[at : at + deep * height] = planes.reshape((deep * height,) + planes.shape[2:])
        at += deep * height


def plane_kernel(sizes, *refs):
    fields, (handed, planes, corners) = refs[: len(sizes)], refs[len(sizes) :]
    spots, count, few = layout(sizes)
    planes[count:] = handed[...]
    either(sends_high(), lambda high: put_boundary(planes, fields, sizes, high))

    def put(slot, high):
        for (shape, deep, tall), (plane_at, corner_at) in zip(sizes, spots):
            height = shape[1]
            first = height - tall if high else 0
            for part in range(2):
                for layer in range(deep):
                    source = part * count + plane_at + layer * height + first
                    target = part * few + corner_at + layer * tall
                    corners[slot, target : target + tall] = planes[source : source + tall]

    choose_side("narrow", corners, put)


def pass_kernel(sizes, half, *refs):
    own, low, high, planes, corner_low, corner_high, passed, columns, ext = refs
    (shape, deep, tall), (_, count, few) = sizes[0], layout(sizes)
    depth, height = shape[:2]
    passed[:count] = planes[count:]
    passed[count : count + few] = corner_low[few:]
    passed[passed.shape[0] - few :] = corner_high[few:]
    fill_block(ext, own, low, high, 0, deep, tall)
    near = (
        rows_at(planes, 0, deep, height),
        rows_at(corner_low, 0, deep, tall),
        rows_at(corner_high, 0, deep, tall),
    )
    blank = tuple(jnp.zeros_like(part) for part in near)
    either(sends_high(), put_sides(ext, depth, deep, near, blank))
    clear_edges(ext, deep, tall)
    for plane in range(ext.shape[0]):
        left, right = column_values(ext[plane], half)
        write_columns(columns, plane, left, right, slice(None))


def weight_kernel(weight, packed):
    outs = weight.shape[-1]
    for tap in range(9):
        for block in range(weight.shape[2] // outs):
            rows = slice(block * outs, (block + 1) * outs)
            spread_weights(packed, tap, 4 * outs * block, [weight[tap, c, rows] for c in range(3)])


def encode_kernel(
    own,
    low,
    high,
    planes,
    corner_low,
    corner_high,
    passed,
    got,
    packed,
    bias,
    down,
    down_bias,
    encoded,
    coarse,
    ext,
    columns_in,
    frame,
    taps,
):
    lanes = ext.shape[-1]
    spot = (0, 0)
    fill_frame(ext, own, low, high, planes, corner_low, corner_high, passed, spot, 0, 1, 1)
    fill_columns(
        columns_in, got, frame, planes, corner_low, corner_high, spot, own.shape[1], 1, 1, True
    )
    for plane in range(ext.shape[0]):
        before, after = pair_columns(columns_in, plane, slice(None))
        spread_pairs(taps.at[plane], 0, ext[plane], before, after)
    depth, height, columns, _ = encoded.shape
    deep, tall = coarse.shape[:2]
    summed = conv_rows(taps, packed, depth, height)
    fine = leaky_relu(summed + jnp.tile(bias[...], (1, 2))).astype(bf16)
    fine = fine.reshape(deep, 2, tall, 2, columns, lanes)
    encoded[...] = fine.reshape(encoded.shape)
    lifted = None
    for a in range(2):
        for b in range(2):
            part = jnp.dot(
                fine[:, a, :, b].reshape(-1, lanes), down[2 * a + b], preferred_element_type=f32
            )
            lifted = part if lifted is None else lifted + part
    coarse[...] = leaky_relu(lifted + down_bias[...]).astype(bf16).reshape(coarse.shape)


def bottom_kernel(
    sizes,
    coarse,
    encoded,
    low,
    high,
    planes,
    corner_low,
    corner_high,
    passed,
    got,
    weight,
    bias,
    up,
    up_bias,
    raised,
    encoded_ext,
    columns,
    coarse_ext,
    columns_in,
    frame,
    taps,
):
    lanes = coarse_ext.shape[-1]
    spots = layout(sizes)[0]
    at = 0
    for ext, own, spot, (shape, deep, tall) in zip(
        (coarse_ext, encoded_ext), (coarse, encoded), spots, sizes
    ):
        fill_frame(
            ext, own, low, high, planes, corner_low, corner_high, passed, spot, at, deep, tall
        )
        at += shape[0] * tall
    (shape, deep, tall), spot = sizes[0], spots[0]
    fill_columns(
        columns_in, got, frame, planes, corner_low, corner_high, spot, shape[1], deep, tall, False
    )
    for plane in range(coarse_ext.shape[0]):
        before, after = pair_columns(columns_in, plane, slice(None))
        block = coarse_ext[plane]
        wide = block.astype(f32)
        taps[plane, :, :, :lanes] = shifted(wide, before, 1).astype(bf16)
        taps[plane, :, :, lanes : 2 * lanes] = block
        taps[plane, :, :, 2 * lanes :] = shifted(wide, after, -1).astype(bf16)
    deep, _, tall, _, count, _ = raised.shape
    summed = conv_rows(taps, weight, deep, tall)
    bottom = leaky_relu(summed + bias[...]).astype(bf16)
    both = jnp.tile(up_bias[...], (1, 2))
    for a in range(2):
        for b in range(2):
            matrix = jnp.concatenate([up[2 * a + b, 0], up[2 * a + b, 1]], axis=-1)
            lifted = jnp.dot(bottom, matrix, preferred_element_type=f32) + both
            raised[:, a, :, b] = lifted.astype(bf16).reshape(deep, tall, count, lanes)
    blank_plane = jnp.zeros(raised.shape[1:], bf16)
    blank_row = jnp.zeros((deep, 2, 2, count, lanes), bf16)
    first, last = edges("narrow")

    @pl.when(first)
    def _():
        raised[:, :, 0] = blank_row

    @pl.when(last)
    def _():
        raised[:, :, tall - 1] = blank_row

    first, last = edges("wide")

    @pl.when(first)
    def _():
        raised[0] = blank_plane

    @pl.when(last)
    def _():
        raised[deep - 1] = blank_plane

    planes, height = encoded_ext.shape[:2]
    half = lanes // 2
    for plane in range(planes):
        z, a = (plane + 1) // 2, (plane + 1) % 2
        whole = raised[z, a].reshape(2 * tall, count, lanes)[1 : 1 + height]
        low, high = column_values(whole, True)
        write_columns(columns, plane, low, high, slice(0, half))
        low, high = column_values(encoded_ext[plane], True)
        write_columns(columns, plane, low, high, slice(half, lanes))


def decode_kernel(
    raised, encoded_ext, columns_in, packed, bias, decoded, taps, spread
):
    planes, height, columns, lanes = encoded_ext.shape
    half = lanes // 2
    for plane in range(planes):
        low, high = pair_columns(columns_in, plane, slice(0, half))
        spread_pairs(taps.at[plane], 0, raised[plane + 1, 1 : 1 + height], low, high)
        low, high = pair_columns(columns_in, plane, slice(half, lanes))
        spread_pairs(taps.at[plane], 2 * lanes, encoded_ext[plane], low, high)
    depth, rows, _, outs = decoded.shape
    summed = conv_rows(taps, packed, depth, rows)
    summed = leaky_relu(summed + jnp.tile(bias[...], (1, 2)))
    for odd in range(2):
        half = summed[:, odd * outs : (odd + 1) * outs].reshape(depth, rows, columns, outs)
        spread[:, :, pl.ds(odd, columns, stride=2), :] = half
    decoded[...] = spread[...].astype(bf16)


def exchange(fields, halos, half, weight):
    sizes = [(field.shape, deep, tall) for field, (deep, tall) in zip(fields, halos)]
    _, planes, corners = layout(sizes)
    cells = fields[0].shape[2:]
    sides = sides_of("narrow")
    swap = [(0, 1), (1, 0)]
    rows = sum(shape[0] * tall for shape, _, tall in sizes)
    edge_rows, handed = call(
        functools.partial(edge_kernel, sizes), [(sides, rows) + cells, (planes,) + cells], (), 8
    )(*fields)
    handed = lax.ppermute(handed, "pair", swap)
    low, high = line_exchange("narrow", edge_rows)
    ring, corner = call(
        functools.partial(plane_kernel, sizes),
        [(2 * planes,) + cells, (sides, 2 * corners) + cells],
        (),
        8,
    )(*fields, handed)
    ring = ring_exchange(ring)
    corner_low, corner_high = corner_exchange(corner)
    outs = weight.shape[-1]
    (weights,) = call(weight_kernel, [(9, 4 * weight.shape[2], 2 * outs)], (), 8)(weight)
    received = (low, high, ring, corner_low, corner_high)
    shape, deep, tall = sizes[0]
    framed = (shape[0] + 2 * deep, shape[1] + 2 * tall)
    lanes = cells[1] // 2 if half else cells[1]
    passed, columns = call(
        functools.partial(pass_kernel, sizes, half),
        [(planes + sides * corners,) + cells, framed + (lanes,)],
        [pltpu.VMEM(framed + cells, bf16)],
        8,
    )(fields[0], *received)
    passed = lax.ppermute(passed, "pair", swap)
    columns = lax.ppermute(columns, "pair", swap)
    return sizes, weights, received + (passed, columns)


def body(
    volume, w_encode, b_encode, w_down, b_down, w_bottom, b_bottom, w_up, b_up, w_decode, b_decode
):
    depth, height, width, skip = volume.shape
    deep_width = w_down.shape[4]
    half_depth, half_height, pairs = depth // 2, height // 2, width // 2
    lanes = 2 * skip
    framed = (depth + 2, height + 2)
    coarse_framed = (half_depth + 4, half_height + 4)

    (packed,) = call(
        pack_kernel,
        [(depth, height, pairs, lanes)],
        [pltpu.VMEM((depth, height, width, skip), f32)],
        8,
    )(volume)
    _, encode_weights, received = exchange(
        [packed], [(1, 1)], True, w_encode.reshape(9, 3, skip, skip)
    )
    encoded, coarse = call(
        encode_kernel,
        [(depth, height, pairs, lanes), (half_depth, half_height, pairs, deep_width)],
        [
            pltpu.VMEM(framed + (pairs, lanes), bf16),
            pltpu.VMEM(framed + (skip,), bf16),
            pltpu.VMEM((1, height + 2, pairs, lanes), bf16),
            pltpu.VMEM(framed + (pairs, 2 * lanes), bf16),
        ],
    )(
        packed,
        *received,
        encode_weights,
        b_encode.reshape(1, skip),
        w_down.reshape(4, lanes, deep_width),
        b_down.reshape(1, deep_width),
    )

    sizes, decode_weights, received = exchange(
        [coarse, encoded], [(2, 2), (1, 1)], False, w_decode.reshape(9, 3, lanes, skip)
    )
    raised, encoded_ext, columns = call(
        functools.partial(bottom_kernel, sizes),
        [
            (half_depth + 2, 2, half_height + 2, 2, pairs, lanes),
            framed + (pairs, lanes),
            framed + (lanes,),
        ],
        [
            pltpu.VMEM(coarse_framed + (pairs, deep_width), bf16),
            pltpu.VMEM(coarse_framed + (deep_width,), bf16),
            pltpu.VMEM((2, half_height + 4, pairs, deep_width), bf16),
            pltpu.VMEM(coarse_framed + (pairs, 3 * deep_width), bf16),
        ],
    )(
        coarse,
        encoded,
        *received,
        w_bottom.reshape(9, 3 * deep_width, deep_width),
        b_bottom.reshape(1, deep_width),
        w_up.reshape(4, 2, deep_width, skip),
        b_up.reshape(1, skip),
    )
    columns = lax.ppermute(columns, "pair", [(0, 1), (1, 0)])

    (decoded,) = call(
        decode_kernel,
        [(depth, height, width, skip)],
        [
            pltpu.VMEM(framed + (pairs, 4 * lanes), bf16),
            pltpu.VMEM((depth, height, width, skip), f32),
        ],
    )(
        raised.reshape(depth + 4, height + 4, pairs, lanes),
        encoded_ext,
        columns,
        decode_weights,
        b_decode.reshape(1, skip),
    )
    return decoded


def solution(mesh):
    return jax.shard_map(
        body,
        mesh=mesh,
        in_specs=(
            P(("groups", "wide"), "narrow", "pair", None),
            P(),
            P(),
            P(),
            P(),
            P(),
            P(),
            P(),
            P(),
            P(),
            P(),
        ),
        out_specs=P(("groups", "wide"), "narrow", "pair", None),
        check_vma=False,
    )
```

```python
import functools

import jax
import jax.numpy as jnp
from jax import lax
from jax.experimental import pallas as pl
from jax.experimental.pallas import tpu as pltpu
from jax.sharding import PartitionSpec as P


leak_slope = 0.01
f32 = jnp.float32
bf16 = jnp.bfloat16


def leaky_relu(values):
    return jnp.maximum(values, leak_slope * values)


def sides_of(axis):
    return 1 if lax.axis_size(axis) == 2 else 2


def line_exchange(axis, sent):
    count = lax.axis_size(axis)
    if count == 2:
        got = lax.ppermute(sent[0], axis, [(0, 1), (1, 0)])
        return got, got
    up = [(i, i + 1) for i in range(count - 1)]
    down = [(b, a) for a, b in up]
    return lax.ppermute(sent[1], axis, up), lax.ppermute(sent[0], axis, down)


def snake_pairs(groups, count, step):
    order = [
        group * count + (place if group % 2 == 0 else count - 1 - place)
        for group in range(groups)
        for place in range(count)
    ]
    total = len(order)
    return [(order[i], order[(i + step) % total]) for i in range(total)]


def ring_exchange(sent):
    groups, count = lax.axis_size("groups"), lax.axis_size("wide")
    pairs = [
        (2 * a + core, 2 * b + core)
        for core, step in ((0, 1), (1, -1))
        for a, b in snake_pairs(groups, count, step)
    ]
    return lax.ppermute(sent, ("groups", "wide", "pair"), pairs)


def corner_exchange(sent):
    groups, count, tall = (lax.axis_size(axis) for axis in ("groups", "wide", "narrow"))
    moves = [(0, 1), (1, 0)] if tall == 2 else [(i, i + 1) for i in range(tall - 1)]

    def move(array, rows):
        pairs = [
            ((a * tall + c) * 2 + core, (b * tall + d) * 2 + core)
            for core, step in ((0, 1), (1, -1))
            for a, b in snake_pairs(groups, count, step)
            for c, d in rows
        ]
        return lax.ppermute(array, ("groups", "wide", "narrow", "pair"), pairs)

    if tall == 2:
        got = move(sent[0], moves)
        return got, got
    return move(sent[1], moves), move(sent[0], [(d, c) for c, d in moves])


def call(kernel, outs, scratch=(), megabytes=24, dtype=bf16):
    return pl.pallas_call(
        kernel,
        out_shape=[jax.ShapeDtypeStruct(shape, dtype) for shape in outs],
        scratch_shapes=list(scratch),
        cost_estimate=pl.CostEstimate(flops=4 * 10**9, transcendentals=0, bytes_accessed=10**6),
        compiler_params=pltpu.CompilerParams(vmem_limit_bytes=megabytes << 20),
    )


def edges(axis):
    place = lax.axis_index(axis)
    return place == 0, place == lax.axis_size(axis) - 1


def sends_high():
    even = lax.axis_index("groups") % 2 == 0
    return (lax.axis_index("pair") == 0) == even


def either(condition, put):
    @pl.when(condition)
    def _():
        put(True)

    @pl.when(jnp.logical_not(condition))
    def _():
        put(False)


def rows_at(ref, at, *lead):
    count = 1
    for size in lead:
        count *= size
    return ref[at : at + count].reshape(lead + tuple(ref.shape[1:]))


def layout(fields):
    planes, corners, spots = 0, 0, []
    for shape, deep, tall in fields:
        spots.append((planes, corners))
        planes += deep * shape[1]
        corners += deep * tall
    return spots, planes, corners


def fill_planes(ext, base, middle, low, high):
    deep, height = middle.shape[:2]
    tall = low.shape[1]
    ext[base : base + deep, :tall] = low
    ext[base : base + deep, tall : tall + height] = middle
    ext[base : base + deep, tall + height :] = high


def fill_block(ext, own, low, high, at, deep, tall):
    depth = own.shape[0]
    fill_planes(
        ext,
        deep,
        own[...],
        rows_at(low, at, depth, tall),
        rows_at(high, at, depth, tall),
    )


def clear_edges(ext, deep, tall):
    first, last = edges("narrow")
    planes, rows = ext.shape[:2]
    blank_rows = jnp.zeros((planes, tall) + ext.shape[2:], bf16)
    blank_planes = jnp.zeros((deep,) + ext.shape[1:], bf16)

    @pl.when(first)
    def _():
        ext[:, :tall] = blank_rows

    @pl.when(last)
    def _():
        ext[:, rows - tall :] = blank_rows

    first, last = edges("wide")

    @pl.when(first)
    def _():
        ext[:deep] = blank_planes

    @pl.when(last)
    def _():
        ext[planes - deep :] = blank_planes


def fill_frame(ext, own, low, high, planes, corner_low, corner_high, passed, spot, at, deep, tall):
    depth, height = own.shape[:2]
    plane_at, corner_at = spot
    count = corner_low.shape[0] // 2
    split = planes.shape[0] // 2
    fill_block(ext, own, low, high, at, deep, tall)
    near = (
        rows_at(planes, plane_at, deep, height),
        rows_at(corner_low, corner_at, deep, tall),
        rows_at(corner_high, corner_at, deep, tall),
    )
    last = split + (sides_of("narrow") - 1) * count
    far = (
        rows_at(passed, plane_at, deep, height),
        rows_at(passed, split + corner_at, deep, tall),
        rows_at(passed, last + corner_at, deep, tall),
    )

    either(sends_high(), put_sides(ext, depth, deep, near, far))
    clear_edges(ext, deep, tall)


def put_sides(ext, depth, deep, near, far):
    def put(low_is_near):
        fill_planes(ext, 0, *(near if low_is_near else far))
        fill_planes(ext, deep + depth, *(far if low_is_near else near))

    return put


def fill_columns(columns, passed, frame, planes, corner_low, corner_high, spot, height, deep, tall, half):
    plane_at, corner_at = spot
    count, corners = planes.shape[0] // 2, corner_low.shape[0] // 2
    total, rows, lanes = columns.shape
    start = passed.shape[0] - total
    for plane in range(total):
        columns[plane] = passed[start + plane, :rows, :lanes]
    fill_planes(
        frame,
        0,
        rows_at(planes, count + plane_at, deep, height),
        rows_at(corner_low, corners + corner_at, deep, tall),
        rows_at(corner_high, corners + corner_at, deep, tall),
    )
    first, last = edges("narrow")
    blank = jnp.zeros((deep, tall) + frame.shape[2:], bf16)

    @pl.when(first)
    def _():
        frame[:, :tall] = blank

    @pl.when(last)
    def _():
        frame[:, tall + height :] = blank

    at_low = lax.axis_index("pair") == 0
    at_edge = edges("wide")

    def put(low_side):
        edge = at_edge[0] if low_side else at_edge[1]
        for layer in range(deep):
            low, high = column_values(frame[layer], half)
            chosen = jnp.where(at_low, low, high)
            chosen = jnp.where(edge, jnp.zeros_like(chosen), chosen)
            columns[layer if low_side else total - deep + layer] = chosen

    either(sends_high(), put)


def inner_column(block, half):
    low, high = column_values(block, half)
    return jnp.where(lax.axis_index("pair") == 0, high, low)


def column_values(block, half):
    lanes = block.shape[-1]
    wide = block.astype(f32)
    if half:
        return wide[:, 0, : lanes // 2].astype(bf16), wide[:, -1, lanes // 2 :].astype(bf16)
    return wide[:, 0, :].astype(bf16), wide[:, -1, :].astype(bf16)


def shifted(values, column, step):
    columns = values.shape[1]
    spot = lax.broadcasted_iota(jnp.int32, values.shape, 1)
    if step > 0:
        return jnp.where(spot == 0, column[:, None, :], pltpu.roll(values, 1, 1))
    return jnp.where(
        spot == columns - 1, column[:, None, :], pltpu.roll(values, columns - 1, 1)
    )


def pair_columns(got, plane, lanes):
    first, last = edges("pair")
    column = got[plane, :, lanes].astype(f32)
    blank = jnp.zeros_like(column)
    return jnp.where(first, blank, column), jnp.where(last, blank, column)


def spread_pairs(taps, base, block, low, high):
    lanes = block.shape[-1] // 2
    wide = block.astype(f32)
    taps[:, :, base : base + lanes] = shifted(wide[:, :, lanes:], low, 1).astype(bf16)
    taps[:, :, base + lanes : base + 3 * lanes] = block
    taps[:, :, base + 3 * lanes : base + 4 * lanes] = shifted(
        wide[:, :, :lanes], high, -1
    ).astype(bf16)


def spread_weights(packed, tap, base, taken):
    rows, outs = taken[0].shape
    blank = jnp.zeros((rows, outs), bf16)
    for cell in range(4):
        at = base + cell * rows
        packed[tap, at : at + rows, :outs] = taken[cell] if cell < 3 else blank
        packed[tap, at : at + rows, outs:] = taken[cell - 1] if cell > 0 else blank


def conv_sum(taps, packed, base, select):
    lanes = taps.shape[-1]
    summed = None
    for a in range(3):
        for b in range(3):
            rows = [taps[part].reshape(-1, lanes) for part in select(a, b)]
            rows = rows[0] if len(rows) == 1 else jnp.concatenate(rows, axis=0)
            part = jnp.dot(
                rows, packed[3 * a + b, base : base + lanes], preferred_element_type=f32
            )
            summed = part if summed is None else summed + part
    return summed


def conv_rows(taps, packed, depth, height, base=0):
    return conv_sum(
        taps, packed, base, lambda a, b: [(slice(a, a + depth), slice(b, b + height))]
    )


def conv_border(taps, packed, depth, height, base=0):
    def select(a, b):
        planes = slice(a + 1, a + depth - 1)
        rows = slice(b, b + height)
        return [(a, rows), (a + depth - 1, rows), (planes, b), (planes, b + height - 1)]

    summed = conv_sum(taps, packed, base, select)
    columns, lanes = taps.shape[2], summed.shape[-1]
    inner = slice(1, depth - 1)
    at = 0
    pieces = []
    for where, count in (
        ((0,), height),
        ((depth - 1,), height),
        ((inner, 0), depth - 2),
        ((inner, height - 1), depth - 2),
    ):
        block = summed[at : at + count * columns].reshape(count, columns, lanes)
        pieces.append((where, block))
        at += count * columns
    return pieces


def inner_kernel(base, final, field, handed, packed, bias, out, taps):
    depth, height, _, lanes = field.shape
    start = handed.shape[0] - depth
    columns_in = handed.at[start:, :height, : lanes // 2]
    for plane in range(depth):
        before, after = pair_columns(columns_in, plane, slice(None))
        spread_pairs(taps.at[plane], 0, field[plane], before, after)
    summed = conv_rows(taps, packed, depth - 2, height - 2, base)
    if final:
        summed = leaky_relu(summed + jnp.tile(bias[...], (1, 2))).astype(bf16)
    out[...] = summed.reshape(out.shape)


def choose_side(axis, sent, put):
    if sent.shape[0] == 1:
        at_low = lax.axis_index(axis) == 0

        @pl.when(at_low)
        def _():
            put(0, True)

        @pl.when(jnp.logical_not(at_low))
        def _():
            put(0, False)

    else:
        put(0, False)
        put(1, True)


def pack_pairs(out, cells, spread):
    pairs, lanes = out.shape[1], cells.shape[-1]
    spread[...] = cells.astype(f32)
    for odd in range(2):
        half = spread[:, pl.ds(odd, pairs, stride=2), :]
        out[:, :, odd * lanes : (odd + 1) * lanes] = half.astype(bf16)


def pack_kernel(volume, packed, spread):
    for plane in range(volume.shape[0]):
        pack_pairs(packed.at[plane], volume[plane], spread.at[plane])


def put_column(ref, at, column):
    ref[at] = jnp.zeros(ref.shape[1:], bf16)
    ref[at, : column.shape[0], : column.shape[1]] = column


def edge_kernel(sizes, *refs):
    fields, (edge_rows, handed) = refs[: len(sizes)], refs[len(sizes) :]

    def put_rows(slot, high):
        at = 0
        for field, (_, _, tall) in zip(fields, sizes):
            depth, height = field.shape[:2]
            first = height - tall if high else 0
            rows = field[:, first : first + tall]
            edge_rows[slot, at : at + depth * tall] = rows.reshape((depth * tall,) + rows.shape[2:])
            at += depth * tall

    choose_side("narrow", edge_rows, put_rows)
    either(sends_high(), lambda high: put_boundary(handed, fields, sizes, not high))
    field, start = fields[-1], layout(sizes)[1]
    for plane in range(field.shape[0]):
        put_column(handed, start + plane, inner_column(field[plane], True))


def put_boundary(out, fields, sizes, high):
    at = 0
    for field, (_, deep, _) in zip(fields, sizes):
        depth, height = field.shape[:2]
        planes = field[depth - deep :] if high else field[:deep]
        out[at : at + deep * height] = planes.reshape((deep * height,) + planes.shape[2:])
        at += deep * height


def plane_kernel(sizes, *refs):
    fields, (handed, planes, corners) = refs[: len(sizes)], refs[len(sizes) :]
    spots, count, few = layout(sizes)
    planes[count:] = handed[:count]
    either(sends_high(), lambda high: put_boundary(planes, fields, sizes, high))

    def put(slot, high):
        for (shape, deep, tall), (plane_at, corner_at) in zip(sizes, spots):
            height = shape[1]
            first = height - tall if high else 0
            for part in range(2):
                for layer in range(deep):
                    source = part * count + plane_at + layer * height + first
                    target = part * few + corner_at + layer * tall
                    corners[slot, target : target + tall] = planes[source : source + tall]

    choose_side("narrow", corners, put)


def pass_kernel(sizes, half, *refs):
    own, low, high, planes, corner_low, corner_high, passed, ext = refs
    (shape, deep, tall), (_, count, few) = sizes[0], layout(sizes)
    depth, height = shape[:2]
    passed[:count] = planes[count:]
    passed[count : count + few] = corner_low[few:]
    start = passed.shape[0] - ext.shape[0]
    passed[start - few : start] = corner_high[few:]
    fill_block(ext, own, low, high, 0, deep, tall)
    near = (
        rows_at(planes, 0, deep, height),
        rows_at(corner_low, 0, deep, tall),
        rows_at(corner_high, 0, deep, tall),
    )
    blank = tuple(jnp.zeros_like(part) for part in near)
    either(sends_high(), put_sides(ext, depth, deep, near, blank))
    clear_edges(ext, deep, tall)
    for plane in range(ext.shape[0]):
        put_column(passed, start + plane, inner_column(ext[plane], half))


def weight_kernel(weight, packed):
    outs = weight.shape[-1]
    for tap in range(9):
        for block in range(weight.shape[2] // outs):
            rows = slice(block * outs, (block + 1) * outs)
            spread_weights(packed, tap, 4 * outs * block, [weight[tap, c, rows] for c in range(3)])


def encode_kernel(
    own,
    low,
    high,
    planes,
    corner_low,
    corner_high,
    passed,
    packed,
    inner,
    bias,
    down,
    down_bias,
    encoded,
    coarse,
    ext,
    columns_in,
    frame,
    taps,
):
    lanes = ext.shape[-1]
    spot = (0, 0)
    fill_frame(ext, own, low, high, planes, corner_low, corner_high, passed, spot, 0, 1, 1)
    fill_columns(
        columns_in, passed, frame, planes, corner_low, corner_high, spot, own.shape[1], 1, 1, True
    )
    for plane in range(ext.shape[0]):
        before, after = pair_columns(columns_in, plane, slice(None))
        spread_pairs(taps.at[plane], 0, ext[plane], before, after)
    depth, height, columns, _ = encoded.shape
    deep, tall = coarse.shape[:2]
    both = jnp.tile(bias[...], (1, 2))
    encoded[1 : depth - 1, 1 : height - 1] = inner[...]
    for where, block in conv_border(taps, packed, depth, height):
        encoded[where] = leaky_relu(block + both).astype(bf16)
    fine = encoded[...].reshape(deep, 2, tall, 2, columns, lanes)
    lifted = None
    for a in range(2):
        for b in range(2):
            part = jnp.dot(
                fine[:, a, :, b].reshape(-1, lanes), down[2 * a + b], preferred_element_type=f32
            )
            lifted = part if lifted is None else lifted + part
    coarse[...] = leaky_relu(lifted + down_bias[...]).astype(bf16).reshape(coarse.shape)


def bottom_kernel(
    sizes,
    coarse,
    encoded,
    low,
    high,
    planes,
    corner_low,
    corner_high,
    passed,
    weight,
    bias,
    up,
    up_bias,
    raised,
    encoded_ext,
    columns,
    coarse_ext,
    columns_in,
    frame,
    taps,
):
    lanes = coarse_ext.shape[-1]
    spots = layout(sizes)[0]
    at = 0
    for ext, own, spot, (shape, deep, tall) in zip(
        (coarse_ext, encoded_ext), (coarse, encoded), spots, sizes
    ):
        fill_frame(
            ext, own, low, high, planes, corner_low, corner_high, passed, spot, at, deep, tall
        )
        at += shape[0] * tall
    (shape, deep, tall), spot = sizes[0], spots[0]
    fill_columns(
        columns_in, passed, frame, planes, corner_low, corner_high, spot, shape[1], deep, tall, False
    )
    for plane in range(coarse_ext.shape[0]):
        before, after = pair_columns(columns_in, plane, slice(None))
        block = coarse_ext[plane]
        wide = block.astype(f32)
        taps[plane, :, :, :lanes] = shifted(wide, before, 1).astype(bf16)
        taps[plane, :, :, lanes : 2 * lanes] = block
        taps[plane, :, :, 2 * lanes :] = shifted(wide, after, -1).astype(bf16)
    deep, _, tall, _, count, _ = raised.shape
    summed = conv_rows(taps, weight, deep, tall)
    bottom = leaky_relu(summed + bias[...]).astype(bf16)
    both = jnp.tile(up_bias[...], (1, 2))
    for a in range(2):
        for b in range(2):
            matrix = jnp.concatenate([up[2 * a + b, 0], up[2 * a + b, 1]], axis=-1)
            lifted = jnp.dot(bottom, matrix, preferred_element_type=f32) + both
            raised[:, a, :, b] = lifted.astype(bf16).reshape(deep, tall, count, lanes)
    blank_plane = jnp.zeros(raised.shape[1:], bf16)
    blank_row = jnp.zeros((deep, 2, 2, count, lanes), bf16)
    first, last = edges("narrow")

    @pl.when(first)
    def _():
        raised[:, :, 0] = blank_row

    @pl.when(last)
    def _():
        raised[:, :, tall - 1] = blank_row

    first, last = edges("wide")

    @pl.when(first)
    def _():
        raised[0] = blank_plane

    @pl.when(last)
    def _():
        raised[deep - 1] = blank_plane

    planes, height = encoded_ext.shape[:2]
    half = lanes // 2
    for plane in range(planes):
        z, a = (plane + 1) // 2, (plane + 1) % 2
        whole = raised[z, a].reshape(2 * tall, count, lanes)[1 : 1 + height]
        columns[plane, :, :half] = inner_column(whole, True)
        columns[plane, :, half:] = inner_column(encoded_ext[plane], True)


def decode_kernel(
    raised,
    encoded_ext,
    columns_in,
    packed,
    inner,
    bias,
    decoded,
    raised_taps,
    encoded_taps,
    sums,
    spread,
):
    planes, height, columns, lanes = encoded_ext.shape
    half = lanes // 2
    for plane in range(planes):
        low, high = pair_columns(columns_in, plane, slice(0, half))
        spread_pairs(raised_taps.at[plane], 0, raised[plane + 1, 1 : 1 + height], low, high)
        low, high = pair_columns(columns_in, plane, slice(half, lanes))
        spread_pairs(encoded_taps.at[plane], 0, encoded_ext[plane], low, high)
    depth, rows, _, outs = decoded.shape
    sums[...] = conv_rows(raised_taps, packed, depth, rows).reshape(sums.shape)
    sums[1 : depth - 1, 1 : rows - 1] += inner[...]
    for where, block in conv_border(encoded_taps, packed, depth, rows, 2 * lanes):
        sums[where] += block
    summed = leaky_relu(sums[...] + jnp.tile(bias[...], (1, 2)))
    for odd in range(2):
        half = summed[:, :, :, odd * outs : (odd + 1) * outs]
        spread[:, :, pl.ds(odd, columns, stride=2), :] = half
    decoded[...] = spread[...].astype(bf16)


def exchange(fields, halos, half, weight, bias):
    sizes = [(field.shape, deep, tall) for field, (deep, tall) in zip(fields, halos)]
    _, planes, corners = layout(sizes)
    depth, height = fields[-1].shape[:2]
    cells = fields[-1].shape[2:]
    sides = sides_of("narrow")
    swap = [(0, 1), (1, 0)]
    rows = sum(shape[0] * tall for shape, _, tall in sizes)
    edge_rows, handed = call(
        functools.partial(edge_kernel, sizes), [(sides, rows) + cells, (planes + depth,) + cells], (), 8
    )(*fields)
    handed = lax.ppermute(handed, "pair", swap)
    low, high = line_exchange("narrow", edge_rows)
    ring, corner = call(
        functools.partial(plane_kernel, sizes),
        [(2 * planes,) + cells, (sides, 2 * corners) + cells],
        (),
        8,
    )(*fields, handed)
    ring = ring_exchange(ring)
    corner_low, corner_high = corner_exchange(corner)
    outs = weight.shape[-1]
    (weights,) = call(weight_kernel, [(9, 4 * weight.shape[2], 2 * outs)], (), 8)(weight)
    lanes = 2 * cells[1]
    (inner,) = call(
        functools.partial(inner_kernel, weights.shape[1] - lanes, half),
        [(depth - 2, height - 2) + cells],
        [pltpu.VMEM((depth, height, cells[0], lanes), bf16)],
        dtype=bf16 if half else f32,
    )(fields[-1], handed, weights, bias)
    received = (low, high, ring, corner_low, corner_high)
    shape, deep, tall = sizes[0]
    framed = (shape[0] + 2 * deep, shape[1] + 2 * tall)
    (passed,) = call(
        functools.partial(pass_kernel, sizes, half),
        [(planes + sides * corners + framed[0],) + cells],
        [pltpu.VMEM(framed + cells, bf16)],
        8,
    )(fields[0], *received)
    passed = lax.ppermute(passed, "pair", swap)
    return sizes, weights, inner, received + (passed,)


def body(
    volume, w_encode, b_encode, w_down, b_down, w_bottom, b_bottom, w_up, b_up, w_decode, b_decode
):
    depth, height, width, skip = volume.shape
    deep_width = w_down.shape[4]
    half_depth, half_height, pairs = depth // 2, height // 2, width // 2
    lanes = 2 * skip
    framed = (depth + 2, height + 2)
    coarse_framed = (half_depth + 4, half_height + 4)

    (packed,) = call(
        pack_kernel,
        [(depth, height, pairs, lanes)],
        [pltpu.VMEM((depth, height, width, skip), f32)],
        8,
    )(volume)
    encode_bias, decode_bias = b_encode.reshape(1, skip), b_decode.reshape(1, skip)
    _, encode_weights, inner, received = exchange(
        [packed], [(1, 1)], True, w_encode.reshape(9, 3, skip, skip), encode_bias
    )
    encoded, coarse = call(
        encode_kernel,
        [(depth, height, pairs, lanes), (half_depth, half_height, pairs, deep_width)],
        [
            pltpu.VMEM(framed + (pairs, lanes), bf16),
            pltpu.VMEM(framed + (skip,), bf16),
            pltpu.VMEM((1, height + 2, pairs, lanes), bf16),
            pltpu.VMEM(framed + (pairs, 2 * lanes), bf16),
        ],
    )(
        packed,
        *received,
        encode_weights,
        inner,
        encode_bias,
        w_down.reshape(4, lanes, deep_width),
        b_down.reshape(1, deep_width),
    )

    sizes, decode_weights, inner, received = exchange(
        [coarse, encoded], [(2, 2), (1, 1)], False, w_decode.reshape(9, 3, lanes, skip), decode_bias
    )
    raised, encoded_ext, columns = call(
        functools.partial(bottom_kernel, sizes),
        [
            (half_depth + 2, 2, half_height + 2, 2, pairs, lanes),
            framed + (pairs, lanes),
            framed + (lanes,),
        ],
        [
            pltpu.VMEM(coarse_framed + (pairs, deep_width), bf16),
            pltpu.VMEM(coarse_framed + (deep_width,), bf16),
            pltpu.VMEM((2, half_height + 4, pairs, deep_width), bf16),
            pltpu.VMEM(coarse_framed + (pairs, 3 * deep_width), bf16),
        ],
    )(
        coarse,
        encoded,
        *received,
        w_bottom.reshape(9, 3 * deep_width, deep_width),
        b_bottom.reshape(1, deep_width),
        w_up.reshape(4, 2, deep_width, skip),
        b_up.reshape(1, skip),
    )
    columns = lax.ppermute(columns, "pair", [(0, 1), (1, 0)])

    (decoded,) = call(
        decode_kernel,
        [(depth, height, width, skip)],
        [
            pltpu.VMEM(framed + (pairs, 2 * lanes), bf16),
            pltpu.VMEM(framed + (pairs, 2 * lanes), bf16),
            pltpu.VMEM((depth, height, pairs, lanes), f32),
            pltpu.VMEM((depth, height, width, skip), f32),
        ],
    )(
        raised.reshape(depth + 4, height + 4, pairs, lanes),
        encoded_ext,
        columns,
        decode_weights,
        inner,
        decode_bias,
    )
    return decoded


def solution(mesh):
    return jax.shard_map(
        body,
        mesh=mesh,
        in_specs=(
            P(("groups", "wide"), "narrow", "pair", None),
            P(),
            P(),
            P(),
            P(),
            P(),
            P(),
            P(),
            P(),
            P(),
            P(),
        ),
        out_specs=P(("groups", "wide"), "narrow", "pair", None),
        check_vma=False,
    )
```

```python
import functools

import jax
import jax.numpy as jnp
from jax import lax
from jax.experimental import pallas as pl
from jax.experimental.pallas import tpu as pltpu
from jax.sharding import PartitionSpec as P


leak_slope = 0.01
f32 = jnp.float32
bf16 = jnp.bfloat16


def leaky_relu(values):
    return jnp.maximum(values, leak_slope * values)


def sides_of(axis):
    return 1 if lax.axis_size(axis) == 2 else 2


def line_exchange(axis, sent):
    count = lax.axis_size(axis)
    if count == 2:
        got = lax.ppermute(sent[0], axis, [(0, 1), (1, 0)])
        return got, got
    up = [(i, i + 1) for i in range(count - 1)]
    down = [(b, a) for a, b in up]
    return lax.ppermute(sent[1], axis, up), lax.ppermute(sent[0], axis, down)


def snake_pairs(groups, count, step):
    order = [
        group * count + (place if group % 2 == 0 else count - 1 - place)
        for group in range(groups)
        for place in range(count)
    ]
    total = len(order)
    return [(order[i], order[(i + step) % total]) for i in range(total)]


def ring_exchange(sent):
    groups, count = lax.axis_size("groups"), lax.axis_size("wide")
    pairs = [
        (2 * a + core, 2 * b + core)
        for core, step in ((0, 1), (1, -1))
        for a, b in snake_pairs(groups, count, step)
    ]
    return lax.ppermute(sent, ("groups", "wide", "pair"), pairs)


def corner_exchange(sent):
    groups, count, tall = (lax.axis_size(axis) for axis in ("groups", "wide", "narrow"))
    moves = [(0, 1), (1, 0)] if tall == 2 else [(i, i + 1) for i in range(tall - 1)]

    def move(array, rows):
        pairs = [
            ((a * tall + c) * 2 + core, (b * tall + d) * 2 + core)
            for core, step in ((0, 1), (1, -1))
            for a, b in snake_pairs(groups, count, step)
            for c, d in rows
        ]
        return lax.ppermute(array, ("groups", "wide", "narrow", "pair"), pairs)

    if tall == 2:
        got = move(sent[0], moves)
        return got, got
    return move(sent[1], moves), move(sent[0], [(d, c) for c, d in moves])


def call(kernel, outs, scratch=(), megabytes=24, dtype=bf16):
    return pl.pallas_call(
        kernel,
        out_shape=[jax.ShapeDtypeStruct(shape, dtype) for shape in outs],
        scratch_shapes=list(scratch),
        cost_estimate=pl.CostEstimate(flops=4 * 10**9, transcendentals=0, bytes_accessed=10**6),
        compiler_params=pltpu.CompilerParams(vmem_limit_bytes=megabytes << 20),
    )


def edges(axis):
    place = lax.axis_index(axis)
    return place == 0, place == lax.axis_size(axis) - 1


def sends_high():
    even = lax.axis_index("groups") % 2 == 0
    return (lax.axis_index("pair") == 0) == even


def either(condition, put):
    @pl.when(condition)
    def _():
        put(True)

    @pl.when(jnp.logical_not(condition))
    def _():
        put(False)


def rows_at(ref, at, *lead):
    count = 1
    for size in lead:
        count *= size
    return ref[at : at + count].reshape(lead + tuple(ref.shape[1:]))


def layout(fields):
    planes, corners, spots = 0, 0, []
    for shape, deep, tall in fields:
        spots.append((planes, corners))
        planes += deep * shape[1]
        corners += deep * tall
    return spots, planes, corners


def fill_planes(ext, base, middle, low, high):
    deep, height = middle.shape[:2]
    tall = low.shape[1]
    ext[base : base + deep, :tall] = low
    ext[base : base + deep, tall : tall + height] = middle
    ext[base : base + deep, tall + height :] = high


def fill_block(ext, own, low, high, at, deep, tall):
    depth = own.shape[0]
    fill_planes(
        ext,
        deep,
        own[...],
        rows_at(low, at, depth, tall),
        rows_at(high, at, depth, tall),
    )


def clear_edges(ext, deep, tall):
    first, last = edges("narrow")
    planes, rows = ext.shape[:2]
    blank_rows = jnp.zeros((planes, tall) + ext.shape[2:], bf16)
    blank_planes = jnp.zeros((deep,) + ext.shape[1:], bf16)

    @pl.when(first)
    def _():
        ext[:, :tall] = blank_rows

    @pl.when(last)
    def _():
        ext[:, rows - tall :] = blank_rows

    first, last = edges("wide")

    @pl.when(first)
    def _():
        ext[:deep] = blank_planes

    @pl.when(last)
    def _():
        ext[planes - deep :] = blank_planes


def fill_frame(ext, own, low, high, planes, corner_low, corner_high, passed, spot, at, deep, tall):
    depth, height = own.shape[:2]
    plane_at, corner_at = spot
    count = corner_low.shape[0] // 2
    split = planes.shape[0] // 2
    fill_block(ext, own, low, high, at, deep, tall)
    near = (
        rows_at(planes, plane_at, deep, height),
        rows_at(corner_low, corner_at, deep, tall),
        rows_at(corner_high, corner_at, deep, tall),
    )
    last = split + (sides_of("narrow") - 1) * count
    far = (
        rows_at(passed, plane_at, deep, height),
        rows_at(passed, split + corner_at, deep, tall),
        rows_at(passed, last + corner_at, deep, tall),
    )

    either(sends_high(), put_sides(ext, depth, deep, near, far))
    clear_edges(ext, deep, tall)


def put_sides(ext, depth, deep, near, far):
    def put(low_is_near):
        fill_planes(ext, 0, *(near if low_is_near else far))
        fill_planes(ext, deep + depth, *(far if low_is_near else near))

    return put


def fill_columns(
    columns, passed, start, frame, planes, corner_low, corner_high, spot, height, deep, tall, half
):
    plane_at, corner_at = spot
    count, corners = planes.shape[0] // 2, corner_low.shape[0] // 2
    total, rows, lanes = columns.shape
    for plane in range(total):
        columns[plane] = passed[start + plane, :rows, :lanes]
    fill_planes(
        frame,
        0,
        rows_at(planes, count + plane_at, deep, height),
        rows_at(corner_low, corners + corner_at, deep, tall),
        rows_at(corner_high, corners + corner_at, deep, tall),
    )
    first, last = edges("narrow")
    blank = jnp.zeros((deep, tall) + frame.shape[2:], bf16)

    @pl.when(first)
    def _():
        frame[:, :tall] = blank

    @pl.when(last)
    def _():
        frame[:, tall + height :] = blank

    at_low = lax.axis_index("pair") == 0
    at_edge = edges("wide")

    def put(low_side):
        edge = at_edge[0] if low_side else at_edge[1]
        for layer in range(deep):
            low, high = column_values(frame[layer], half)
            chosen = jnp.where(at_low, low, high)
            chosen = jnp.where(edge, jnp.zeros_like(chosen), chosen)
            columns[layer if low_side else total - deep + layer] = chosen

    either(sends_high(), put)


def inner_column(block, half):
    low, high = column_values(block, half)
    return jnp.where(lax.axis_index("pair") == 0, high, low)


def column_values(block, half):
    lanes = block.shape[-1]
    wide = block.astype(f32)
    if half:
        return wide[:, 0, : lanes // 2].astype(bf16), wide[:, -1, lanes // 2 :].astype(bf16)
    return wide[:, 0, :].astype(bf16), wide[:, -1, :].astype(bf16)


def shifted(values, column, step):
    columns = values.shape[1]
    spot = lax.broadcasted_iota(jnp.int32, values.shape, 1)
    if step > 0:
        return jnp.where(spot == 0, column[:, None, :], pltpu.roll(values, 1, 1))
    return jnp.where(
        spot == columns - 1, column[:, None, :], pltpu.roll(values, columns - 1, 1)
    )


def pair_columns(got, plane, lanes):
    first, last = edges("pair")
    column = got[plane, :, lanes].astype(f32)
    blank = jnp.zeros_like(column)
    return jnp.where(first, blank, column), jnp.where(last, blank, column)


def spread_pairs(taps, base, block, low, high):
    lanes = block.shape[-1] // 2
    wide = block.astype(f32)
    taps[:, :, base : base + lanes] = shifted(wide[:, :, lanes:], low, 1).astype(bf16)
    taps[:, :, base + lanes : base + 3 * lanes] = block
    taps[:, :, base + 3 * lanes : base + 4 * lanes] = shifted(
        wide[:, :, :lanes], high, -1
    ).astype(bf16)


def spread_weights(packed, tap, base, taken):
    rows, outs = taken[0].shape
    blank = jnp.zeros((rows, outs), bf16)
    for cell in range(4):
        at = base + cell * rows
        packed[tap, at : at + rows, :outs] = taken[cell] if cell < 3 else blank
        packed[tap, at : at + rows, outs:] = taken[cell - 1] if cell > 0 else blank


def conv_sum(taps, packed, base, select):
    lanes = taps.shape[-1]
    summed = None
    for a in range(3):
        for b in range(3):
            rows = [taps[part].reshape(-1, lanes) for part in select(a, b)]
            rows = rows[0] if len(rows) == 1 else jnp.concatenate(rows, axis=0)
            part = jnp.dot(
                rows, packed[3 * a + b, base : base + lanes], preferred_element_type=f32
            )
            summed = part if summed is None else summed + part
    return summed


def conv_rows(taps, packed, depth, height, base=0):
    return conv_sum(
        taps, packed, base, lambda a, b: [(slice(a, a + depth), slice(b, b + height))]
    )


def conv_border(taps, packed, depth, height, base=0):
    def select(a, b):
        planes = slice(a + 1, a + depth - 1)
        rows = slice(b, b + height)
        return [(a, rows), (a + depth - 1, rows), (planes, b), (planes, b + height - 1)]

    summed = conv_sum(taps, packed, base, select)
    columns, lanes = taps.shape[2], summed.shape[-1]
    inner = slice(1, depth - 1)
    at = 0
    pieces = []
    for where, count in (
        ((0,), height),
        ((depth - 1,), height),
        ((inner, 0), depth - 2),
        ((inner, height - 1), depth - 2),
    ):
        block = summed[at : at + count * columns].reshape(count, columns, lanes)
        pieces.append((where, block))
        at += count * columns
    return pieces


def inner_kernel(base, final, field, handed, packed, bias, out, taps):
    depth, height, _, lanes = field.shape
    start = handed.shape[0] - depth
    columns_in = handed.at[start:, :height, : lanes // 2]
    for plane in range(depth):
        before, after = pair_columns(columns_in, plane, slice(None))
        spread_pairs(taps.at[plane], 0, field[plane], before, after)
    summed = conv_rows(taps, packed, depth - 2, height - 2, base)
    if final:
        summed = leaky_relu(summed + jnp.tile(bias[...], (1, 2))).astype(bf16)
    out[...] = summed.reshape(out.shape)


def choose_side(axis, sent, put):
    if sent.shape[0] == 1:
        at_low = lax.axis_index(axis) == 0

        @pl.when(at_low)
        def _():
            put(0, True)

        @pl.when(jnp.logical_not(at_low))
        def _():
            put(0, False)

    else:
        put(0, False)
        put(1, True)


def pack_pairs(out, cells, spread):
    pairs, lanes = out.shape[1], cells.shape[-1]
    spread[...] = cells.astype(f32)
    for odd in range(2):
        half = spread[:, pl.ds(odd, pairs, stride=2), :]
        out[:, :, odd * lanes : (odd + 1) * lanes] = half.astype(bf16)


def pack_kernel(volume, packed, spread):
    for plane in range(volume.shape[0]):
        pack_pairs(packed.at[plane], volume[plane], spread.at[plane])


def put_column(ref, at, column):
    ref[at] = jnp.zeros(ref.shape[1:], bf16)
    ref[at, : column.shape[0], : column.shape[1]] = column


def edge_kernel(sizes, *refs):
    fields, (edge_rows, handed) = refs[: len(sizes)], refs[len(sizes) :]

    def put_rows(slot, high):
        at = 0
        for field, (_, _, tall) in zip(fields, sizes):
            depth, height = field.shape[:2]
            first = height - tall if high else 0
            rows = field[:, first : first + tall]
            edge_rows[slot, at : at + depth * tall] = rows.reshape((depth * tall,) + rows.shape[2:])
            at += depth * tall

    choose_side("narrow", edge_rows, put_rows)
    either(sends_high(), lambda high: put_boundary(handed, fields, sizes, not high))
    field, start = fields[-1], layout(sizes)[1]
    for plane in range(field.shape[0]):
        put_column(handed, start + plane, inner_column(field[plane], True))


def put_boundary(out, fields, sizes, high):
    at = 0
    for field, (_, deep, _) in zip(fields, sizes):
        depth, height = field.shape[:2]
        planes = field[depth - deep :] if high else field[:deep]
        out[at : at + deep * height] = planes.reshape((deep * height,) + planes.shape[2:])
        at += deep * height


def plane_kernel(sizes, *refs):
    fields, (handed, planes, corners) = refs[: len(sizes)], refs[len(sizes) :]
    spots, count, few = layout(sizes)
    planes[count:] = handed[:count]
    either(sends_high(), lambda high: put_boundary(planes, fields, sizes, high))

    def put(slot, high):
        for (shape, deep, tall), (plane_at, corner_at) in zip(sizes, spots):
            height = shape[1]
            first = height - tall if high else 0
            for part in range(2):
                for layer in range(deep):
                    source = part * count + plane_at + layer * height + first
                    target = part * few + corner_at + layer * tall
                    corners[slot, target : target + tall] = planes[source : source + tall]

    choose_side("narrow", corners, put)


def pass_kernel(sizes, halves, *refs):
    fields, (low, high, planes, corner_low, corner_high) = refs[: len(sizes)], refs[len(sizes) :][:5]
    passed, frames = refs[len(sizes) + 5], refs[len(sizes) + 6 :]
    spots, count, few = layout(sizes)
    start = count + sides_of("narrow") * few
    passed[:count] = planes[count:]
    passed[count : count + few] = corner_low[few:]
    passed[start - few : start] = corner_high[few:]
    at = 0
    for own, ext, half, (shape, deep, tall), (plane_at, corner_at) in zip(
        fields, frames, halves, sizes, spots
    ):
        depth, height = shape[:2]
        fill_block(ext, own, low, high, at, deep, tall)
        at += depth * tall
        near = (
            rows_at(planes, plane_at, deep, height),
            rows_at(corner_low, corner_at, deep, tall),
            rows_at(corner_high, corner_at, deep, tall),
        )
        blank = tuple(jnp.zeros_like(part) for part in near)
        either(sends_high(), put_sides(ext, depth, deep, near, blank))
        clear_edges(ext, deep, tall)
        for plane in range(ext.shape[0]):
            put_column(passed, start + plane, inner_column(ext[plane], half))
        start += ext.shape[0]


def weight_kernel(weight, packed):
    outs = weight.shape[-1]
    for tap in range(9):
        for block in range(weight.shape[2] // outs):
            rows = slice(block * outs, (block + 1) * outs)
            spread_weights(packed, tap, 4 * outs * block, [weight[tap, c, rows] for c in range(3)])


def encode_kernel(
    own,
    low,
    high,
    planes,
    corner_low,
    corner_high,
    passed,
    packed,
    inner,
    bias,
    down,
    down_bias,
    encoded,
    coarse,
    ext,
    columns_in,
    frame,
    taps,
):
    lanes = ext.shape[-1]
    spot = (0, 0)
    fill_frame(ext, own, low, high, planes, corner_low, corner_high, passed, spot, 0, 1, 1)
    start = passed.shape[0] - ext.shape[0]
    fill_columns(
        columns_in,
        passed,
        start,
        frame,
        planes,
        corner_low,
        corner_high,
        spot,
        own.shape[1],
        1,
        1,
        True,
    )
    for plane in range(ext.shape[0]):
        before, after = pair_columns(columns_in, plane, slice(None))
        spread_pairs(taps.at[plane], 0, ext[plane], before, after)
    depth, height, columns, _ = encoded.shape
    deep, tall = coarse.shape[:2]
    both = jnp.tile(bias[...], (1, 2))
    encoded[1 : depth - 1, 1 : height - 1] = inner[...]
    for where, block in conv_border(taps, packed, depth, height):
        encoded[where] = leaky_relu(block + both).astype(bf16)
    fine = encoded[...].reshape(deep, 2, tall, 2, columns, lanes)
    lifted = None
    for a in range(2):
        for b in range(2):
            part = jnp.dot(
                fine[:, a, :, b].reshape(-1, lanes), down[2 * a + b], preferred_element_type=f32
            )
            lifted = part if lifted is None else lifted + part
    coarse[...] = leaky_relu(lifted + down_bias[...]).astype(bf16).reshape(coarse.shape)


def bottom_kernel(
    sizes,
    coarse,
    encoded,
    low,
    high,
    planes,
    corner_low,
    corner_high,
    passed,
    weight,
    bias,
    up,
    up_bias,
    raised,
    encoded_ext,
    columns,
    encoded_columns,
    coarse_ext,
    columns_in,
    frame,
    encoded_frame,
    taps,
):
    lanes = coarse_ext.shape[-1]
    spots = layout(sizes)[0]
    at, start = 0, passed.shape[0] - coarse_ext.shape[0] - encoded_ext.shape[0]
    for ext, own, side, edge, half, spot, (shape, deep, tall) in zip(
        (coarse_ext, encoded_ext),
        (coarse, encoded),
        (columns_in, encoded_columns),
        (frame, encoded_frame),
        (False, True),
        spots,
        sizes,
    ):
        fill_frame(
            ext, own, low, high, planes, corner_low, corner_high, passed, spot, at, deep, tall
        )
        fill_columns(
            side,
            passed,
            start,
            edge,
            planes,
            corner_low,
            corner_high,
            spot,
            shape[1],
            deep,
            tall,
            half,
        )
        at += shape[0] * tall
        start += ext.shape[0]
    for plane in range(coarse_ext.shape[0]):
        before, after = pair_columns(columns_in, plane, slice(None))
        block = coarse_ext[plane]
        wide = block.astype(f32)
        taps[plane, :, :, :lanes] = shifted(wide, before, 1).astype(bf16)
        taps[plane, :, :, lanes : 2 * lanes] = block
        taps[plane, :, :, 2 * lanes :] = shifted(wide, after, -1).astype(bf16)
    deep, _, tall, _, count, _ = raised.shape
    start, span = 0, tall
    if sides_of("narrow") == 1:
        start, span = jnp.where(lax.axis_index("narrow") == 0, 1, 0), tall - 1
    summed = conv_sum(
        taps, weight, 0, lambda a, b: [(slice(a, a + deep), pl.ds(b + start, span))]
    )
    bottom = leaky_relu(summed + bias[...]).astype(bf16)
    both = jnp.tile(up_bias[...], (1, 2))
    for a in range(2):
        for b in range(2):
            matrix = jnp.concatenate([up[2 * a + b, 0], up[2 * a + b, 1]], axis=-1)
            lifted = jnp.dot(bottom, matrix, preferred_element_type=f32) + both
            lifted = lifted.astype(bf16).reshape(deep, span, count, lanes)
            raised[:, a, pl.ds(start, span), b] = lifted
    blank_plane = jnp.zeros(raised.shape[1:], bf16)
    blank_row = jnp.zeros((deep, 2, 2, count, lanes), bf16)
    first, last = edges("narrow")

    @pl.when(first)
    def _():
        raised[:, :, 0] = blank_row

    @pl.when(last)
    def _():
        raised[:, :, tall - 1] = blank_row

    first, last = edges("wide")

    @pl.when(first)
    def _():
        raised[0] = blank_plane

    @pl.when(last)
    def _():
        raised[deep - 1] = blank_plane

    planes, height = encoded_ext.shape[:2]
    for plane in range(planes):
        z, a = (plane + 1) // 2, (plane + 1) % 2
        whole = raised[z, a].reshape(2 * tall, count, lanes)[1 : 1 + height]
        columns[plane] = inner_column(whole, True)


def border_kernel(encoded_ext, columns_in, packed, inner, sums, taps):
    lanes = taps.shape[-1]
    for plane in range(encoded_ext.shape[0]):
        low, high = pair_columns(columns_in, plane, slice(None))
        spread_pairs(taps.at[plane], 0, encoded_ext[plane], low, high)
    depth, height = sums.shape[:2]
    sums[1 : depth - 1, 1 : height - 1] = inner[...]
    for where, block in conv_border(taps, packed, depth, height, packed.shape[1] - lanes):
        sums[where] = block


def decode_kernel(raised, columns_in, packed, partial, bias, decoded, taps, spread):
    planes, height, columns, _ = taps.shape
    for plane in range(planes):
        low, high = pair_columns(columns_in, plane, slice(None))
        spread_pairs(taps.at[plane], 0, raised[plane + 1, 1 : 1 + height], low, high)
    depth, rows, _, outs = decoded.shape
    summed = conv_rows(taps, packed, depth, rows).reshape(partial.shape) + partial[...]
    summed = leaky_relu(summed + jnp.tile(bias[...], (1, 2)))
    for odd in range(2):
        half = summed[:, :, :, odd * outs : (odd + 1) * outs]
        spread[:, :, pl.ds(odd, columns, stride=2), :] = half
    decoded[...] = spread[...].astype(bf16)


def exchange(turn, fields, halos, halves, weight, bias):
    sizes = [(field.shape, deep, tall) for field, (deep, tall) in zip(fields, halos)]
    _, planes, corners = layout(sizes)
    depth, height = fields[-1].shape[:2]
    cells = fields[-1].shape[2:]
    sides = sides_of("narrow")
    swap = [(0, 1), (1, 0)]
    rows = sum(shape[0] * tall for shape, _, tall in sizes)
    edge_rows, handed = call(
        functools.partial(edge_kernel, sizes), [(sides, rows) + cells, (planes + depth,) + cells], (), 8
    )(*fields)
    handed = lax.ppermute(handed, "pair", swap)
    low, high = line_exchange("narrow", edge_rows)
    ring, corner = call(
        functools.partial(plane_kernel, sizes),
        [(2 * planes,) + cells, (sides, 2 * corners) + cells],
        (),
        8,
    )(*fields, handed)
    ring = ring_exchange(ring)
    corner_low, corner_high = corner_exchange(corner)
    outs = weight.shape[-1]
    (weights,) = call(weight_kernel, [(9, 4 * weight.shape[2], 2 * outs)], (), 8)(weight)
    lanes = 2 * cells[1]
    (inner,) = call(
        functools.partial(inner_kernel, weights.shape[1] - lanes, turn == 0),
        [(depth - 2, height - 2) + cells],
        [pltpu.VMEM((depth, height, cells[0], lanes), bf16)],
        dtype=bf16 if turn == 0 else f32,
    )(fields[-1], handed, weights, bias)
    received = (low, high, ring, corner_low, corner_high)
    frames = [
        (shape[0] + 2 * deep, shape[1] + 2 * tall) + cells for shape, deep, tall in sizes
    ]
    (passed,) = call(
        functools.partial(pass_kernel, sizes, halves),
        [(planes + sides * corners + sum(frame[0] for frame in frames),) + cells],
        [pltpu.VMEM(frame, bf16) for frame in frames],
        8,
    )(*fields, *received)
    passed = lax.ppermute(passed, "pair", swap)
    return sizes, weights, inner, received + (passed,)


def body(
    volume, w_encode, b_encode, w_down, b_down, w_bottom, b_bottom, w_up, b_up, w_decode, b_decode
):
    depth, height, width, skip = volume.shape
    deep_width = w_down.shape[4]
    half_depth, half_height, pairs = depth // 2, height // 2, width // 2
    lanes = 2 * skip
    framed = (depth + 2, height + 2)
    coarse_framed = (half_depth + 4, half_height + 4)

    (packed,) = call(
        pack_kernel,
        [(depth, height, pairs, lanes)],
        [pltpu.VMEM((depth, height, width, skip), f32)],
        8,
    )(volume)
    encode_bias, decode_bias = b_encode.reshape(1, skip), b_decode.reshape(1, skip)
    _, encode_weights, inner, received = exchange(
        0, [packed], [(1, 1)], [True], w_encode.reshape(9, 3, skip, skip), encode_bias
    )
    encoded, coarse = call(
        encode_kernel,
        [(depth, height, pairs, lanes), (half_depth, half_height, pairs, deep_width)],
        [
            pltpu.VMEM(framed + (pairs, lanes), bf16),
            pltpu.VMEM(framed + (skip,), bf16),
            pltpu.VMEM((1, height + 2, pairs, lanes), bf16),
            pltpu.VMEM(framed + (pairs, 2 * lanes), bf16),
        ],
    )(
        packed,
        *received,
        encode_weights,
        inner,
        encode_bias,
        w_down.reshape(4, lanes, deep_width),
        b_down.reshape(1, deep_width),
    )

    sizes, decode_weights, inner, received = exchange(
        1,
        [coarse, encoded],
        [(2, 2), (1, 1)],
        [False, True],
        w_decode.reshape(9, 3, lanes, skip),
        decode_bias,
    )
    raised, encoded_ext, columns, encoded_columns = call(
        functools.partial(bottom_kernel, sizes),
        [
            (half_depth + 2, 2, half_height + 2, 2, pairs, lanes),
            framed + (pairs, lanes),
            framed + (skip,),
            framed + (skip,),
        ],
        [
            pltpu.VMEM(coarse_framed + (pairs, deep_width), bf16),
            pltpu.VMEM(coarse_framed + (deep_width,), bf16),
            pltpu.VMEM((2, half_height + 4, pairs, deep_width), bf16),
            pltpu.VMEM((1, height + 2, pairs, lanes), bf16),
            pltpu.VMEM(coarse_framed + (pairs, 3 * deep_width), bf16),
        ],
    )(
        coarse,
        encoded,
        *received,
        w_bottom.reshape(9, 3 * deep_width, deep_width),
        b_bottom.reshape(1, deep_width),
        w_up.reshape(4, 2, deep_width, skip),
        b_up.reshape(1, skip),
    )
    taps = pltpu.VMEM(framed + (pairs, 2 * lanes), bf16)
    columns = lax.ppermute(columns, "pair", [(0, 1), (1, 0)])
    (partial,) = call(
        border_kernel, [(depth, height, pairs, lanes)], [taps], dtype=f32
    )(encoded_ext, encoded_columns, decode_weights, inner)

    (decoded,) = call(
        decode_kernel,
        [(depth, height, width, skip)],
        [taps, pltpu.VMEM((depth, height, width, skip), f32)],
    )(
        raised.reshape(depth + 4, height + 4, pairs, lanes),
        columns,
        decode_weights,
        partial,
        decode_bias,
    )
    return decoded


def solution(mesh):
    return jax.shard_map(
        body,
        mesh=mesh,
        in_specs=(
            P(("groups", "wide"), "narrow", "pair", None),
            P(),
            P(),
            P(),
            P(),
            P(),
            P(),
            P(),
            P(),
            P(),
            P(),
        ),
        out_specs=P(("groups", "wide"), "narrow", "pair", None),
        check_vma=False,
    )
```

```python
import functools

import jax
import jax.numpy as jnp
from jax import lax
from jax.experimental import pallas as pl
from jax.experimental.pallas import tpu as pltpu
from jax.sharding import PartitionSpec as P


leak_slope = 0.01
f32 = jnp.float32
bf16 = jnp.bfloat16


def leaky_relu(values):
    return jnp.maximum(values, leak_slope * values)


def sides_of(axis):
    return 1 if lax.axis_size(axis) == 2 else 2


def line_exchange(axis, sent):
    count = lax.axis_size(axis)
    if count == 2:
        got = lax.ppermute(sent[0], axis, [(0, 1), (1, 0)])
        return got, got
    up = [(i, i + 1) for i in range(count - 1)]
    down = [(b, a) for a, b in up]
    return lax.ppermute(sent[1], axis, up), lax.ppermute(sent[0], axis, down)


def snake_pairs(groups, count, step):
    order = [
        group * count + (place if group % 2 == 0 else count - 1 - place)
        for group in range(groups)
        for place in range(count)
    ]
    total = len(order)
    return [(order[i], order[(i + step) % total]) for i in range(total)]


def ring_exchange(sent):
    groups, count = lax.axis_size("groups"), lax.axis_size("wide")
    pairs = [
        (2 * a + core, 2 * b + core)
        for core, step in ((0, 1), (1, -1))
        for a, b in snake_pairs(groups, count, step)
    ]
    return lax.ppermute(sent, ("groups", "wide", "pair"), pairs)


def corner_exchange(sent):
    groups, count, tall = (lax.axis_size(axis) for axis in ("groups", "wide", "narrow"))
    moves = [(0, 1), (1, 0)] if tall == 2 else [(i, i + 1) for i in range(tall - 1)]

    def move(array, rows):
        pairs = [
            ((a * tall + c) * 2 + core, (b * tall + d) * 2 + core)
            for core, step in ((0, 1), (1, -1))
            for a, b in snake_pairs(groups, count, step)
            for c, d in rows
        ]
        return lax.ppermute(array, ("groups", "wide", "narrow", "pair"), pairs)

    if tall == 2:
        got = move(sent[0], moves)
        return got, got
    return move(sent[1], moves), move(sent[0], [(d, c) for c, d in moves])


def call(kernel, outs, scratch=(), megabytes=24, dtype=bf16, **specs):
    return pl.pallas_call(
        kernel,
        **specs,
        out_shape=[jax.ShapeDtypeStruct(shape, dtype) for shape in outs],
        scratch_shapes=list(scratch),
        cost_estimate=pl.CostEstimate(flops=4 * 10**9, transcendentals=0, bytes_accessed=10**6),
        compiler_params=pltpu.CompilerParams(vmem_limit_bytes=megabytes << 20),
    )


def edges(axis):
    place = lax.axis_index(axis)
    return place == 0, place == lax.axis_size(axis) - 1


def sends_high():
    even = lax.axis_index("groups") % 2 == 0
    return (lax.axis_index("pair") == 0) == even


def either(condition, put):
    @pl.when(condition)
    def _():
        put(True)

    @pl.when(jnp.logical_not(condition))
    def _():
        put(False)


def rows_at(ref, at, *lead):
    count = 1
    for size in lead:
        count *= size
    return ref[at : at + count].reshape(lead + tuple(ref.shape[1:]))


def layout(fields):
    planes, corners, spots = 0, 0, []
    for shape, deep, tall in fields:
        spots.append((planes, corners))
        planes += deep * shape[1]
        corners += deep * tall
    return spots, planes, corners


def fill_planes(ext, base, middle, low, high):
    deep, height = middle.shape[:2]
    tall = low.shape[1]
    ext[base : base + deep, :tall] = low
    ext[base : base + deep, tall : tall + height] = middle
    ext[base : base + deep, tall + height :] = high


def fill_block(ext, own, low, high, at, deep, tall):
    depth = own.shape[0]
    fill_planes(
        ext,
        deep,
        own[...],
        rows_at(low, at, depth, tall),
        rows_at(high, at, depth, tall),
    )


def clear_edges(ext, deep, tall):
    first, last = edges("narrow")
    planes, rows = ext.shape[:2]
    blank_rows = jnp.zeros((planes, tall) + ext.shape[2:], bf16)
    blank_planes = jnp.zeros((deep,) + ext.shape[1:], bf16)

    @pl.when(first)
    def _():
        ext[:, :tall] = blank_rows

    @pl.when(last)
    def _():
        ext[:, rows - tall :] = blank_rows

    first, last = edges("wide")

    @pl.when(first)
    def _():
        ext[:deep] = blank_planes

    @pl.when(last)
    def _():
        ext[planes - deep :] = blank_planes


def fill_frame(ext, own, low, high, planes, corner_low, corner_high, passed, spot, at, deep, tall):
    depth, height = own.shape[:2]
    plane_at, corner_at = spot
    count = corner_low.shape[0] // 2
    split = planes.shape[0] // 2
    fill_block(ext, own, low, high, at, deep, tall)
    near = (
        rows_at(planes, plane_at, deep, height),
        rows_at(corner_low, corner_at, deep, tall),
        rows_at(corner_high, corner_at, deep, tall),
    )
    last = split + (sides_of("narrow") - 1) * count
    far = (
        rows_at(passed, plane_at, deep, height),
        rows_at(passed, split + corner_at, deep, tall),
        rows_at(passed, last + corner_at, deep, tall),
    )

    either(sends_high(), put_sides(ext, depth, deep, near, far))
    clear_edges(ext, deep, tall)


def put_sides(ext, depth, deep, near, far):
    def put(low_is_near):
        fill_planes(ext, 0, *(near if low_is_near else far))
        fill_planes(ext, deep + depth, *(far if low_is_near else near))

    return put


def fill_columns(
    columns, passed, start, frame, planes, corner_low, corner_high, spot, height, deep, tall, half
):
    plane_at, corner_at = spot
    count, corners = planes.shape[0] // 2, corner_low.shape[0] // 2
    total, rows, lanes = columns.shape
    for plane in range(total):
        columns[plane] = passed[column_place(passed, start, plane, rows, lanes)]
    fill_planes(
        frame,
        0,
        rows_at(planes, count + plane_at, deep, height),
        rows_at(corner_low, corners + corner_at, deep, tall),
        rows_at(corner_high, corners + corner_at, deep, tall),
    )
    first, last = edges("narrow")
    blank = jnp.zeros((deep, tall) + frame.shape[2:], bf16)

    @pl.when(first)
    def _():
        frame[:, :tall] = blank

    @pl.when(last)
    def _():
        frame[:, tall + height :] = blank

    at_low = lax.axis_index("pair") == 0
    at_edge = edges("wide")

    def put(low_side):
        edge = at_edge[0] if low_side else at_edge[1]
        for layer in range(deep):
            low, high = column_values(frame[layer], half)
            chosen = jnp.where(at_low, low, high)
            chosen = jnp.where(edge, jnp.zeros_like(chosen), chosen)
            columns[layer if low_side else total - deep + layer] = chosen

    either(sends_high(), put)


def inner_column(block, half):
    low, high = column_values(block, half)
    return jnp.where(lax.axis_index("pair") == 0, high, low)


def column_values(block, half):
    lanes = block.shape[-1]
    wide = block.astype(f32)
    if half:
        return wide[:, 0, : lanes // 2].astype(bf16), wide[:, -1, lanes // 2 :].astype(bf16)
    return wide[:, 0, :].astype(bf16), wide[:, -1, :].astype(bf16)


def shifted(values, column, step):
    columns = values.shape[1]
    spot = lax.broadcasted_iota(jnp.int32, values.shape, 1)
    if step > 0:
        return jnp.where(spot == 0, column[:, None, :], pltpu.roll(values, 1, 1))
    return jnp.where(
        spot == columns - 1, column[:, None, :], pltpu.roll(values, columns - 1, 1)
    )


def pair_columns(column):
    first, last = edges("pair")
    column = column.astype(f32)
    blank = jnp.zeros_like(column)
    return jnp.where(first, blank, column), jnp.where(last, blank, column)


def spread_pairs(taps, base, block, low, high):
    lanes = block.shape[-1] // 2
    wide = block.astype(f32)
    taps[:, :, base : base + lanes] = shifted(wide[:, :, lanes:], low, 1).astype(bf16)
    taps[:, :, base + lanes : base + 3 * lanes] = block
    taps[:, :, base + 3 * lanes : base + 4 * lanes] = shifted(
        wide[:, :, :lanes], high, -1
    ).astype(bf16)


def spread_weights(packed, tap, base, taken):
    rows, outs = taken[0].shape
    blank = jnp.zeros((rows, outs), bf16)
    for cell in range(4):
        at = base + cell * rows
        packed[tap, at : at + rows, :outs] = taken[cell] if cell < 3 else blank
        packed[tap, at : at + rows, outs:] = taken[cell - 1] if cell > 0 else blank


def conv_sum(taps, packed, base, select):
    lanes = taps.shape[-1]
    summed = None
    for a in range(3):
        for b in range(3):
            rows = [taps[part].reshape(-1, lanes) for part in select(a, b)]
            rows = rows[0] if len(rows) == 1 else jnp.concatenate(rows, axis=0)
            part = jnp.dot(
                rows, packed[3 * a + b, base : base + lanes], preferred_element_type=f32
            )
            summed = part if summed is None else summed + part
    return summed


def conv_rows(taps, packed, depth, height, base=0):
    return conv_sum(
        taps, packed, base, lambda a, b: [(slice(a, a + depth), slice(b, b + height))]
    )


def conv_border(taps, packed, depth, height, base=0):
    def select(a, b):
        planes = slice(a + 1, a + depth - 1)
        rows = slice(b, b + height)
        return [(a, rows), (a + depth - 1, rows), (planes, b), (planes, b + height - 1)]

    summed = conv_sum(taps, packed, base, select)
    columns, lanes = taps.shape[2], summed.shape[-1]
    inner = slice(1, depth - 1)
    at = 0
    pieces = []
    for where, count in (
        ((0,), height),
        ((depth - 1,), height),
        ((inner, 0), depth - 2),
        ((inner, height - 1), depth - 2),
    ):
        block = summed[at : at + count * columns].reshape(count, columns, lanes)
        pieces.append((where, block))
        at += count * columns
    return pieces


def inner_kernel(base, final, field, handed, packed, bias, out, taps):
    depth, height, _, lanes = field.shape
    start = handed.shape[0] - field_slabs(field.shape, True)
    for plane in range(depth):
        before, after = pair_columns(
            handed[column_place(handed, start, plane, height, lanes // 2)]
        )
        spread_pairs(taps.at[plane], 0, field[plane], before, after)
    summed = conv_rows(taps, packed, depth - 2, height - 2, base)
    if final:
        summed = leaky_relu(summed + jnp.tile(bias[...], (1, 2))).astype(bf16)
    out[...] = summed.reshape(out.shape)


def choose_side(axis, sent, put):
    if sent.shape[0] == 1:
        at_low = lax.axis_index(axis) == 0

        @pl.when(at_low)
        def _():
            put(0, True)

        @pl.when(jnp.logical_not(at_low))
        def _():
            put(0, False)

    else:
        put(0, False)
        put(1, True)


def pack_pairs(out, cells, spread):
    pairs, lanes = out.shape[1], cells.shape[-1]
    spread[...] = cells.astype(f32)
    for odd in range(2):
        half = spread[:, pl.ds(odd, pairs, stride=2), :]
        out[:, :, odd * lanes : (odd + 1) * lanes] = half.astype(bf16)


def pack_kernel(volume, packed, here, spread, arrived):
    copies = [
        pltpu.make_async_copy(volume.at[plane], here.at[plane], arrived.at[plane])
        for plane in range(volume.shape[0])
    ]
    for copy in copies:
        copy.start()
    for plane, copy in enumerate(copies):
        copy.wait()
        pack_pairs(packed.at[plane], here[plane], spread.at[plane])


def per_tile(cells, rows, lanes):
    return max(cells[0] // (-(-rows // 8) * 8), 1), cells[1] // lanes


def slabs(cells, planes, rows, lanes):
    down, across = per_tile(cells, rows, lanes)
    return -(-planes // (down * across))


def column_place(ref, start, plane, rows, lanes):
    down, across = per_tile(ref.shape[1:], rows, lanes)
    slab, spot = divmod(plane, down * across)
    row, lane = spot // across * (-(-rows // 8) * 8), spot % across * lanes
    return start + slab, slice(row, row + rows), slice(lane, lane + lanes)


def put_column(ref, start, plane, column):
    place = column_place(ref, start, plane, *column.shape)
    ref[place] = column


def field_slabs(shape, half):
    return slabs(shape[2:], shape[0], shape[1], shape[3] // 2 if half else shape[3])


def edge_kernel(sizes, *refs):
    fields, (edge_rows, handed) = refs[: len(sizes)], refs[len(sizes) :]

    def put_rows(slot, high):
        at = 0
        for field, (_, _, tall) in zip(fields, sizes):
            depth, height = field.shape[:2]
            first = height - tall if high else 0
            rows = field[:, first : first + tall]
            edge_rows[slot, at : at + depth * tall] = rows.reshape((depth * tall,) + rows.shape[2:])
            at += depth * tall

    choose_side("narrow", edge_rows, put_rows)
    either(sends_high(), lambda high: put_boundary(handed, fields, sizes, not high))
    field, start = fields[-1], layout(sizes)[1]
    handed[start:] = jnp.zeros((handed.shape[0] - start,) + handed.shape[1:], bf16)
    for plane in range(field.shape[0]):
        put_column(handed, start, plane, inner_column(field[plane], True))


def put_boundary(out, fields, sizes, high):
    at = 0
    for field, (_, deep, _) in zip(fields, sizes):
        depth, height = field.shape[:2]
        planes = field[depth - deep :] if high else field[:deep]
        out[at : at + deep * height] = planes.reshape((deep * height,) + planes.shape[2:])
        at += deep * height


def plane_kernel(sizes, *refs):
    fields, (handed, planes, corners) = refs[: len(sizes)], refs[len(sizes) :]
    spots, count, few = layout(sizes)
    planes[count:] = handed[:count]
    either(sends_high(), lambda high: put_boundary(planes, fields, sizes, high))

    def put(slot, high):
        for (shape, deep, tall), (plane_at, corner_at) in zip(sizes, spots):
            height = shape[1]
            first = height - tall if high else 0
            for part in range(2):
                for layer in range(deep):
                    source = part * count + plane_at + layer * height + first
                    target = part * few + corner_at + layer * tall
                    corners[slot, target : target + tall] = planes[source : source + tall]

    choose_side("narrow", corners, put)


def pass_kernel(sizes, halves, *refs):
    fields, (low, high, planes, corner_low, corner_high) = refs[: len(sizes)], refs[len(sizes) :][:5]
    passed, frames = refs[len(sizes) + 5], refs[len(sizes) + 6 :]
    spots, count, few = layout(sizes)
    start = count + sides_of("narrow") * few
    passed[:count] = planes[count:]
    passed[count : count + few] = corner_low[few:]
    passed[start - few : start] = corner_high[few:]
    passed[start:] = jnp.zeros((passed.shape[0] - start,) + passed.shape[1:], bf16)
    at = 0
    for own, ext, half, (shape, deep, tall), (plane_at, corner_at) in zip(
        fields, frames, halves, sizes, spots
    ):
        depth, height = shape[:2]
        fill_block(ext, own, low, high, at, deep, tall)
        at += depth * tall
        near = (
            rows_at(planes, plane_at, deep, height),
            rows_at(corner_low, corner_at, deep, tall),
            rows_at(corner_high, corner_at, deep, tall),
        )
        blank = tuple(jnp.zeros_like(part) for part in near)
        either(sends_high(), put_sides(ext, depth, deep, near, blank))
        clear_edges(ext, deep, tall)
        for plane in range(ext.shape[0]):
            put_column(passed, start, plane, inner_column(ext[plane], half))
        start += field_slabs(ext.shape, half)


def weight_kernel(weight, packed):
    outs = weight.shape[-1]
    for tap in range(9):
        for block in range(weight.shape[2] // outs):
            rows = slice(block * outs, (block + 1) * outs)
            spread_weights(packed, tap, 4 * outs * block, [weight[tap, c, rows] for c in range(3)])


def encode_kernel(
    own,
    low,
    high,
    planes,
    corner_low,
    corner_high,
    passed,
    packed,
    inner,
    bias,
    down,
    down_bias,
    encoded,
    coarse,
    ext,
    columns_in,
    frame,
    taps,
):
    lanes = ext.shape[-1]
    spot = (0, 0)
    fill_frame(ext, own, low, high, planes, corner_low, corner_high, passed, spot, 0, 1, 1)
    start = passed.shape[0] - field_slabs(ext.shape, True)
    fill_columns(
        columns_in,
        passed,
        start,
        frame,
        planes,
        corner_low,
        corner_high,
        spot,
        own.shape[1],
        1,
        1,
        True,
    )
    for plane in range(ext.shape[0]):
        before, after = pair_columns(columns_in[plane])
        spread_pairs(taps.at[plane], 0, ext[plane], before, after)
    depth, height, columns, _ = encoded.shape
    deep, tall = coarse.shape[:2]
    both = jnp.tile(bias[...], (1, 2))
    encoded[1 : depth - 1, 1 : height - 1] = inner[...]
    for where, block in conv_border(taps, packed, depth, height):
        encoded[where] = leaky_relu(block + both).astype(bf16)
    fine = encoded[...].reshape(deep, 2, tall, 2, columns, lanes)
    lifted = None
    for a in range(2):
        for b in range(2):
            part = jnp.dot(
                fine[:, a, :, b].reshape(-1, lanes), down[2 * a + b], preferred_element_type=f32
            )
            lifted = part if lifted is None else lifted + part
    coarse[...] = leaky_relu(lifted + down_bias[...]).astype(bf16).reshape(coarse.shape)


def bottom_kernel(
    sizes,
    coarse,
    encoded,
    low,
    high,
    planes,
    corner_low,
    corner_high,
    passed,
    weight,
    bias,
    up,
    up_bias,
    raised,
    encoded_ext,
    columns,
    encoded_columns,
    coarse_ext,
    columns_in,
    frame,
    encoded_frame,
    taps,
):
    lanes = coarse_ext.shape[-1]
    spots = layout(sizes)[0]
    at, start = 0, passed.shape[0]
    start -= field_slabs(coarse_ext.shape, False) + field_slabs(encoded_ext.shape, True)
    for ext, own, side, edge, half, spot, (shape, deep, tall) in zip(
        (coarse_ext, encoded_ext),
        (coarse, encoded),
        (columns_in, encoded_columns),
        (frame, encoded_frame),
        (False, True),
        spots,
        sizes,
    ):
        fill_frame(
            ext, own, low, high, planes, corner_low, corner_high, passed, spot, at, deep, tall
        )
        fill_columns(
            side,
            passed,
            start,
            edge,
            planes,
            corner_low,
            corner_high,
            spot,
            shape[1],
            deep,
            tall,
            half,
        )
        at += shape[0] * tall
        start += field_slabs(ext.shape, half)
    for plane in range(coarse_ext.shape[0]):
        before, after = pair_columns(columns_in[plane])
        block = coarse_ext[plane]
        wide = block.astype(f32)
        taps[plane, :, :, :lanes] = shifted(wide, before, 1).astype(bf16)
        taps[plane, :, :, lanes : 2 * lanes] = block
        taps[plane, :, :, 2 * lanes :] = shifted(wide, after, -1).astype(bf16)
    deep, _, tall, _, count, _ = raised.shape
    start, span = 0, tall
    if sides_of("narrow") == 1:
        start, span = jnp.where(lax.axis_index("narrow") == 0, 1, 0), tall - 1
    summed = conv_sum(
        taps, weight, 0, lambda a, b: [(slice(a, a + deep), pl.ds(b + start, span))]
    )
    bottom = leaky_relu(summed + bias[...]).astype(bf16)
    both = jnp.tile(up_bias[...], (1, 2))
    for a in range(2):
        for b in range(2):
            matrix = jnp.concatenate([up[2 * a + b, 0], up[2 * a + b, 1]], axis=-1)
            lifted = jnp.dot(bottom, matrix, preferred_element_type=f32) + both
            lifted = lifted.astype(bf16).reshape(deep, span, count, lanes)
            raised[:, a, pl.ds(start, span), b] = lifted
    blank_plane = jnp.zeros(raised.shape[1:], bf16)
    blank_row = jnp.zeros((deep, 2, 2, count, lanes), bf16)
    first, last = edges("narrow")

    @pl.when(first)
    def _():
        raised[:, :, 0] = blank_row

    @pl.when(last)
    def _():
        raised[:, :, tall - 1] = blank_row

    first, last = edges("wide")

    @pl.when(first)
    def _():
        raised[0] = blank_plane

    @pl.when(last)
    def _():
        raised[deep - 1] = blank_plane

    planes, height = encoded_ext.shape[:2]
    for plane in range(planes):
        z, a = (plane + 1) // 2, (plane + 1) % 2
        whole = raised[z, a].reshape(2 * tall, count, lanes)[1 : 1 + height]
        columns[plane] = inner_column(whole, True)


def border_kernel(encoded_ext, columns_in, packed, inner, sums, taps):
    lanes = taps.shape[-1]
    for plane in range(encoded_ext.shape[0]):
        low, high = pair_columns(columns_in[plane])
        spread_pairs(taps.at[plane], 0, encoded_ext[plane], low, high)
    depth, height = sums.shape[:2]
    sums[1 : depth - 1, 1 : height - 1] = inner[...]
    for where, block in conv_border(taps, packed, depth, height, packed.shape[1] - lanes):
        sums[where] = block


def decode_kernel(raised, columns_in, packed, partial, bias, decoded, taps, spread):
    planes, height, columns, _ = taps.shape
    for plane in range(planes):
        low, high = pair_columns(columns_in[plane])
        spread_pairs(taps.at[plane], 0, raised[plane + 1, 1 : 1 + height], low, high)
    depth, rows, _, outs = decoded.shape
    summed = conv_rows(taps, packed, depth, rows).reshape(partial.shape) + partial[...]
    summed = leaky_relu(summed + jnp.tile(bias[...], (1, 2)))
    for odd in range(2):
        half = summed[:, :, :, odd * outs : (odd + 1) * outs]
        spread[:, :, pl.ds(odd, columns, stride=2), :] = half
    decoded[...] = spread[...].astype(bf16)


def exchange(turn, fields, halos, halves, weight, bias):
    sizes = [(field.shape, deep, tall) for field, (deep, tall) in zip(fields, halos)]
    _, planes, corners = layout(sizes)
    depth, height = fields[-1].shape[:2]
    cells = fields[-1].shape[2:]
    sides = sides_of("narrow")
    swap = [(0, 1), (1, 0)]
    rows = sum(shape[0] * tall for shape, _, tall in sizes)
    edge_rows, handed = call(
        functools.partial(edge_kernel, sizes), [(sides, rows) + cells, (planes + field_slabs(fields[-1].shape, True),) + cells], (), 8
    )(*fields)
    handed = lax.ppermute(handed, "pair", swap)
    low, high = line_exchange("narrow", edge_rows)
    ring, corner = call(
        functools.partial(plane_kernel, sizes),
        [(2 * planes,) + cells, (sides, 2 * corners) + cells],
        (),
        8,
    )(*fields, handed)
    ring = ring_exchange(ring)
    corner_low, corner_high = corner_exchange(corner)
    outs = weight.shape[-1]
    (weights,) = call(weight_kernel, [(9, 4 * weight.shape[2], 2 * outs)], (), 8)(weight)
    lanes = 2 * cells[1]
    (inner,) = call(
        functools.partial(inner_kernel, weights.shape[1] - lanes, turn == 0),
        [(depth - 2, height - 2) + cells],
        [pltpu.VMEM((depth, height, cells[0], lanes), bf16)],
        dtype=bf16 if turn == 0 else f32,
    )(fields[-1], handed, weights, bias)
    received = (low, high, ring, corner_low, corner_high)
    frames = [
        (shape[0] + 2 * deep, shape[1] + 2 * tall) + cells for shape, deep, tall in sizes
    ]
    tail = sum(field_slabs(frame, half) for frame, half in zip(frames, halves))
    (passed,) = call(
        functools.partial(pass_kernel, sizes, halves),
        [(planes + sides * corners + tail,) + cells],
        [pltpu.VMEM(frame, bf16) for frame in frames],
        8,
    )(*fields, *received)
    passed = lax.ppermute(passed, "pair", swap)
    return sizes, weights, inner, received + (passed,)


def body(
    volume, w_encode, b_encode, w_down, b_down, w_bottom, b_bottom, w_up, b_up, w_decode, b_decode
):
    depth, height, width, skip = volume.shape
    deep_width = w_down.shape[4]
    half_depth, half_height, pairs = depth // 2, height // 2, width // 2
    lanes = 2 * skip
    framed = (depth + 2, height + 2)
    coarse_framed = (half_depth + 4, half_height + 4)

    (packed,) = call(
        pack_kernel,
        [(depth, height, pairs, lanes)],
        [
            pltpu.VMEM((depth, height, width, skip), bf16),
            pltpu.VMEM((depth, height, width, skip), f32),
            pltpu.SemaphoreType.DMA((depth,)),
        ],
        8,
        in_specs=[pl.BlockSpec(memory_space=pltpu.HBM)],
    )(pltpu.with_memory_space_constraint(volume, pltpu.HBM))
    encode_bias, decode_bias = b_encode.reshape(1, skip), b_decode.reshape(1, skip)
    _, encode_weights, inner, received = exchange(
        0, [packed], [(1, 1)], [True], w_encode.reshape(9, 3, skip, skip), encode_bias
    )
    encoded, coarse = call(
        encode_kernel,
        [(depth, height, pairs, lanes), (half_depth, half_height, pairs, deep_width)],
        [
            pltpu.VMEM(framed + (pairs, lanes), bf16),
            pltpu.VMEM(framed + (skip,), bf16),
            pltpu.VMEM((1, height + 2, pairs, lanes), bf16),
            pltpu.VMEM(framed + (pairs, 2 * lanes), bf16),
        ],
    )(
        packed,
        *received,
        encode_weights,
        inner,
        encode_bias,
        w_down.reshape(4, lanes, deep_width),
        b_down.reshape(1, deep_width),
    )

    sizes, decode_weights, inner, received = exchange(
        1,
        [coarse, encoded],
        [(2, 2), (1, 1)],
        [False, True],
        w_decode.reshape(9, 3, lanes, skip),
        decode_bias,
    )
    raised, encoded_ext, columns, encoded_columns = call(
        functools.partial(bottom_kernel, sizes),
        [
            (half_depth + 2, 2, half_height + 2, 2, pairs, lanes),
            framed + (pairs, lanes),
            framed + (skip,),
            framed + (skip,),
        ],
        [
            pltpu.VMEM(coarse_framed + (pairs, deep_width), bf16),
            pltpu.VMEM(coarse_framed + (deep_width,), bf16),
            pltpu.VMEM((2, half_height + 4, pairs, deep_width), bf16),
            pltpu.VMEM((1, height + 2, pairs, lanes), bf16),
            pltpu.VMEM(coarse_framed + (pairs, 3 * deep_width), bf16),
        ],
    )(
        coarse,
        encoded,
        *received,
        w_bottom.reshape(9, 3 * deep_width, deep_width),
        b_bottom.reshape(1, deep_width),
        w_up.reshape(4, 2, deep_width, skip),
        b_up.reshape(1, skip),
    )
    taps = pltpu.VMEM(framed + (pairs, 2 * lanes), bf16)
    columns = lax.ppermute(columns, "pair", [(0, 1), (1, 0)])
    (partial,) = call(
        border_kernel, [(depth, height, pairs, lanes)], [taps], dtype=f32
    )(encoded_ext, encoded_columns, decode_weights, inner)

    (decoded,) = call(
        decode_kernel,
        [(depth, height, width, skip)],
        [taps, pltpu.VMEM((depth, height, width, skip), f32)],
    )(
        raised.reshape(depth + 4, height + 4, pairs, lanes),
        columns,
        decode_weights,
        partial,
        decode_bias,
    )
    return decoded


def solution(mesh):
    return jax.shard_map(
        body,
        mesh=mesh,
        in_specs=(
            P(("groups", "wide"), "narrow", "pair", None),
            P(),
            P(),
            P(),
            P(),
            P(),
            P(),
            P(),
            P(),
            P(),
            P(),
        ),
        out_specs=P(("groups", "wide"), "narrow", "pair", None),
        check_vma=False,
    )
```

```python
import functools

import jax
import jax.numpy as jnp
from jax import lax
from jax.experimental import pallas as pl
from jax.experimental.pallas import tpu as pltpu
from jax.sharding import PartitionSpec as P


leak_slope = 0.01
f32 = jnp.float32
bf16 = jnp.bfloat16


def leaky_relu(values):
    return jnp.maximum(values, leak_slope * values)


def sides_of(axis):
    return 1 if lax.axis_size(axis) == 2 else 2


def line_exchange(axis, sent):
    count = lax.axis_size(axis)
    if count == 2:
        got = lax.ppermute(sent[0], axis, [(0, 1), (1, 0)])
        return got, got
    up = [(i, i + 1) for i in range(count - 1)]
    down = [(b, a) for a, b in up]
    return lax.ppermute(sent[1], axis, up), lax.ppermute(sent[0], axis, down)


def snake_pairs(groups, count, step):
    order = [
        group * count + (place if group % 2 == 0 else count - 1 - place)
        for group in range(groups)
        for place in range(count)
    ]
    total = len(order)
    return [(order[i], order[(i + step) % total]) for i in range(total)]


def ring_exchange(sent):
    groups, count = lax.axis_size("groups"), lax.axis_size("wide")
    pairs = [
        (2 * a + core, 2 * b + core)
        for core, step in ((0, 1), (1, -1))
        for a, b in snake_pairs(groups, count, step)
    ]
    return lax.ppermute(sent, ("groups", "wide", "pair"), pairs)


def corner_exchange(sent):
    groups, count, tall = (lax.axis_size(axis) for axis in ("groups", "wide", "narrow"))
    moves = [(0, 1), (1, 0)] if tall == 2 else [(i, i + 1) for i in range(tall - 1)]

    def move(array, rows):
        pairs = [
            ((a * tall + c) * 2 + core, (b * tall + d) * 2 + core)
            for core, step in ((0, 1), (1, -1))
            for a, b in snake_pairs(groups, count, step)
            for c, d in rows
        ]
        return lax.ppermute(array, ("groups", "wide", "narrow", "pair"), pairs)

    if tall == 2:
        got = move(sent[0], moves)
        return got, got
    return move(sent[1], moves), move(sent[0], [(d, c) for c, d in moves])


def call(kernel, outs, scratch=(), megabytes=24, dtype=bf16, **specs):
    return pl.pallas_call(
        kernel,
        **specs,
        out_shape=[jax.ShapeDtypeStruct(shape, dtype) for shape in outs],
        scratch_shapes=list(scratch),
        cost_estimate=pl.CostEstimate(flops=4 * 10**9, transcendentals=0, bytes_accessed=10**6),
        compiler_params=pltpu.CompilerParams(vmem_limit_bytes=megabytes << 20),
    )


def edges(axis):
    place = lax.axis_index(axis)
    return place == 0, place == lax.axis_size(axis) - 1


def sends_high():
    even = lax.axis_index("groups") % 2 == 0
    return (lax.axis_index("pair") == 0) == even


def either(condition, put):
    @pl.when(condition)
    def _():
        put(True)

    @pl.when(jnp.logical_not(condition))
    def _():
        put(False)


def rows_at(ref, at, *lead):
    count = 1
    for size in lead:
        count *= size
    return ref[at : at + count].reshape(lead + tuple(ref.shape[1:]))


def layout(fields):
    planes, corners, spots = 0, 0, []
    for shape, deep, tall in fields:
        spots.append((planes, corners))
        planes += deep * shape[1]
        corners += deep * tall
    return spots, planes, corners


def fill_planes(ext, base, middle, low, high):
    deep, height = middle.shape[:2]
    tall = low.shape[1]
    ext[base : base + deep, :tall] = low
    ext[base : base + deep, tall : tall + height] = middle
    ext[base : base + deep, tall + height :] = high


def fill_block(ext, own, low, high, at, deep, tall):
    depth = own.shape[0]
    fill_planes(
        ext,
        deep,
        own[...],
        rows_at(low, at, depth, tall),
        rows_at(high, at, depth, tall),
    )


def clear_edges(ext, deep, tall):
    first, last = edges("narrow")
    planes, rows = ext.shape[:2]
    blank_rows = jnp.zeros((planes, tall) + ext.shape[2:], bf16)
    blank_planes = jnp.zeros((deep,) + ext.shape[1:], bf16)

    @pl.when(first)
    def _():
        ext[:, :tall] = blank_rows

    @pl.when(last)
    def _():
        ext[:, rows - tall :] = blank_rows

    first, last = edges("wide")

    @pl.when(first)
    def _():
        ext[:deep] = blank_planes

    @pl.when(last)
    def _():
        ext[planes - deep :] = blank_planes


def fill_frame(ext, own, low, high, planes, corner_low, corner_high, passed, spot, at, deep, tall):
    depth, height = own.shape[:2]
    plane_at, corner_at = spot
    count = corner_low.shape[0] // 2
    split = planes.shape[0] // 2
    fill_block(ext, own, low, high, at, deep, tall)
    near = (
        rows_at(planes, plane_at, deep, height),
        rows_at(corner_low, corner_at, deep, tall),
        rows_at(corner_high, corner_at, deep, tall),
    )
    last = split + (sides_of("narrow") - 1) * count
    far = (
        rows_at(passed, plane_at, deep, height),
        rows_at(passed, split + corner_at, deep, tall),
        rows_at(passed, last + corner_at, deep, tall),
    )

    either(sends_high(), put_sides(ext, depth, deep, near, far))
    clear_edges(ext, deep, tall)


def put_sides(ext, depth, deep, near, far):
    def put(low_is_near):
        fill_planes(ext, 0, *(near if low_is_near else far))
        fill_planes(ext, deep + depth, *(far if low_is_near else near))

    return put


def fill_columns(
    columns, passed, start, frame, planes, corner_low, corner_high, spot, height, deep, tall, half
):
    plane_at, corner_at = spot
    count, corners = planes.shape[0] // 2, corner_low.shape[0] // 2
    total, rows, lanes = columns.shape
    for plane in range(total):
        columns[plane] = passed[column_place(passed, start, plane, rows, lanes)]
    fill_planes(
        frame,
        0,
        rows_at(planes, count + plane_at, deep, height),
        rows_at(corner_low, corners + corner_at, deep, tall),
        rows_at(corner_high, corners + corner_at, deep, tall),
    )
    first, last = edges("narrow")
    blank = jnp.zeros((deep, tall) + frame.shape[2:], bf16)

    @pl.when(first)
    def _():
        frame[:, :tall] = blank

    @pl.when(last)
    def _():
        frame[:, tall + height :] = blank

    at_low = lax.axis_index("pair") == 0
    at_edge = edges("wide")

    def put(low_side):
        edge = at_edge[0] if low_side else at_edge[1]
        for layer in range(deep):
            low, high = column_values(frame[layer], half)
            chosen = jnp.where(at_low, low, high)
            chosen = jnp.where(edge, jnp.zeros_like(chosen), chosen)
            columns[layer if low_side else total - deep + layer] = chosen

    either(sends_high(), put)


def inner_column(block, half):
    low, high = column_values(block, half)
    return jnp.where(lax.axis_index("pair") == 0, high, low)


def column_values(block, half):
    lanes = block.shape[-1]
    wide = block.astype(f32)
    if half:
        return wide[:, 0, : lanes // 2].astype(bf16), wide[:, -1, lanes // 2 :].astype(bf16)
    return wide[:, 0, :].astype(bf16), wide[:, -1, :].astype(bf16)


def shifted(values, column, step):
    columns = values.shape[1]
    spot = lax.broadcasted_iota(jnp.int32, values.shape, 1)
    if step > 0:
        return jnp.where(spot == 0, column[:, None, :], pltpu.roll(values, 1, 1))
    return jnp.where(
        spot == columns - 1, column[:, None, :], pltpu.roll(values, columns - 1, 1)
    )


def pair_columns(column):
    first, last = edges("pair")
    column = column.astype(f32)
    blank = jnp.zeros_like(column)
    return jnp.where(first, blank, column), jnp.where(last, blank, column)


def spread_pairs(taps, base, block, low, high):
    lanes = block.shape[-1] // 2
    wide = block.astype(f32)
    taps[:, :, base : base + lanes] = shifted(wide[:, :, lanes:], low, 1).astype(bf16)
    taps[:, :, base + lanes : base + 3 * lanes] = block
    taps[:, :, base + 3 * lanes : base + 4 * lanes] = shifted(
        wide[:, :, :lanes], high, -1
    ).astype(bf16)


def spread_weights(packed, tap, base, taken):
    rows, outs = taken[0].shape
    blank = jnp.zeros((rows, outs), bf16)
    for cell in range(4):
        at = base + cell * rows
        packed[tap, at : at + rows, :outs] = taken[cell] if cell < 3 else blank
        packed[tap, at : at + rows, outs:] = taken[cell - 1] if cell > 0 else blank


def conv_sum(taps, packed, base, select):
    lanes = taps.shape[-1]
    summed = None
    for a in range(3):
        for b in range(3):
            rows = [taps[part].reshape(-1, lanes) for part in select(a, b)]
            rows = rows[0] if len(rows) == 1 else jnp.concatenate(rows, axis=0)
            part = jnp.dot(
                rows, packed[3 * a + b, base : base + lanes], preferred_element_type=f32
            )
            summed = part if summed is None else summed + part
    return summed


def conv_rows(taps, packed, depth, height, base=0):
    return conv_sum(
        taps, packed, base, lambda a, b: [(slice(a, a + depth), slice(b, b + height))]
    )


def conv_border(taps, packed, depth, height, base=0):
    def select(a, b):
        planes = slice(a + 1, a + depth - 1)
        rows = slice(b, b + height)
        return [(a, rows), (a + depth - 1, rows), (planes, b), (planes, b + height - 1)]

    summed = conv_sum(taps, packed, base, select)
    columns, lanes = taps.shape[2], summed.shape[-1]
    inner = slice(1, depth - 1)
    at = 0
    pieces = []
    for where, count in (
        ((0,), height),
        ((depth - 1,), height),
        ((inner, 0), depth - 2),
        ((inner, height - 1), depth - 2),
    ):
        block = summed[at : at + count * columns].reshape(count, columns, lanes)
        pieces.append((where, block))
        at += count * columns
    return pieces


def inner_kernel(base, final, field, handed, packed, bias, out, taps):
    depth, height, _, lanes = field.shape
    start = handed.shape[0] - field_slabs(field.shape, True)
    for plane in range(depth):
        before, after = pair_columns(
            handed[column_place(handed, start, plane, height, lanes // 2)]
        )
        spread_pairs(taps.at[plane], 0, field[plane], before, after)
    summed = conv_rows(taps, packed, depth - 2, height - 2, base)
    if final:
        summed = leaky_relu(summed + jnp.tile(bias[...], (1, 2))).astype(bf16)
    out[...] = summed.reshape(out.shape)


def choose_side(axis, sent, put):
    if sent.shape[0] == 1:
        at_low = lax.axis_index(axis) == 0

        @pl.when(at_low)
        def _():
            put(0, True)

        @pl.when(jnp.logical_not(at_low))
        def _():
            put(0, False)

    else:
        put(0, False)
        put(1, True)


def pack_pairs(out, cells, spread):
    pairs, lanes = out.shape[1], cells.shape[-1]
    spread[...] = cells.astype(f32)
    for odd in range(2):
        half = spread[:, pl.ds(odd, pairs, stride=2), :]
        out[:, :, odd * lanes : (odd + 1) * lanes] = half.astype(bf16)


def pack_kernel(volume, packed, here, spread, arrived):
    copies = [
        pltpu.make_async_copy(volume.at[plane], here.at[plane], arrived.at[plane])
        for plane in range(volume.shape[0])
    ]
    for copy in copies:
        copy.start()
    for plane, copy in enumerate(copies):
        copy.wait()
        pack_pairs(packed.at[plane], here[plane], spread.at[plane])


def per_tile(cells, rows, lanes):
    return max(cells[0] // (-(-rows // 8) * 8), 1), cells[1] // lanes


def slabs(cells, planes, rows, lanes):
    down, across = per_tile(cells, rows, lanes)
    return -(-planes // (down * across))


def column_place(ref, start, plane, rows, lanes):
    down, across = per_tile(ref.shape[1:], rows, lanes)
    slab, spot = divmod(plane, down * across)
    row, lane = spot // across * (-(-rows // 8) * 8), spot % across * lanes
    return start + slab, slice(row, row + rows), slice(lane, lane + lanes)


def put_column(ref, start, plane, column):
    place = column_place(ref, start, plane, *column.shape)
    ref[place] = column


def field_slabs(shape, half):
    return slabs(shape[2:], shape[0], shape[1], shape[3] // 2 if half else shape[3])


def edge_kernel(sizes, *refs):
    fields, (edge_rows, handed) = refs[: len(sizes)], refs[len(sizes) :]

    def put_rows(slot, high):
        at = 0
        for field, (_, _, tall) in zip(fields, sizes):
            depth, height = field.shape[:2]
            first = height - tall if high else 0
            rows = field[:, first : first + tall]
            edge_rows[slot, at : at + depth * tall] = rows.reshape((depth * tall,) + rows.shape[2:])
            at += depth * tall

    choose_side("narrow", edge_rows, put_rows)
    either(sends_high(), lambda high: put_boundary(handed, fields, sizes, not high))
    field, start = fields[-1], layout(sizes)[1]
    handed[start:] = jnp.zeros((handed.shape[0] - start,) + handed.shape[1:], bf16)
    for plane in range(field.shape[0]):
        put_column(handed, start, plane, inner_column(field[plane], True))


def put_boundary(out, fields, sizes, high):
    at = 0
    for field, (_, deep, _) in zip(fields, sizes):
        depth, height = field.shape[:2]
        planes = field[depth - deep :] if high else field[:deep]
        out[at : at + deep * height] = planes.reshape((deep * height,) + planes.shape[2:])
        at += deep * height


def plane_kernel(sizes, *refs):
    fields, (handed, planes, corners) = refs[: len(sizes)], refs[len(sizes) :]
    spots, count, few = layout(sizes)
    planes[count:] = handed[:count]
    either(sends_high(), lambda high: put_boundary(planes, fields, sizes, high))

    def put(slot, high):
        for (shape, deep, tall), (plane_at, corner_at) in zip(sizes, spots):
            height = shape[1]
            first = height - tall if high else 0
            for part in range(2):
                for layer in range(deep):
                    source = part * count + plane_at + layer * height + first
                    target = part * few + corner_at + layer * tall
                    corners[slot, target : target + tall] = planes[source : source + tall]

    choose_side("narrow", corners, put)


def pass_kernel(sizes, halves, *refs):
    fields, (low, high, planes, corner_low, corner_high) = refs[: len(sizes)], refs[len(sizes) :][:5]
    passed, frames = refs[len(sizes) + 5], refs[len(sizes) + 6 :]
    spots, count, few = layout(sizes)
    start = count + sides_of("narrow") * few
    passed[:count] = planes[count:]
    passed[count : count + few] = corner_low[few:]
    passed[start - few : start] = corner_high[few:]
    passed[start:] = jnp.zeros((passed.shape[0] - start,) + passed.shape[1:], bf16)
    at = 0
    for own, ext, half, (shape, deep, tall), (plane_at, corner_at) in zip(
        fields, frames, halves, sizes, spots
    ):
        depth, height = shape[:2]
        fill_block(ext, own, low, high, at, deep, tall)
        at += depth * tall
        near = (
            rows_at(planes, plane_at, deep, height),
            rows_at(corner_low, corner_at, deep, tall),
            rows_at(corner_high, corner_at, deep, tall),
        )
        blank = tuple(jnp.zeros_like(part) for part in near)
        either(sends_high(), put_sides(ext, depth, deep, near, blank))
        clear_edges(ext, deep, tall)
        for plane in range(ext.shape[0]):
            put_column(passed, start, plane, inner_column(ext[plane], half))
        start += field_slabs(ext.shape, half)


def weight_kernel(weight, packed):
    outs = weight.shape[-1]
    for tap in range(9):
        for block in range(weight.shape[2] // outs):
            rows = slice(block * outs, (block + 1) * outs)
            spread_weights(packed, tap, 4 * outs * block, [weight[tap, c, rows] for c in range(3)])


def encode_kernel(
    own,
    low,
    high,
    planes,
    corner_low,
    corner_high,
    passed,
    packed,
    inner,
    bias,
    down,
    down_bias,
    encoded,
    coarse,
    ext,
    columns_in,
    frame,
    taps,
):
    lanes = ext.shape[-1]
    spot = (0, 0)
    fill_frame(ext, own, low, high, planes, corner_low, corner_high, passed, spot, 0, 1, 1)
    start = passed.shape[0] - field_slabs(ext.shape, True)
    fill_columns(
        columns_in,
        passed,
        start,
        frame,
        planes,
        corner_low,
        corner_high,
        spot,
        own.shape[1],
        1,
        1,
        True,
    )
    for plane in range(ext.shape[0]):
        before, after = pair_columns(columns_in[plane])
        spread_pairs(taps.at[plane], 0, ext[plane], before, after)
    depth, height, columns, _ = encoded.shape
    deep, tall = coarse.shape[:2]
    both = jnp.tile(bias[...], (1, 2))
    encoded[1 : depth - 1, 1 : height - 1] = inner[...]
    for where, block in conv_border(taps, packed, depth, height):
        encoded[where] = leaky_relu(block + both).astype(bf16)
    fine = encoded[...].reshape(deep, 2, tall, 2, columns, lanes)
    lifted = None
    for a in range(2):
        for b in range(2):
            part = jnp.dot(
                fine[:, a, :, b].reshape(-1, lanes), down[2 * a + b], preferred_element_type=f32
            )
            lifted = part if lifted is None else lifted + part
    coarse[...] = leaky_relu(lifted + down_bias[...]).astype(bf16).reshape(coarse.shape)


def bottom_kernel(
    sizes,
    coarse,
    encoded,
    low,
    high,
    planes,
    corner_low,
    corner_high,
    passed,
    weight,
    bias,
    up,
    up_bias,
    raised,
    encoded_ext,
    columns,
    encoded_columns,
    coarse_ext,
    columns_in,
    frame,
    encoded_frame,
    taps,
):
    lanes = coarse_ext.shape[-1]
    spots = layout(sizes)[0]
    at, start = 0, passed.shape[0]
    start -= field_slabs(coarse_ext.shape, False) + field_slabs(encoded_ext.shape, True)
    for ext, own, side, edge, half, spot, (shape, deep, tall) in zip(
        (coarse_ext, encoded_ext),
        (coarse, encoded),
        (columns_in, encoded_columns),
        (frame, encoded_frame),
        (False, True),
        spots,
        sizes,
    ):
        fill_frame(
            ext, own, low, high, planes, corner_low, corner_high, passed, spot, at, deep, tall
        )
        fill_columns(
            side,
            passed,
            start,
            edge,
            planes,
            corner_low,
            corner_high,
            spot,
            shape[1],
            deep,
            tall,
            half,
        )
        at += shape[0] * tall
        start += field_slabs(ext.shape, half)
    for plane in range(coarse_ext.shape[0]):
        before, after = pair_columns(columns_in[plane])
        block = coarse_ext[plane]
        wide = block.astype(f32)
        taps[plane, :, :, :lanes] = shifted(wide, before, 1).astype(bf16)
        taps[plane, :, :, lanes : 2 * lanes] = block
        taps[plane, :, :, 2 * lanes :] = shifted(wide, after, -1).astype(bf16)
    deep, _, tall, _, count, _ = raised.shape
    start, span = 0, tall
    if sides_of("narrow") == 1:
        start, span = jnp.where(lax.axis_index("narrow") == 0, 1, 0), tall - 1
    summed = conv_sum(
        taps, weight, 0, lambda a, b: [(slice(a, a + deep), pl.ds(b + start, span))]
    )
    bottom = leaky_relu(summed + bias[...]).astype(bf16)
    both = jnp.tile(up_bias[...], (1, 2))
    size = span * count
    for a in range(2):
        for b in range(2):
            matrix = jnp.concatenate([up[2 * a + b, 0], up[2 * a + b, 1]], axis=-1)
            used = bottom[size : deep * size] if a == 0 else bottom[: (deep - 1) * size]
            lifted = jnp.dot(used, matrix, preferred_element_type=f32) + both
            lifted = lifted.astype(bf16).reshape(deep - 1, span, count, lanes)
            raised[1 - a : deep - a, a, pl.ds(start, span), b] = lifted
    blank_plane = jnp.zeros(raised.shape[1:], bf16)
    blank_row = jnp.zeros((deep, 2, 2, count, lanes), bf16)
    first, last = edges("narrow")

    @pl.when(first)
    def _():
        raised[:, :, 0] = blank_row

    @pl.when(last)
    def _():
        raised[:, :, tall - 1] = blank_row

    first, last = edges("wide")

    @pl.when(first)
    def _():
        raised[0] = blank_plane

    @pl.when(last)
    def _():
        raised[deep - 1] = blank_plane

    planes, height = encoded_ext.shape[:2]
    for plane in range(planes):
        z, a = (plane + 1) // 2, (plane + 1) % 2
        whole = raised[z, a].reshape(2 * tall, count, lanes)[1 : 1 + height]
        columns[plane] = inner_column(whole, True)


def border_kernel(encoded_ext, columns_in, packed, inner, sums, taps):
    lanes = taps.shape[-1]
    for plane in range(encoded_ext.shape[0]):
        low, high = pair_columns(columns_in[plane])
        spread_pairs(taps.at[plane], 0, encoded_ext[plane], low, high)
    depth, height = sums.shape[:2]
    sums[1 : depth - 1, 1 : height - 1] = inner[...]
    for where, block in conv_border(taps, packed, depth, height, packed.shape[1] - lanes):
        sums[where] = block


def decode_kernel(raised, columns_in, packed, partial, bias, decoded, taps, spread):
    planes, height, columns, _ = taps.shape
    for plane in range(planes):
        low, high = pair_columns(columns_in[plane])
        spread_pairs(taps.at[plane], 0, raised[plane + 1, 1 : 1 + height], low, high)
    depth, rows, _, outs = decoded.shape
    summed = conv_rows(taps, packed, depth, rows).reshape(partial.shape) + partial[...]
    summed = leaky_relu(summed + jnp.tile(bias[...], (1, 2)))
    for odd in range(2):
        half = summed[:, :, :, odd * outs : (odd + 1) * outs]
        spread[:, :, pl.ds(odd, columns, stride=2), :] = half
    decoded[...] = spread[...].astype(bf16)


def exchange(turn, fields, halos, halves, weight, bias):
    sizes = [(field.shape, deep, tall) for field, (deep, tall) in zip(fields, halos)]
    _, planes, corners = layout(sizes)
    depth, height = fields[-1].shape[:2]
    cells = fields[-1].shape[2:]
    sides = sides_of("narrow")
    swap = [(0, 1), (1, 0)]
    rows = sum(shape[0] * tall for shape, _, tall in sizes)
    edge_rows, handed = call(
        functools.partial(edge_kernel, sizes), [(sides, rows) + cells, (planes + field_slabs(fields[-1].shape, True),) + cells], (), 8
    )(*fields)
    handed = lax.ppermute(handed, "pair", swap)
    low, high = line_exchange("narrow", edge_rows)
    ring, corner = call(
        functools.partial(plane_kernel, sizes),
        [(2 * planes,) + cells, (sides, 2 * corners) + cells],
        (),
        8,
    )(*fields, handed)
    ring = ring_exchange(ring)
    corner_low, corner_high = corner_exchange(corner)
    outs = weight.shape[-1]
    (weights,) = call(weight_kernel, [(9, 4 * weight.shape[2], 2 * outs)], (), 8)(weight)
    lanes = 2 * cells[1]
    (inner,) = call(
        functools.partial(inner_kernel, weights.shape[1] - lanes, turn == 0),
        [(depth - 2, height - 2) + cells],
        [pltpu.VMEM((depth, height, cells[0], lanes), bf16)],
        dtype=bf16 if turn == 0 else f32,
    )(fields[-1], handed, weights, bias)
    received = (low, high, ring, corner_low, corner_high)
    frames = [
        (shape[0] + 2 * deep, shape[1] + 2 * tall) + cells for shape, deep, tall in sizes
    ]
    tail = sum(field_slabs(frame, half) for frame, half in zip(frames, halves))
    (passed,) = call(
        functools.partial(pass_kernel, sizes, halves),
        [(planes + sides * corners + tail,) + cells],
        [pltpu.VMEM(frame, bf16) for frame in frames],
        8,
    )(*fields, *received)
    passed = lax.ppermute(passed, "pair", swap)
    return sizes, weights, inner, received + (passed,)


def body(
    volume, w_encode, b_encode, w_down, b_down, w_bottom, b_bottom, w_up, b_up, w_decode, b_decode
):
    depth, height, width, skip = volume.shape
    deep_width = w_down.shape[4]
    half_depth, half_height, pairs = depth // 2, height // 2, width // 2
    lanes = 2 * skip
    framed = (depth + 2, height + 2)
    coarse_framed = (half_depth + 4, half_height + 4)

    (packed,) = call(
        pack_kernel,
        [(depth, height, pairs, lanes)],
        [
            pltpu.VMEM((depth, height, width, skip), bf16),
            pltpu.VMEM((depth, height, width, skip), f32),
            pltpu.SemaphoreType.DMA((depth,)),
        ],
        8,
        in_specs=[pl.BlockSpec(memory_space=pltpu.HBM)],
    )(pltpu.with_memory_space_constraint(volume, pltpu.HBM))
    encode_bias, decode_bias = b_encode.reshape(1, skip), b_decode.reshape(1, skip)
    _, encode_weights, inner, received = exchange(
        0, [packed], [(1, 1)], [True], w_encode.reshape(9, 3, skip, skip), encode_bias
    )
    encoded, coarse = call(
        encode_kernel,
        [(depth, height, pairs, lanes), (half_depth, half_height, pairs, deep_width)],
        [
            pltpu.VMEM(framed + (pairs, lanes), bf16),
            pltpu.VMEM(framed + (skip,), bf16),
            pltpu.VMEM((1, height + 2, pairs, lanes), bf16),
            pltpu.VMEM(framed + (pairs, 2 * lanes), bf16),
        ],
    )(
        packed,
        *received,
        encode_weights,
        inner,
        encode_bias,
        w_down.reshape(4, lanes, deep_width),
        b_down.reshape(1, deep_width),
    )

    sizes, decode_weights, inner, received = exchange(
        1,
        [coarse, encoded],
        [(2, 2), (1, 1)],
        [False, True],
        w_decode.reshape(9, 3, lanes, skip),
        decode_bias,
    )
    raised, encoded_ext, columns, encoded_columns = call(
        functools.partial(bottom_kernel, sizes),
        [
            (half_depth + 2, 2, half_height + 2, 2, pairs, lanes),
            framed + (pairs, lanes),
            framed + (skip,),
            framed + (skip,),
        ],
        [
            pltpu.VMEM(coarse_framed + (pairs, deep_width), bf16),
            pltpu.VMEM(coarse_framed + (deep_width,), bf16),
            pltpu.VMEM((2, half_height + 4, pairs, deep_width), bf16),
            pltpu.VMEM((1, height + 2, pairs, lanes), bf16),
            pltpu.VMEM(coarse_framed + (pairs, 3 * deep_width), bf16),
        ],
    )(
        coarse,
        encoded,
        *received,
        w_bottom.reshape(9, 3 * deep_width, deep_width),
        b_bottom.reshape(1, deep_width),
        w_up.reshape(4, 2, deep_width, skip),
        b_up.reshape(1, skip),
    )
    taps = pltpu.VMEM(framed + (pairs, 2 * lanes), bf16)
    columns = lax.ppermute(columns, "pair", [(0, 1), (1, 0)])
    (partial,) = call(
        border_kernel, [(depth, height, pairs, lanes)], [taps], dtype=f32
    )(encoded_ext, encoded_columns, decode_weights, inner)

    (decoded,) = call(
        decode_kernel,
        [(depth, height, width, skip)],
        [taps, pltpu.VMEM((depth, height, width, skip), f32)],
    )(
        raised.reshape(depth + 4, height + 4, pairs, lanes),
        columns,
        decode_weights,
        partial,
        decode_bias,
    )
    return decoded


def solution(mesh):
    return jax.shard_map(
        body,
        mesh=mesh,
        in_specs=(
            P(("groups", "wide"), "narrow", "pair", None),
            P(),
            P(),
            P(),
            P(),
            P(),
            P(),
            P(),
            P(),
            P(),
            P(),
        ),
        out_specs=P(("groups", "wide"), "narrow", "pair", None),
        check_vma=False,
    )
```

```python
import functools

import jax
import jax.numpy as jnp
from jax import lax
from jax.experimental import pallas as pl
from jax.experimental.pallas import tpu as pltpu
from jax.sharding import PartitionSpec as P


leak_slope = 0.01
f32 = jnp.float32
bf16 = jnp.bfloat16


def leaky_relu(values):
    return jnp.maximum(values, leak_slope * values)


def sides_of(axis):
    return 1 if lax.axis_size(axis) == 2 else 2


def line_exchange(axis, sent):
    count = lax.axis_size(axis)
    if count == 2:
        got = lax.ppermute(sent[0], axis, [(0, 1), (1, 0)])
        return got, got
    up = [(i, i + 1) for i in range(count - 1)]
    down = [(b, a) for a, b in up]
    return lax.ppermute(sent[1], axis, up), lax.ppermute(sent[0], axis, down)


def snake_pairs(groups, count, step):
    order = [
        group * count + (place if group % 2 == 0 else count - 1 - place)
        for group in range(groups)
        for place in range(count)
    ]
    total = len(order)
    return [(order[i], order[(i + step) % total]) for i in range(total)]


def ring_exchange(sent):
    groups, count = lax.axis_size("groups"), lax.axis_size("wide")
    pairs = [
        (2 * a + core, 2 * b + core)
        for core, step in ((0, 1), (1, -1))
        for a, b in snake_pairs(groups, count, step)
    ]
    return lax.ppermute(sent, ("groups", "wide", "pair"), pairs)


def corner_exchange(sent):
    groups, count, tall = (lax.axis_size(axis) for axis in ("groups", "wide", "narrow"))
    moves = [(0, 1), (1, 0)] if tall == 2 else [(i, i + 1) for i in range(tall - 1)]

    def move(array, rows):
        pairs = [
            ((a * tall + c) * 2 + core, (b * tall + d) * 2 + core)
            for core, step in ((0, 1), (1, -1))
            for a, b in snake_pairs(groups, count, step)
            for c, d in rows
        ]
        return lax.ppermute(array, ("groups", "wide", "narrow", "pair"), pairs)

    if tall == 2:
        got = move(sent[0], moves)
        return got, got
    return move(sent[1], moves), move(sent[0], [(d, c) for c, d in moves])


def call(kernel, outs, scratch=(), megabytes=24, dtype=bf16, **specs):
    return pl.pallas_call(
        kernel,
        **specs,
        out_shape=[jax.ShapeDtypeStruct(shape, dtype) for shape in outs],
        scratch_shapes=list(scratch),
        cost_estimate=pl.CostEstimate(flops=4 * 10**9, transcendentals=0, bytes_accessed=10**6),
        compiler_params=pltpu.CompilerParams(vmem_limit_bytes=megabytes << 20),
    )


def edges(axis):
    place = lax.axis_index(axis)
    return place == 0, place == lax.axis_size(axis) - 1


def sends_high():
    even = lax.axis_index("groups") % 2 == 0
    return (lax.axis_index("pair") == 0) == even


def either(condition, put):
    @pl.when(condition)
    def _():
        put(True)

    @pl.when(jnp.logical_not(condition))
    def _():
        put(False)


def rows_at(ref, at, *lead):
    count = 1
    for size in lead:
        count *= size
    return ref[at : at + count].reshape(lead + tuple(ref.shape[1:]))


def layout(fields):
    planes, corners, spots = 0, 0, []
    for shape, deep, tall in fields:
        spots.append((planes, corners))
        planes += deep * shape[1]
        corners += deep * tall
    return spots, planes, corners


def fill_planes(ext, base, middle, low, high):
    deep, height = middle.shape[:2]
    tall = low.shape[1]
    ext[base : base + deep, :tall] = low
    ext[base : base + deep, tall : tall + height] = middle
    ext[base : base + deep, tall + height :] = high


def fill_block(ext, own, low, high, at, deep, tall):
    depth = own.shape[0]
    fill_planes(
        ext,
        deep,
        own[...],
        rows_at(low, at, depth, tall),
        rows_at(high, at, depth, tall),
    )


def clear_edges(ext, deep, tall):
    first, last = edges("narrow")
    planes, rows = ext.shape[:2]
    blank_rows = jnp.zeros((planes, tall) + ext.shape[2:], bf16)
    blank_planes = jnp.zeros((deep,) + ext.shape[1:], bf16)

    @pl.when(first)
    def _():
        ext[:, :tall] = blank_rows

    @pl.when(last)
    def _():
        ext[:, rows - tall :] = blank_rows

    first, last = edges("wide")

    @pl.when(first)
    def _():
        ext[:deep] = blank_planes

    @pl.when(last)
    def _():
        ext[planes - deep :] = blank_planes


def fill_frame(ext, own, low, high, planes, corner_low, corner_high, passed, spot, at, deep, tall):
    depth, height = own.shape[:2]
    plane_at, corner_at = spot
    count = corner_low.shape[0] // 2
    split = planes.shape[0] // 2
    fill_block(ext, own, low, high, at, deep, tall)
    near = (
        rows_at(planes, plane_at, deep, height),
        rows_at(corner_low, corner_at, deep, tall),
        rows_at(corner_high, corner_at, deep, tall),
    )
    last = split + (sides_of("narrow") - 1) * count
    far = (
        rows_at(passed, plane_at, deep, height),
        rows_at(passed, split + corner_at, deep, tall),
        rows_at(passed, last + corner_at, deep, tall),
    )

    either(sends_high(), put_sides(ext, depth, deep, near, far))
    clear_edges(ext, deep, tall)


def put_sides(ext, depth, deep, near, far):
    def put(low_is_near):
        fill_planes(ext, 0, *(near if low_is_near else far))
        fill_planes(ext, deep + depth, *(far if low_is_near else near))

    return put


def fill_columns(
    columns, passed, start, frame, planes, corner_low, corner_high, spot, height, deep, tall, half
):
    plane_at, corner_at = spot
    count, corners = planes.shape[0] // 2, corner_low.shape[0] // 2
    total, rows, lanes = columns.shape
    for plane in range(total):
        columns[plane] = passed[column_place(passed, start, plane, rows, lanes)]
    fill_planes(
        frame,
        0,
        rows_at(planes, count + plane_at, deep, height),
        rows_at(corner_low, corners + corner_at, deep, tall),
        rows_at(corner_high, corners + corner_at, deep, tall),
    )
    first, last = edges("narrow")
    blank = jnp.zeros((deep, tall) + frame.shape[2:], bf16)

    @pl.when(first)
    def _():
        frame[:, :tall] = blank

    @pl.when(last)
    def _():
        frame[:, tall + height :] = blank

    at_low = lax.axis_index("pair") == 0
    at_edge = edges("wide")

    def put(low_side):
        edge = at_edge[0] if low_side else at_edge[1]
        for layer in range(deep):
            low, high = column_values(frame[layer], half)
            chosen = jnp.where(at_low, low, high)
            chosen = jnp.where(edge, jnp.zeros_like(chosen), chosen)
            columns[layer if low_side else total - deep + layer] = chosen

    either(sends_high(), put)


def inner_column(block, half):
    low, high = column_values(block, half)
    return jnp.where(lax.axis_index("pair") == 0, high, low)


def column_values(block, half):
    lanes = block.shape[-1]
    wide = block.astype(f32)
    if half:
        return wide[:, 0, : lanes // 2].astype(bf16), wide[:, -1, lanes // 2 :].astype(bf16)
    return wide[:, 0, :].astype(bf16), wide[:, -1, :].astype(bf16)


def shifted(values, column, step):
    columns = values.shape[1]
    spot = lax.broadcasted_iota(jnp.int32, values.shape, 1)
    if step > 0:
        return jnp.where(spot == 0, column[:, None, :], pltpu.roll(values, 1, 1))
    return jnp.where(
        spot == columns - 1, column[:, None, :], pltpu.roll(values, columns - 1, 1)
    )


def pair_columns(column):
    first, last = edges("pair")
    column = column.astype(f32)
    blank = jnp.zeros_like(column)
    return jnp.where(first, blank, column), jnp.where(last, blank, column)


def spread_pairs(taps, base, block, low, high):
    lanes = block.shape[-1] // 2
    wide = block.astype(f32)
    taps[:, :, base : base + lanes] = shifted(wide[:, :, lanes:], low, 1).astype(bf16)
    taps[:, :, base + lanes : base + 3 * lanes] = block
    taps[:, :, base + 3 * lanes : base + 4 * lanes] = shifted(
        wide[:, :, :lanes], high, -1
    ).astype(bf16)


def spread_weights(packed, tap, base, taken):
    rows, outs = taken[0].shape
    blank = jnp.zeros((rows, outs), bf16)
    for cell in range(4):
        at = base + cell * rows
        packed[tap, at : at + rows, :outs] = taken[cell] if cell < 3 else blank
        packed[tap, at : at + rows, outs:] = taken[cell - 1] if cell > 0 else blank


def conv_sum(taps, packed, base, select):
    lanes = taps.shape[-1]
    summed = None
    for a in range(3):
        for b in range(3):
            rows = [taps[part].reshape(-1, lanes) for part in select(a, b)]
            rows = rows[0] if len(rows) == 1 else jnp.concatenate(rows, axis=0)
            part = jnp.dot(
                rows, packed[3 * a + b, base : base + lanes], preferred_element_type=f32
            )
            summed = part if summed is None else summed + part
    return summed


def conv_rows(taps, packed, depth, height, base=0):
    return conv_sum(
        taps, packed, base, lambda a, b: [(slice(a, a + depth), slice(b, b + height))]
    )


def conv_border(taps, packed, depth, height, base=0):
    def select(a, b):
        planes = slice(a + 1, a + depth - 1)
        rows = slice(b, b + height)
        return [(a, rows), (a + depth - 1, rows), (planes, b), (planes, b + height - 1)]

    summed = conv_sum(taps, packed, base, select)
    columns, lanes = taps.shape[2], summed.shape[-1]
    inner = slice(1, depth - 1)
    at = 0
    pieces = []
    for where, count in (
        ((0,), height),
        ((depth - 1,), height),
        ((inner, 0), depth - 2),
        ((inner, height - 1), depth - 2),
    ):
        block = summed[at : at + count * columns].reshape(count, columns, lanes)
        pieces.append((where, block))
        at += count * columns
    return pieces


def inner_kernel(base, final, field, handed, packed, bias, out, taps):
    depth, height, _, lanes = field.shape
    start = handed.shape[0] - field_slabs(field.shape, True)
    for plane in range(depth):
        before, after = pair_columns(
            handed[column_place(handed, start, plane, height, lanes // 2)]
        )
        spread_pairs(taps.at[plane], 0, field[plane], before, after)
    summed = conv_rows(taps, packed, depth - 2, height - 2, base)
    if final:
        summed = leaky_relu(summed + jnp.tile(bias[...], (1, 2))).astype(bf16)
    out[...] = summed.reshape(out.shape)


def choose_side(axis, sent, put):
    if sent.shape[0] == 1:
        at_low = lax.axis_index(axis) == 0

        @pl.when(at_low)
        def _():
            put(0, True)

        @pl.when(jnp.logical_not(at_low))
        def _():
            put(0, False)

    else:
        put(0, False)
        put(1, True)


def pack_pairs(out, cells, spread):
    pairs, lanes = out.shape[1], cells.shape[-1]
    spread[...] = cells.astype(f32)
    for odd in range(2):
        half = spread[:, pl.ds(odd, pairs, stride=2), :]
        out[:, :, odd * lanes : (odd + 1) * lanes] = half.astype(bf16)


def pack_kernel(sizes, volume, packed, edge_rows, handed, here, spread, arrived):
    copies = [
        pltpu.make_async_copy(volume.at[plane], here.at[plane], arrived.at[plane])
        for plane in range(volume.shape[0])
    ]
    for copy in copies:
        copy.start()
    for plane, copy in enumerate(copies):
        copy.wait()
        pack_pairs(packed.at[plane], here[plane], spread.at[plane])
    edge_kernel(sizes, packed, edge_rows, handed)


def per_tile(cells, rows, lanes):
    return max(cells[0] // (-(-rows // 8) * 8), 1), cells[1] // lanes


def slabs(cells, planes, rows, lanes):
    down, across = per_tile(cells, rows, lanes)
    return -(-planes // (down * across))


def column_place(ref, start, plane, rows, lanes):
    down, across = per_tile(ref.shape[1:], rows, lanes)
    slab, spot = divmod(plane, down * across)
    row, lane = spot // across * (-(-rows // 8) * 8), spot % across * lanes
    return start + slab, slice(row, row + rows), slice(lane, lane + lanes)


def put_column(ref, start, plane, column):
    place = column_place(ref, start, plane, *column.shape)
    ref[place] = column


def field_slabs(shape, half):
    return slabs(shape[2:], shape[0], shape[1], shape[3] // 2 if half else shape[3])


def edge_kernel(sizes, *refs):
    fields, (edge_rows, handed) = refs[: len(sizes)], refs[len(sizes) :]

    def put_rows(slot, high):
        at = 0
        for field, (_, _, tall) in zip(fields, sizes):
            depth, height = field.shape[:2]
            first = height - tall if high else 0
            rows = field[:, first : first + tall]
            edge_rows[slot, at : at + depth * tall] = rows.reshape((depth * tall,) + rows.shape[2:])
            at += depth * tall

    choose_side("narrow", edge_rows, put_rows)
    either(sends_high(), lambda high: put_boundary(handed, fields, sizes, not high))
    field, start = fields[-1], layout(sizes)[1]
    handed[start:] = jnp.zeros((handed.shape[0] - start,) + handed.shape[1:], bf16)
    for plane in range(field.shape[0]):
        put_column(handed, start, plane, inner_column(field[plane], True))


def put_boundary(out, fields, sizes, high):
    at = 0
    for field, (_, deep, _) in zip(fields, sizes):
        depth, height = field.shape[:2]
        planes = field[depth - deep :] if high else field[:deep]
        out[at : at + deep * height] = planes.reshape((deep * height,) + planes.shape[2:])
        at += deep * height


def plane_kernel(sizes, *refs):
    fields, (handed, planes, corners) = refs[: len(sizes)], refs[len(sizes) :]
    spots, count, few = layout(sizes)
    planes[count:] = handed[:count]
    either(sends_high(), lambda high: put_boundary(planes, fields, sizes, high))

    def put(slot, high):
        for (shape, deep, tall), (plane_at, corner_at) in zip(sizes, spots):
            height = shape[1]
            first = height - tall if high else 0
            for part in range(2):
                for layer in range(deep):
                    source = part * count + plane_at + layer * height + first
                    target = part * few + corner_at + layer * tall
                    corners[slot, target : target + tall] = planes[source : source + tall]

    choose_side("narrow", corners, put)


def pass_kernel(sizes, halves, *refs):
    fields, (low, high, planes, corner_low, corner_high) = refs[: len(sizes)], refs[len(sizes) :][:5]
    passed, frames = refs[len(sizes) + 5], refs[len(sizes) + 6 :]
    spots, count, few = layout(sizes)
    start = count + sides_of("narrow") * few
    passed[:count] = planes[count:]
    passed[count : count + few] = corner_low[few:]
    passed[start - few : start] = corner_high[few:]
    passed[start:] = jnp.zeros((passed.shape[0] - start,) + passed.shape[1:], bf16)
    at = 0
    for own, ext, half, (shape, deep, tall), (plane_at, corner_at) in zip(
        fields, frames, halves, sizes, spots
    ):
        depth, height = shape[:2]
        fill_block(ext, own, low, high, at, deep, tall)
        at += depth * tall
        near = (
            rows_at(planes, plane_at, deep, height),
            rows_at(corner_low, corner_at, deep, tall),
            rows_at(corner_high, corner_at, deep, tall),
        )
        blank = tuple(jnp.zeros_like(part) for part in near)
        either(sends_high(), put_sides(ext, depth, deep, near, blank))
        clear_edges(ext, deep, tall)
        for plane in range(ext.shape[0]):
            put_column(passed, start, plane, inner_column(ext[plane], half))
        start += field_slabs(ext.shape, half)


def weight_kernel(weight, packed):
    outs = weight.shape[-1]
    for tap in range(9):
        for block in range(weight.shape[2] // outs):
            rows = slice(block * outs, (block + 1) * outs)
            spread_weights(packed, tap, 4 * outs * block, [weight[tap, c, rows] for c in range(3)])


def encode_kernel(
    sizes,
    own,
    low,
    high,
    planes,
    corner_low,
    corner_high,
    passed,
    packed,
    inner,
    bias,
    down,
    down_bias,
    encoded,
    coarse,
    edge_rows,
    handed,
    ext,
    columns_in,
    frame,
    taps,
):
    lanes = ext.shape[-1]
    spot = (0, 0)
    fill_frame(ext, own, low, high, planes, corner_low, corner_high, passed, spot, 0, 1, 1)
    start = passed.shape[0] - field_slabs(ext.shape, True)
    fill_columns(
        columns_in,
        passed,
        start,
        frame,
        planes,
        corner_low,
        corner_high,
        spot,
        own.shape[1],
        1,
        1,
        True,
    )
    for plane in range(ext.shape[0]):
        before, after = pair_columns(columns_in[plane])
        spread_pairs(taps.at[plane], 0, ext[plane], before, after)
    depth, height, columns, _ = encoded.shape
    deep, tall = coarse.shape[:2]
    both = jnp.tile(bias[...], (1, 2))
    encoded[1 : depth - 1, 1 : height - 1] = inner[...]
    for where, block in conv_border(taps, packed, depth, height):
        encoded[where] = leaky_relu(block + both).astype(bf16)
    fine = encoded[...].reshape(deep, 2, tall, 2, columns, lanes)
    lifted = None
    for a in range(2):
        for b in range(2):
            part = jnp.dot(
                fine[:, a, :, b].reshape(-1, lanes), down[2 * a + b], preferred_element_type=f32
            )
            lifted = part if lifted is None else lifted + part
    coarse[...] = leaky_relu(lifted + down_bias[...]).astype(bf16).reshape(coarse.shape)
    edge_kernel(sizes, coarse, encoded, edge_rows, handed)


def bottom_kernel(
    sizes,
    coarse,
    encoded,
    low,
    high,
    planes,
    corner_low,
    corner_high,
    passed,
    weight,
    bias,
    up,
    up_bias,
    raised,
    encoded_ext,
    columns,
    encoded_columns,
    coarse_ext,
    columns_in,
    frame,
    encoded_frame,
    taps,
):
    lanes = coarse_ext.shape[-1]
    spots = layout(sizes)[0]
    at, start = 0, passed.shape[0]
    start -= field_slabs(coarse_ext.shape, False) + field_slabs(encoded_ext.shape, True)
    for ext, own, side, edge, half, spot, (shape, deep, tall) in zip(
        (coarse_ext, encoded_ext),
        (coarse, encoded),
        (columns_in, encoded_columns),
        (frame, encoded_frame),
        (False, True),
        spots,
        sizes,
    ):
        fill_frame(
            ext, own, low, high, planes, corner_low, corner_high, passed, spot, at, deep, tall
        )
        fill_columns(
            side,
            passed,
            start,
            edge,
            planes,
            corner_low,
            corner_high,
            spot,
            shape[1],
            deep,
            tall,
            half,
        )
        at += shape[0] * tall
        start += field_slabs(ext.shape, half)
    for plane in range(coarse_ext.shape[0]):
        before, after = pair_columns(columns_in[plane])
        block = coarse_ext[plane]
        wide = block.astype(f32)
        taps[plane, :, :, :lanes] = shifted(wide, before, 1).astype(bf16)
        taps[plane, :, :, lanes : 2 * lanes] = block
        taps[plane, :, :, 2 * lanes :] = shifted(wide, after, -1).astype(bf16)
    deep, _, tall, _, count, _ = raised.shape
    start, span = 0, tall
    if sides_of("narrow") == 1:
        start, span = jnp.where(lax.axis_index("narrow") == 0, 1, 0), tall - 1
    summed = conv_sum(
        taps, weight, 0, lambda a, b: [(slice(a, a + deep), pl.ds(b + start, span))]
    )
    bottom = leaky_relu(summed + bias[...]).astype(bf16)
    both = jnp.tile(up_bias[...], (1, 2))
    size = span * count
    for a in range(2):
        for b in range(2):
            matrix = jnp.concatenate([up[2 * a + b, 0], up[2 * a + b, 1]], axis=-1)
            used = bottom[size : deep * size] if a == 0 else bottom[: (deep - 1) * size]
            lifted = jnp.dot(used, matrix, preferred_element_type=f32) + both
            lifted = lifted.astype(bf16).reshape(deep - 1, span, count, lanes)
            raised[1 - a : deep - a, a, pl.ds(start, span), b] = lifted
    blank_plane = jnp.zeros(raised.shape[1:], bf16)
    blank_row = jnp.zeros((deep, 2, 2, count, lanes), bf16)
    first, last = edges("narrow")

    @pl.when(first)
    def _():
        raised[:, :, 0] = blank_row

    @pl.when(last)
    def _():
        raised[:, :, tall - 1] = blank_row

    first, last = edges("wide")

    @pl.when(first)
    def _():
        raised[0] = blank_plane

    @pl.when(last)
    def _():
        raised[deep - 1] = blank_plane

    planes, height = encoded_ext.shape[:2]
    for plane in range(planes):
        z, a = (plane + 1) // 2, (plane + 1) % 2
        whole = raised[z, a].reshape(2 * tall, count, lanes)[1 : 1 + height]
        columns[plane] = inner_column(whole, True)


def border_kernel(encoded_ext, columns_in, packed, inner, sums, taps):
    lanes = taps.shape[-1]
    for plane in range(encoded_ext.shape[0]):
        low, high = pair_columns(columns_in[plane])
        spread_pairs(taps.at[plane], 0, encoded_ext[plane], low, high)
    depth, height = sums.shape[:2]
    sums[1 : depth - 1, 1 : height - 1] = inner[...]
    for where, block in conv_border(taps, packed, depth, height, packed.shape[1] - lanes):
        sums[where] = block


def decode_kernel(raised, columns_in, packed, partial, bias, decoded, taps, spread):
    planes, height, columns, _ = taps.shape
    for plane in range(planes):
        low, high = pair_columns(columns_in[plane])
        spread_pairs(taps.at[plane], 0, raised[plane + 1, 1 : 1 + height], low, high)
    depth, rows, _, outs = decoded.shape
    summed = conv_rows(taps, packed, depth, rows).reshape(partial.shape) + partial[...]
    summed = leaky_relu(summed + jnp.tile(bias[...], (1, 2)))
    for odd in range(2):
        half = summed[:, :, :, odd * outs : (odd + 1) * outs]
        spread[:, :, pl.ds(odd, columns, stride=2), :] = half
    decoded[...] = spread[...].astype(bf16)


def sizes_of(shapes, halos):
    return [(shape, deep, tall) for shape, (deep, tall) in zip(shapes, halos)]


def edge_shapes(sizes):
    last = sizes[-1][0]
    rows = sum(shape[0] * tall for shape, _, tall in sizes)
    planes = layout(sizes)[1] + field_slabs(last, True)
    return [(sides_of("narrow"), rows) + last[2:], (planes,) + last[2:]]


def exchange(turn, fields, edge_rows, handed, sizes, halves, weight, bias):
    _, planes, corners = layout(sizes)
    depth, height = fields[-1].shape[:2]
    cells = fields[-1].shape[2:]
    sides = sides_of("narrow")
    swap = [(0, 1), (1, 0)]
    handed = lax.ppermute(handed, "pair", swap)
    low, high = line_exchange("narrow", edge_rows)
    ring, corner = call(
        functools.partial(plane_kernel, sizes),
        [(2 * planes,) + cells, (sides, 2 * corners) + cells],
        (),
        8,
    )(*fields, handed)
    ring = ring_exchange(ring)
    corner_low, corner_high = corner_exchange(corner)
    outs = weight.shape[-1]
    (weights,) = call(weight_kernel, [(9, 4 * weight.shape[2], 2 * outs)], (), 8)(weight)
    lanes = 2 * cells[1]
    (inner,) = call(
        functools.partial(inner_kernel, weights.shape[1] - lanes, turn == 0),
        [(depth - 2, height - 2) + cells],
        [pltpu.VMEM((depth, height, cells[0], lanes), bf16)],
        dtype=bf16 if turn == 0 else f32,
    )(fields[-1], handed, weights, bias)
    received = (low, high, ring, corner_low, corner_high)
    frames = [
        (shape[0] + 2 * deep, shape[1] + 2 * tall) + cells for shape, deep, tall in sizes
    ]
    tail = sum(field_slabs(frame, half) for frame, half in zip(frames, halves))
    (passed,) = call(
        functools.partial(pass_kernel, sizes, halves),
        [(planes + sides * corners + tail,) + cells],
        [pltpu.VMEM(frame, bf16) for frame in frames],
        8,
    )(*fields, *received)
    passed = lax.ppermute(passed, "pair", swap)
    return weights, inner, received + (passed,)


def body(
    volume, w_encode, b_encode, w_down, b_down, w_bottom, b_bottom, w_up, b_up, w_decode, b_decode
):
    depth, height, width, skip = volume.shape
    deep_width = w_down.shape[4]
    half_depth, half_height, pairs = depth // 2, height // 2, width // 2
    lanes = 2 * skip
    framed = (depth + 2, height + 2)
    coarse_framed = (half_depth + 4, half_height + 4)

    fine, half = (depth, height, pairs, lanes), (half_depth, half_height, pairs, deep_width)
    sizes = sizes_of([fine], [(1, 1)])
    packed, edge_rows, handed = call(
        functools.partial(pack_kernel, sizes),
        [fine] + edge_shapes(sizes),
        [
            pltpu.VMEM((depth, height, width, skip), bf16),
            pltpu.VMEM((depth, height, width, skip), f32),
            pltpu.SemaphoreType.DMA((depth,)),
        ],
        8,
        in_specs=[pl.BlockSpec(memory_space=pltpu.HBM)],
    )(pltpu.with_memory_space_constraint(volume, pltpu.HBM))
    encode_bias, decode_bias = b_encode.reshape(1, skip), b_decode.reshape(1, skip)
    encode_weights, inner, received = exchange(
        0,
        [packed],
        edge_rows,
        handed,
        sizes,
        [True],
        w_encode.reshape(9, 3, skip, skip),
        encode_bias,
    )
    sizes = sizes_of([half, fine], [(2, 2), (1, 1)])
    encoded, coarse, edge_rows, handed = call(
        functools.partial(encode_kernel, sizes),
        [fine, half] + edge_shapes(sizes),
        [
            pltpu.VMEM(framed + (pairs, lanes), bf16),
            pltpu.VMEM(framed + (skip,), bf16),
            pltpu.VMEM((1, height + 2, pairs, lanes), bf16),
            pltpu.VMEM(framed + (pairs, 2 * lanes), bf16),
        ],
    )(
        packed,
        *received,
        encode_weights,
        inner,
        encode_bias,
        w_down.reshape(4, lanes, deep_width),
        b_down.reshape(1, deep_width),
    )

    decode_weights, inner, received = exchange(
        1,
        [coarse, encoded],
        edge_rows,
        handed,
        sizes,
        [False, True],
        w_decode.reshape(9, 3, lanes, skip),
        decode_bias,
    )
    raised, encoded_ext, columns, encoded_columns = call(
        functools.partial(bottom_kernel, sizes),
        [
            (half_depth + 2, 2, half_height + 2, 2, pairs, lanes),
            framed + (pairs, lanes),
            framed + (skip,),
            framed + (skip,),
        ],
        [
            pltpu.VMEM(coarse_framed + (pairs, deep_width), bf16),
            pltpu.VMEM(coarse_framed + (deep_width,), bf16),
            pltpu.VMEM((2, half_height + 4, pairs, deep_width), bf16),
            pltpu.VMEM((1, height + 2, pairs, lanes), bf16),
            pltpu.VMEM(coarse_framed + (pairs, 3 * deep_width), bf16),
        ],
    )(
        coarse,
        encoded,
        *received,
        w_bottom.reshape(9, 3 * deep_width, deep_width),
        b_bottom.reshape(1, deep_width),
        w_up.reshape(4, 2, deep_width, skip),
        b_up.reshape(1, skip),
    )
    taps = pltpu.VMEM(framed + (pairs, 2 * lanes), bf16)
    columns = lax.ppermute(columns, "pair", [(0, 1), (1, 0)])
    (partial,) = call(
        border_kernel, [(depth, height, pairs, lanes)], [taps], dtype=f32
    )(encoded_ext, encoded_columns, decode_weights, inner)

    (decoded,) = call(
        decode_kernel,
        [(depth, height, width, skip)],
        [taps, pltpu.VMEM((depth, height, width, skip), f32)],
    )(
        raised.reshape(depth + 4, height + 4, pairs, lanes),
        columns,
        decode_weights,
        partial,
        decode_bias,
    )
    return decoded


def solution(mesh):
    return jax.shard_map(
        body,
        mesh=mesh,
        in_specs=(
            P(("groups", "wide"), "narrow", "pair", None),
            P(),
            P(),
            P(),
            P(),
            P(),
            P(),
            P(),
            P(),
            P(),
            P(),
        ),
        out_specs=P(("groups", "wide"), "narrow", "pair", None),
        check_vma=False,
    )
```
